128 devices in a mesh: blk: 32 (over x, y, z_lo), segment: 4 (over z_hi, core).
Axes of the slice: x: 4, y: 4, z: 4 (z_hi: 2, z_lo: 2; z = z_hi * 2 + z_lo), core: 2. Of those that a mesh axis runs over, the one named last changes fastest.
Arguments:
- latent_queries: bfloat16 [2, 128, 2048], P(None, 'blk'), may hold values from -400 to 400
- latent_embed: bfloat16 [2, 128, 2048], P(None, 'blk'), may hold values from -6 to 6
- history_keys: bfloat16 [2, 32768, 2048], P(None, ('blk', 'segment')), may hold values from -6 to 6
- history_values: bfloat16 [2, 32768, 2048], P(None, ('blk', 'segment')), may hold values from -7 to 7
- latent_pos: int32 [2, 128], replicated, may hold values from 1 to 32768, as said below
- norm_gain: float32 [4, 2048], P('segment'), may hold values from 0.25 to 1.75
- w_qkv: bfloat16 [4, 2048, 3, 2048], P('segment', None, None, 'blk'), may hold values from -0.125 to 0.125
- w_out: bfloat16 [4, 2048, 2048], P('segment', 'blk'), may hold values from -0.125 to 0.125
Outputs:
- latents_out: float32 [2, 128, 2048], P(None, 'blk', 'segment')
The draws below stay inside these ranges and needn't reach their ends.
Inputs may be any that keep to these rules, and one draw needn't show every extreme that they name: `latent_pos`: Non-decreasing along the latents of a micro-batch; latent i sees at least (i + 1) * 256 positions and the last latent sees all 32768.
All inputs are finite; a program needn't handle non-finite values.
Results may differ from the reference program's by a relative error of at most 0.0085.
Values may be sent and summed in bfloat16 or wider, within the bound.
A program may use at most 64 MiB of HBM per device.

```python
import math
import jax
import jax.numpy as jnp
from jax import lax

D = 2048
HEADS = 16
MB = 2
LAT = 128
HIST = 32768
LAYERS = 4


def history_row_values(key, micro_ids, row_ids):
    base_key = jax.random.fold_in(key, 31)

    def one_row(micro_id, row_id):
        row_key = jax.random.fold_in(jax.random.fold_in(base_key, micro_id), row_id)
        return jnp.clip(jax.random.normal(row_key, (D,), jnp.float32), -6.0, 6.0)
    return jax.vmap(one_row)(micro_ids, row_ids)


def drawn_rows(key):
    chosen = jnp.arange(8, dtype=jnp.int32) * (LAT // 8) + (LAT // 8 - 1)
    reach = (chosen + 1) * (HIST // LAT) - 1
    drawn = jax.random.randint(jax.random.fold_in(key, 41), (MB, 8), 0, 1 << 20)
    targets = (drawn % reach[None, :]).astype(jnp.int32)
    head_size = D // HEADS
    strength = jax.random.uniform(jax.random.fold_in(key, 42), (MB, 8), jnp.float32, 150.0, 260.0) / math.sqrt(head_size)
    micro_grid = jnp.broadcast_to(jnp.arange(MB, dtype=jnp.int32)[:, None], (MB, 8))
    chosen_grid = jnp.broadcast_to(chosen[None, :], (MB, 8))
    return (micro_grid, chosen_grid, targets, strength)


def draw_history_keys(key, part):
    micro_ids = jnp.repeat(jnp.arange(MB, dtype=jnp.int32), HIST)
    row_ids = jnp.tile(jnp.arange(HIST, dtype=jnp.int32), MB)
    table = history_row_values(key, micro_ids, row_ids).reshape(MB, HIST, D)
    micro_grid, chosen_grid, targets, strength = drawn_rows(key)
    table = table.at[micro_grid, targets + 1].set(0.99 * table[micro_grid, targets])
    return table.astype(jnp.bfloat16)


def draw_latent_queries(key, part):
    spread = 2.5
    entries = spread * jnp.clip(jax.random.normal(jax.random.fold_in(key, 51), (MB, LAT, D), jnp.float32), -6.0, 6.0)
    micro_grid, chosen_grid, targets, strength = drawn_rows(key)
    picked = history_row_values(key, micro_grid.reshape(-1), targets.reshape(-1)).reshape(MB, 8, D)
    entries = entries.at[micro_grid, chosen_grid].set(strength[..., None] * picked)
    return entries.astype(jnp.bfloat16)


def draw_history_values(key, part):
    rough = jnp.clip(jax.random.normal(jax.random.fold_in(key, 71), (MB, HIST, D), jnp.float32), -6.0, 6.0)
    freq = jax.random.randint(jax.random.fold_in(key, 72), (D,), 1, 5).astype(jnp.float32)
    phase = jax.random.uniform(jax.random.fold_in(key, 73), (D,), jnp.float32, -math.pi, math.pi)
    amplitude = jax.random.uniform(jax.random.fold_in(key, 74), (D,), jnp.float32, 0.3, 0.7)
    where_at = jnp.arange(HIST, dtype=jnp.float32) / HIST
    smooth = amplitude[None, :] * jnp.sin(2.0 * math.pi * where_at[:, None] * freq[None, :] + phase[None, :])
    return (rough + smooth[None]).astype(jnp.bfloat16)


def draw_latent_pos(key, part):
    stride = HIST // LAT
    increments = jax.random.randint(jax.random.fold_in(key, 61), (MB, LAT), 1, stride + 1)
    climbed = jnp.cumsum(increments, axis=1)
    return (climbed - climbed[:, -1:] + HIST).astype(jnp.int32)


def block_levels(rng, extent, split, least, largest):
    loudness, own = 1.0, jax.random.fold_in(rng, 6)
    for axis_at, shards_of in split:
        heights = jnp.exp(jax.random.uniform(jax.random.fold_in(own, axis_at), (shards_of,), jnp.float32, least / len(split), largest / len(split)))
        loudness = loudness * jnp.repeat(heights, extent[axis_at] // shards_of).reshape([-1 if axis == axis_at else 1 for axis in range(len(extent))])
    return loudness


def gaussian(own_key, shape, deviation, limit, cuts=(), held_as=jnp.bfloat16):
    level = block_levels(own_key, shape, cuts, -0.22, 0.18) if cuts else 1.0
    values = jax.random.normal(own_key, shape, jnp.float32) * deviation * level
    return jnp.minimum(jnp.maximum(values, -limit), limit).astype(held_as)


def setup_inputs(seed: int = 0) -> dict:
    streams_of = jax.random.split(jax.random.key(seed), 9)
    latent_queries = draw_latent_queries(jax.random.fold_in(streams_of[8], 71), 0)
    latent_embed = gaussian(streams_of[1], (MB, LAT, D), 1.0, 6.0, ((1, 32),))
    history_keys = draw_history_keys(jax.random.fold_in(streams_of[8], 71), 0)
    history_values = draw_history_values(jax.random.fold_in(streams_of[8], 71), 0)
    latent_pos = draw_latent_pos(jax.random.fold_in(streams_of[8], 71), 0)
    norm_gain = jnp.clip(1.0 + 0.15 * jax.random.normal(streams_of[5], (LAYERS, D), jnp.float32), 0.25, 1.75)
    w_qkv = gaussian(streams_of[6], (LAYERS, D, 3, D), D ** -0.5, 0.125, ((0, 4), (3, 32)))
    w_out = gaussian(streams_of[7], (LAYERS, D, D), D ** -0.5, 0.125, ((0, 4), (1, 32)))
    return {"latent_queries": latent_queries, "latent_embed": latent_embed, "history_keys": history_keys, "history_values": history_values, "latent_pos": latent_pos, "norm_gain": norm_gain, "w_qkv": w_qkv, "w_out": w_out}


epsilon = 1e-06
masked = -1e+30

def cross_attend(queries, key_rows, value_rows, positions):
    head_size = D // HEADS
    score_scale = head_size ** (-0.5)
    visible = jnp.arange(key_rows.shape[0], dtype=jnp.int32)[None, :] < positions[:, None]

    def one_head(head_index):
        col_start = head_index * head_size
        query_part = lax.dynamic_slice_in_dim(queries, col_start, head_size, 1)
        key_part = lax.dynamic_slice_in_dim(key_rows, col_start, head_size, 1)
        value_part = lax.dynamic_slice_in_dim(value_rows, col_start, head_size, 1)
        scores = jnp.dot(query_part, key_part.T, preferred_element_type=jnp.float32) * score_scale
        scores = jnp.where(visible, scores, masked)
        row_top = lax.optimization_barrier(jnp.max(scores, axis=1, keepdims=True))
        weights = jnp.where(visible, jnp.exp(scores - row_top), 0.0)
        row_total = lax.optimization_barrier(jnp.sum(weights, axis=1, keepdims=True))
        summed = jnp.dot(weights.astype(jnp.bfloat16), value_part, preferred_element_type=jnp.float32)
        return summed / row_total
    per_head = lax.map(one_head, jnp.arange(HEADS, dtype=jnp.int32))
    return jnp.transpose(per_head, (1, 0, 2)).reshape(queries.shape[0], D)

def tower_layer(latent_state, gain_row, projection, output_rows):
    head_size = D // HEADS
    lat_count = latent_state.shape[0]
    factor = lax.rsqrt(lax.optimization_barrier(jnp.mean(latent_state * latent_state, axis=1, keepdims=True)) + epsilon)
    normed = (latent_state * factor * gain_row).astype(jnp.bfloat16)
    mixed_qkv = jnp.dot(normed, projection.reshape(D, 3 * D), preferred_element_type=jnp.float32).astype(jnp.bfloat16)
    query_heads = mixed_qkv[:, :D].reshape(lat_count, HEADS, head_size).astype(jnp.float32)
    key_heads = mixed_qkv[:, D:2 * D].reshape(lat_count, HEADS, head_size).astype(jnp.float32)
    value_heads = mixed_qkv[:, 2 * D:].reshape(lat_count, HEADS, head_size).astype(jnp.float32)
    scores = jnp.einsum('ihd,jhd->hij', query_heads, key_heads) * head_size ** (-0.5)
    row_ids = lax.broadcasted_iota(jnp.int32, (lat_count, lat_count), 0)
    col_ids = lax.broadcasted_iota(jnp.int32, (lat_count, lat_count), 1)
    scores = jnp.where((col_ids <= row_ids)[None], scores, masked)
    row_top = lax.optimization_barrier(jnp.max(scores, axis=2, keepdims=True))
    weights = jnp.exp(scores - row_top)
    soft_weights = (weights / lax.optimization_barrier(jnp.sum(weights, axis=2, keepdims=True))).astype(jnp.bfloat16)
    attended = jnp.einsum('hij,jhd->ihd', soft_weights.astype(jnp.float32), value_heads)
    attended = attended.reshape(lat_count, D).astype(jnp.bfloat16)
    return latent_state + jnp.dot(attended, output_rows, preferred_element_type=jnp.float32)

def reference(latent_queries, latent_embed, history_keys, history_values, latent_pos, norm_gain, w_qkv, w_out):
    outputs = []
    for micro_index in range(MB):
        attended = cross_attend(latent_queries[micro_index], history_keys[micro_index], history_values[micro_index], latent_pos[micro_index])
        latent_state = latent_embed[micro_index].astype(jnp.float32) + attended
        for layer_index in range(LAYERS):
            latent_state = tower_layer(latent_state, norm_gain[layer_index], w_qkv[layer_index], w_out[layer_index])
        outputs.append(latent_state)
    return jnp.stack(outputs)
```

```python
import jax
import jax.numpy as jnp
from jax import lax
from jax.experimental import pallas as pl
from jax.experimental.pallas import tpu as pltpu
from jax.sharding import PartitionSpec as P

HEADS = 16
HD = 128
LAT = 128
D = 2048
ROWS = 256
NB = 32
SR = 144
epsilon = 1e-06
masked = -1e30
MESH = pl.DeviceIdType.MESH
f32, bf16 = jnp.float32, jnp.bfloat16
NN = (((1,), (0,)), ((), ()))
NT = (((1,), (1,)), ((), ()))
TN = (((0,), (0,)), ((), ()))


def dot(a, b, dims):
    return lax.dot_general(a, b, dims, preferred_element_type=f32)


def split3(v):
    hi = v.astype(bf16).astype(f32)
    mid = (v - hi).astype(bf16).astype(f32)
    return hi, mid, v - hi - mid


def stat_rows(*rows):
    ids = lax.broadcasted_iota(jnp.int32, (16, LAT), 0)
    out = jnp.zeros((16, LAT), f32)
    for i, r in enumerate(rows):
        out = jnp.where(ids == i, jnp.broadcast_to(r, (16, LAT)), out)
    return out.astype(bf16)


def stat3(st, i):
    return st[i : i + 1] + st[i + 1 : i + 2] + st[i + 2 : i + 3]


def kernel(
    q_hbm, e_hbm, k_hbm, v_hbm, pos_ref, gain_ref, wt_hbm, wo_hbm, out_ref,
    qbuf, kb, vb, wt, wob, wot, gain2, ob, r1, r2o, r2, ebuf, xs, xb, xr, xn, ub, rb, fb,
    loc_sem, kv_send, kv_recv, w_send, w_recv, g_sem, q1_sem, q_send, q_recv,
    r1_send, r1_recv, r2_sem, r2_recv, e_send, e_recv, x_send, x_recv, u_send, u_recv,
    xr_send, xr_recv, f_send, f_recv,
):
    b = lax.axis_index("blk")
    s = lax.axis_index("segment")
    h = b // 2
    zl = b % 2
    zh = s // 2
    c = s % 2
    sib = (b, s + 1 - 2 * c)
    zpart = (b + 1 - 2 * zl, s)

    def rcopy(src, dst, ss, rs, dev):
        return pltpu.make_async_remote_copy(
            src_ref=src, dst_ref=dst, send_sem=ss, recv_sem=rs, device_id=dev, device_id_type=MESH
        )

    def plane(t):
        return lax.rem(h + t, HEADS)

    half = pl.ds(pl.multiple_of(64 * zl, 64), 64)
    loc = [
        pltpu.make_async_copy(k_hbm.at[c], kb.at[0], loc_sem.at[0]),
        pltpu.make_async_copy(v_hbm.at[c], vb.at[0], loc_sem.at[1]),
        pltpu.make_async_copy(wt_hbm, wt.at[:, half, :], loc_sem.at[2]),
        pltpu.make_async_copy(wo_hbm, wob.at[half, :], loc_sem.at[3]),
        pltpu.make_async_copy(q_hbm.at[c], qbuf.at[b], loc_sem.at[4]),
    ]
    for cp in (loc[4], loc[0], loc[1], loc[2], loc[3]):
        cp.start()

    barrier = pltpu.get_barrier_semaphore()
    for dz in range(2):
        for ds in range(4):
            if dz + ds:
                pl.semaphore_signal(
                    barrier, inc=1, device_id=(2 * h + (zl + dz) % 2, (s + ds) % 4), device_id_type=MESH
                )

    def greet(t, _):
        pl.semaphore_signal(barrier, inc=1, device_id=(plane(t) * 2 + zl, s), device_id_type=MESH)
        return 0

    lax.fori_loop(1, HEADS, greet, 0)
    pl.semaphore_wait(barrier, HEADS + 6)

    q1 = rcopy(q_hbm.at[c], qbuf.at[b], q1_sem.at[0], q1_sem.at[1], zpart)
    q1.start()
    kx = rcopy(k_hbm.at[1 - c], kb.at[1], kv_send.at[0], kv_recv.at[0], sib)
    vx = rcopy(v_hbm.at[1 - c], vb.at[1], kv_send.at[1], kv_recv.at[1], sib)
    gx = rcopy(gain_ref, gain2, g_sem.at[0], g_sem.at[1], sib)
    kx.start()
    vx.start()
    gx.start()
    loc[4].wait()
    q1.wait_recv()
    two = pl.ds(2 * h, 2)

    def q_copy(t):
        p = plane(t)
        return rcopy(qbuf.at[two], qbuf.at[two], q_send.at[t], q_recv.at[h], (p * 2 + zl, s))

    def q_start(t, _):
        q_copy(t).start()
        return 0

    lax.fori_loop(1, HEADS, q_start, 0)
    wx = rcopy(wt_hbm, wt.at[:, half, :], w_send.at[0], w_recv.at[0], zpart)
    wox = rcopy(wo_hbm, wob.at[half, :], w_send.at[1], w_recv.at[1], zpart)
    wx.start()
    wox.start()

    loc[0].wait()
    loc[1].wait()
    kx.wait_recv()
    vx.wait_recv()

    def q_wait(t, _):
        p = plane(t)
        src = pl.ds(2 * p, 2)
        rcopy(qbuf.at[src], qbuf.at[src], q_send.at[t], q_recv.at[p], (p * 2 + zl, s)).wait_recv()
        return 0

    lax.fori_loop(1, HEADS, q_wait, 0)

    def e_copy(m, t):
        p = plane(t)
        dst = p * 2 + 1 - m
        cols = pl.ds(pl.multiple_of(p * HD, HD), HD)
        return (
            e_hbm.at[m, :, cols],
            ebuf.at[b],
            m * HEADS + t,
            dst,
        )

    @pl.when(s == 0)
    def _():
        for m in range(2):
            def e_start(t, _):
                src, dst_ref, i, dst = e_copy(m, t)
                rcopy(src, dst_ref, e_send.at[i], e_recv.at[b], (dst, s)).start()
                return 0
            lax.fori_loop(1, HEADS, e_start, 0)
            src, dst_ref, i, dst = e_copy(m, 0)

            @pl.when(zl == 1 - m)
            def _():
                pltpu.make_async_copy(src, dst_ref, e_recv.at[b]).start()

            @pl.when(zl == m)
            def _():
                rcopy(src, dst_ref, e_send.at[i], e_recv.at[b], (dst, s)).start()

    base0 = (b * 4 + s) * ROWS
    base1 = (b * 4 + s + 1 - 2 * c) * ROWS
    pos = pos_ref[pl.ds(c, 1), :]
    ids = lax.broadcasted_iota(jnp.int32, (ROWS, LAT), 0)
    scale = HD ** (-0.5)

    def head_step(t, _):
        hh = plane(t + 1)
        cols = pl.ds(pl.multiple_of(hh * HD, HD), HD)
        qh = qbuf[:, :, cols].astype(f32).reshape(LAT, HD).astype(bf16)
        vis0 = ids + base0 < pos
        vis1 = ids + base1 < pos
        s0 = jnp.where(vis0, dot(kb[0, :, cols], qh, NT) * scale, masked)
        s1 = jnp.where(vis1, dot(kb[1, :, cols], qh, NT) * scale, masked)
        top = jnp.max(jnp.maximum(s0, s1), axis=0, keepdims=True)
        e0 = jnp.where(vis0, jnp.exp(s0 - top), 0.0)
        e1 = jnp.where(vis1, jnp.exp(s1 - top), 0.0)
        total = jnp.sum(e0 + e1, axis=0, keepdims=True)
        o = dot(vb[0, :, cols], e0.astype(bf16), TN) + dot(vb[1, :, cols], e1.astype(bf16), TN)
        ob[hh, 0:HD, :] = o.astype(bf16)
        ob[hh, HD:SR, :] = stat_rows(*split3(top), *split3(total))

        @pl.when(t < HEADS - 1)
        def _():
            rcopy(ob.at[hh], r1.at[h], r1_send.at[hh], r1_recv.at[h], (hh * 2 + zl, s)).start()

        return 0

    lax.fori_loop(0, HEADS, head_step, 0)

    def r1_wait(t, _):
        p = plane(t)
        rcopy(ob.at[p], r1.at[p], r1_send.at[p], r1_recv.at[p], (p * 2 + zl, s)).wait_recv()
        return 0

    lax.fori_loop(1, HEADS, r1_wait, 0)
    r1[h] = ob[h]

    def combine(buf, n):
        st = [buf[i, HD:SR, :].astype(f32) for i in range(n)]
        tops = [stat3(v, 0) for v in st]
        top = tops[0]
        for v in tops[1:]:
            top = jnp.maximum(top, v)
        total = jnp.zeros((1, LAT), f32)
        acc = jnp.zeros((HD, LAT), f32)
        for i in range(n):
            w = jnp.exp(tops[i] - top)
            total = total + w * stat3(st[i], 3)
            acc = acc + w * buf[i, 0:HD, :].astype(f32)
        return acc, top, total

    acc, top, total = combine(r1, HEADS)
    r2o[0:HD, :] = acc.astype(bf16)
    r2o[HD:SR, :] = stat_rows(*split3(top), *split3(total))
    z = zh * 2 + zl
    r2_home = (s == 0) & (zl == 1 - c)
    r2_dst = (2 * h + 1 - c, 0)

    @pl.when(r2_home)
    def _():
        pltpu.make_async_copy(r2o, r2.at[z], r2_recv.at[z]).start()

    @pl.when(jnp.logical_not(r2_home))
    def _():
        rcopy(r2o, r2.at[z], r2_sem.at[0], r2_recv.at[z], r2_dst).start()

    loc[2].wait()
    loc[3].wait()
    wx.wait_recv()
    wox.wait_recv()
    for j in range(HEADS):
        wot[j] = wob[:, j * HD : (j + 1) * HD].T
    gx.wait_recv()
    my_cols = pl.ds(pl.multiple_of(h * HD, HD), HD)

    def column(ref):
        return jnp.broadcast_to(ref[:, my_cols], (HD, LAT)).T

    def pack_x(x, gain):
        xs[0:HD, :] = (x * gain).astype(bf16)
        xs[HD:SR, :] = stat_rows(*split3(jnp.sum(x * x, axis=0, keepdims=True)))

    @pl.when(c == 0)
    def _():
        @pl.when(s == 0)
        def _():
            def e_wait(i, _):
                pltpu.make_async_copy(e_hbm.at[0, :, pl.ds(0, HD)], ebuf.at[i], e_recv.at[i]).wait()
                return 0

            lax.fori_loop(0, NB, e_wait, 0)
            for i in range(4):
                pltpu.make_async_copy(r2o, r2.at[i], r2_recv.at[i]).wait()
            acc, top, total = combine(r2, 4)
            emb = ebuf[...].astype(f32).reshape(LAT, HD).T
            xr[...] = emb + acc / total

        @pl.when(s == 2)
        def _():
            pltpu.make_async_copy(xn, xr, xr_recv.at[0]).wait()

        pack_x(xr[...], column(gain_ref))

        def x_start(t, _):
            p = plane(t)
            rcopy(xs, xb.at[h], x_send.at[t], x_recv.at[h], (p * 2 + zl, s)).start()
            return 0

        lax.fori_loop(1, HEADS, x_start, 0)
        pltpu.make_async_copy(xs, xb.at[h], x_recv.at[h]).start()

    def x_wait(i, _):
        pltpu.make_async_copy(xs, xb.at[i], x_recv.at[i]).wait()
        return 0

    lax.fori_loop(0, HEADS, x_wait, 0)

    wfull = wt[...].reshape(3 * HD, D)
    qkv = jnp.zeros((3 * HD, LAT), f32)
    ss = jnp.zeros((1, LAT), f32)
    for j in range(HEADS // 2):
        pair = jnp.concatenate([xb[2 * j, 0:HD, :], xb[2 * j + 1, 0:HD, :]], axis=0)
        qkv = qkv + dot(wfull[:, 2 * j * HD : (2 * j + 2) * HD], pair, NN)
    for j in range(HEADS):
        ss = ss + stat3(xb[j, HD:SR, :].astype(f32), 0)
    factor = lax.rsqrt(ss * (1.0 / D) + epsilon)
    qkv = (qkv * factor).astype(bf16)
    qt, kt, vt = qkv[0:HD], qkv[HD : 2 * HD], qkv[2 * HD :]
    sc = dot(kt, qt, TN) * scale
    jj = lax.broadcasted_iota(jnp.int32, (LAT, LAT), 0)
    ii = lax.broadcasted_iota(jnp.int32, (LAT, LAT), 1)
    sc = jnp.where(jj <= ii, sc, masked)
    e = jnp.exp(sc - jnp.max(sc, axis=0, keepdims=True))
    soft = (e / jnp.sum(e, axis=0, keepdims=True)).astype(bf16)
    att = dot(vt, soft, NN).astype(bf16)

    def u_step(t, _):
        p = plane(t + 1)
        ub[p] = dot(wot[p], att, NN).astype(bf16)

        @pl.when(t < HEADS - 1)
        def _():
            rcopy(ub.at[p], rb.at[h], u_send.at[p], u_recv.at[h], (p * 2 + zl, s)).start()

        return 0

    lax.fori_loop(0, HEADS, u_step, 0)

    @pl.when(c == 1)
    def _():
        pltpu.make_async_copy(xn, xr, xr_recv.at[0]).wait()

    def u_wait(t, _):
        p = plane(t)
        rcopy(ub.at[p], rb.at[p], u_send.at[p], u_recv.at[p], (p * 2 + zl, s)).wait_recv()
        return 0

    lax.fori_loop(1, HEADS, u_wait, 0)
    rb[h] = ub[h]
    x = xr[...]
    for j in range(HEADS):
        x = x + rb[j].astype(f32)
    xn[...] = x

    @pl.when(c == 0)
    def _():
        def x_drain(t, _):
            pltpu.make_async_copy(xs, xb.at[0], x_send.at[t]).wait()
            return 0

        lax.fori_loop(1, HEADS, x_drain, 0)
        pack_x(xn[...], column(gain2))

        def x_next(t, _):
            p = plane(t)
            rcopy(xs, xb.at[h], x_send.at[t], x_recv.at[h], (p * 2 + zl, s + 1)).start()
            return 0

        lax.fori_loop(0, HEADS, x_next, 0)
        up = rcopy(xn, xr, xr_send.at[0], xr_recv.at[0], sib)
        up.start()

        def x_drain2(t, _):
            pltpu.make_async_copy(xs, xb.at[0], x_send.at[t]).wait()
            return 0

        lax.fori_loop(0, HEADS, x_drain2, 0)
        up.wait_send()

    @pl.when(s == 1)
    def _():
        up = rcopy(xn, xr, xr_send.at[0], xr_recv.at[0], (b + 1 - 2 * zl, 2))
        up.start()
        up.wait_send()

    seg = h // 4
    f_cols = pl.ds(pl.multiple_of(lax.rem(h, 4) * HD, HD), HD)

    @pl.when(s == 3)
    def _():
        fb[...] = xn[...].T.reshape(NB, 4, HD)

        def f_start(i, _):
            away = jnp.logical_or(i != b, seg != s)
            dst = out_ref.at[zl, :, f_cols]
            sem = f_recv.at[zl * 4 + lax.rem(h, 4)]

            @pl.when(away)
            def _():
                rcopy(fb.at[i], dst, f_send.at[i], sem, (i, seg)).start()

            @pl.when(jnp.logical_not(away))
            def _():
                pltpu.make_async_copy(fb.at[i], dst, sem).start()

            return 0

        lax.fori_loop(0, NB, f_start, 0)

        def f_drain(i, _):
            @pl.when(jnp.logical_or(i != b, seg != s))
            def _():
                pltpu.make_async_copy(fb.at[i], fb.at[i], f_send.at[i]).wait()

            return 0

        lax.fori_loop(0, NB, f_drain, 0)

    q1.wait_send()
    kx.wait_send()
    vx.wait_send()
    gx.wait_send()
    wx.wait_send()
    wox.wait_send()

    def drain(t, _):
        q_copy(t).wait_send()
        p = plane(t)
        rcopy(ob.at[p], r1.at[h], r1_send.at[p], r1_recv.at[h], (p * 2 + zl, s)).wait_send()
        rcopy(ub.at[p], rb.at[h], u_send.at[p], u_recv.at[h], (p * 2 + zl, s)).wait_send()
        return 0

    lax.fori_loop(1, HEADS, drain, 0)

    @pl.when(jnp.logical_not(r2_home))
    def _():
        rcopy(r2o, r2.at[z], r2_sem.at[0], r2_recv.at[z], r2_dst).wait_send()

    @pl.when(s == 0)
    def _():
        for m in range(2):
            def e_drain(t, _):
                src, dst_ref, i, dst = e_copy(m, t)
                pltpu.make_async_copy(src, dst_ref, e_send.at[i]).wait()
                return 0

            lax.fori_loop(1, HEADS, e_drain, 0)

            @pl.when(zl == m)
            def _():
                src, dst_ref, i, dst = e_copy(m, 0)
                pltpu.make_async_copy(src, dst_ref, e_send.at[i]).wait()

    for m in range(2):
        for i in range(4):
            pltpu.make_async_copy(
                fb.at[0], out_ref.at[m, :, i * HD : (i + 1) * HD], f_recv.at[m * 4 + i]
            ).wait()


def on_device(
    latent_queries, latent_embed, history_keys, history_values, latent_pos, norm_gain, w_qkv, w_out
):
    wt = jnp.transpose(w_qkv[0], (1, 2, 0))
    hbm = pl.BlockSpec(memory_space=pl.ANY)
    vmem = pl.BlockSpec(memory_space=pltpu.VMEM)
    dma = pltpu.SemaphoreType.DMA
    return pl.pallas_call(
        kernel,
        out_shape=jax.ShapeDtypeStruct((2, 4, 512), f32),
        in_specs=[hbm, hbm, hbm, hbm, vmem, vmem, hbm, hbm],
        out_specs=vmem,
        scratch_shapes=[
            pltpu.VMEM((NB, 4, D), bf16),
            pltpu.VMEM((2, ROWS, D), bf16),
            pltpu.VMEM((2, ROWS, D), bf16),
            pltpu.VMEM((3, HD, D), bf16),
            pltpu.VMEM((HD, D), bf16),
            pltpu.VMEM((HEADS, HD, HD), bf16),
            pltpu.VMEM((1, D), f32),
            pltpu.VMEM((HEADS, SR, LAT), bf16),
            pltpu.VMEM((HEADS, SR, LAT), bf16),
            pltpu.VMEM((SR, LAT), bf16),
            pltpu.VMEM((4, SR, LAT), bf16),
            pltpu.VMEM((NB, 4, HD), bf16),
            pltpu.VMEM((SR, LAT), bf16),
            pltpu.VMEM((HEADS, SR, LAT), bf16),
            pltpu.VMEM((HD, LAT), f32),
            pltpu.VMEM((HD, LAT), f32),
            pltpu.VMEM((HEADS, HD, LAT), bf16),
            pltpu.VMEM((HEADS, HD, LAT), bf16),
            pltpu.VMEM((NB, 4, HD), f32),
            dma((5,)), dma((2,)), dma((2,)), dma((2,)), dma((2,)), dma((2,)), dma((2,)),
            dma((HEADS,)), dma((HEADS,)), dma((HEADS,)), dma((HEADS,)), dma((1,)), dma((4,)),
            dma((2 * HEADS,)), dma((NB,)), dma((HEADS,)), dma((HEADS,)), dma((HEADS,)), dma((HEADS,)),
            dma((1,)), dma((1,)), dma((NB,)), dma((8,)),
        ],
        compiler_params=pltpu.CompilerParams(
            collective_id=0, has_side_effects=True, vmem_limit_bytes=67043328
        ),
        name="ar_step",
    )(latent_queries, latent_embed, history_keys, history_values, latent_pos, norm_gain, wt, w_out[0])


def solution(mesh):
    return jax.shard_map(
        on_device,
        mesh=mesh,
        in_specs=(
            P(None, "blk", None),
            P(None, "blk", None),
            P(None, ("blk", "segment"), None),
            P(None, ("blk", "segment"), None),
            P(),
            P("segment", None),
            P("segment", None, None, "blk"),
            P("segment", "blk", None),
        ),
        out_specs=P(None, "blk", "segment"),
        check_vma=False,
    )
```

```python
import jax
import jax.numpy as jnp
from jax import lax
from jax.experimental import pallas as pl
from jax.experimental.pallas import tpu as pltpu
from jax.sharding import PartitionSpec as P

HEADS = 16
HD = 128
LAT = 128
D = 2048
ROWS = 256
NB = 32
SR = 144
epsilon = 1e-06
masked = -1e30
MESH = pl.DeviceIdType.MESH
f32, bf16 = jnp.float32, jnp.bfloat16
NN = (((1,), (0,)), ((), ()))
NT = (((1,), (1,)), ((), ()))
TN = (((0,), (0,)), ((), ()))
FAR = sorted(
    ((dx, dy) for dx in range(4) for dy in range(4) if dx or dy),
    key=lambda o: -min(o[0], 4 - o[0]) - min(o[1], 4 - o[1]),
)


def dot(a, b, dims):
    return lax.dot_general(a, b, dims, preferred_element_type=f32)


def split3(v):
    hi = v.astype(bf16).astype(f32)
    mid = (v - hi).astype(bf16).astype(f32)
    return hi, mid, v - hi - mid


def stat_rows(*rows):
    ids = lax.broadcasted_iota(jnp.int32, (16, LAT), 0)
    out = jnp.zeros((16, LAT), f32)
    for i, r in enumerate(rows):
        out = jnp.where(ids == i, jnp.broadcast_to(r, (16, LAT)), out)
    return out.astype(bf16)


def stat3(st, i):
    return st[i : i + 1] + st[i + 1 : i + 2] + st[i + 2 : i + 3]


def kernel(
    q_hbm, e_hbm, k_hbm, v_hbm, pos_ref, gain_ref, wt_hbm, wo_hbm, out_ref,
    qbuf, kb, vb, vts, wt, wob, wot, gain2, ob, r1, r2o, r2, ebuf, xs, xb, xr, xn, ub, rb, fb,
    loc_sem, kv_send, kv_recv, w_send, w_recv, g_sem, q1_sem, q_send, q_recv,
    r1_send, r1_recv, r2_sem, r2_recv, e_send, e_recv, x_send, x_recv, u_send, u_recv,
    xr_send, xr_recv, f_send, f_recv,
):
    b = lax.axis_index("blk")
    s = lax.axis_index("segment")
    h = b // 2
    zl = b % 2
    zh = s // 2
    c = s % 2
    sib = (b, s + 1 - 2 * c)
    zpart = (b + 1 - 2 * zl, s)

    def rcopy(src, dst, ss, rs, dev):
        return pltpu.make_async_remote_copy(
            src_ref=src, dst_ref=dst, send_sem=ss, recv_sem=rs, device_id=dev, device_id_type=MESH
        )

    hx, hy = h // 4, lax.rem(h, 4)

    def chip(dx, dy):
        return lax.rem(hx + dx, 4) * 4 + lax.rem(hy + dy, 4)

    far = [chip(*o) for o in FAR]
    near = [h] + far[::-1]

    half = pl.ds(pl.multiple_of(64 * zl, 64), 64)
    loc = [
        pltpu.make_async_copy(k_hbm.at[c], kb.at[0], loc_sem.at[0]),
        pltpu.make_async_copy(v_hbm.at[c], vb.at[0], loc_sem.at[1]),
        pltpu.make_async_copy(wt_hbm, wt.at[:, half, :], loc_sem.at[2]),
        pltpu.make_async_copy(wo_hbm, wob.at[half, :], loc_sem.at[3]),
        pltpu.make_async_copy(q_hbm.at[c], qbuf.at[b], loc_sem.at[4]),
    ]
    for cp in (loc[4], loc[0], loc[1], loc[2], loc[3]):
        cp.start()

    barrier = pltpu.get_barrier_semaphore()
    for dz in range(2):
        for ds in range(4):
            if dz + ds:
                pl.semaphore_signal(
                    barrier, inc=1, device_id=(2 * h + (zl + dz) % 2, (s + ds) % 4), device_id_type=MESH
                )

    for p in far:
        pl.semaphore_signal(barrier, inc=1, device_id=(p * 2 + zl, s), device_id_type=MESH)
    pl.semaphore_wait(barrier, HEADS + 6)

    other = b + 1 - 2 * zl
    q1 = rcopy(q_hbm.at[c], qbuf.at[b], q1_sem.at[0], q_recv.at[b], zpart)
    q1.start()
    wx = rcopy(wt_hbm, wt.at[:, half, :], w_send.at[0], w_recv.at[0], zpart)
    wx.start()
    sent = []

    def go(cp):
        cp.start()
        sent.append(cp)

    for i, p in enumerate(far):
        go(rcopy(q_hbm.at[c], qbuf.at[b], q_send.at[i], q_recv.at[b], (p * 2 + zl, s)))
    kx = rcopy(k_hbm.at[1 - c], kb.at[1], kv_send.at[0], kv_recv.at[0], sib)
    vx = rcopy(v_hbm.at[1 - c], vb.at[1], kv_send.at[1], kv_recv.at[1], sib)
    gx = rcopy(gain_ref, gain2, g_sem.at[0], g_sem.at[1], sib)
    kx.start()
    vx.start()
    gx.start()

    def q_wait(i):
        pltpu.make_async_copy(q_hbm.at[c], qbuf.at[i], q_recv.at[i]).wait()

    q_wait(other)
    for i, p in enumerate(far):
        go(rcopy(qbuf.at[other], qbuf.at[other], q_send.at[15 + i], q_recv.at[other], (p * 2 + zl, s)))

    loc[1].wait()
    for j in range(HEADS):
        vts[j, :, 0:ROWS] = vb[0, :, j * HD : (j + 1) * HD].T
    vx.wait_recv()
    for j in range(HEADS):
        vts[j, :, ROWS : 2 * ROWS] = vb[1, :, j * HD : (j + 1) * HD].T
    loc[0].wait()
    kx.wait_recv()
    loc[4].wait()
    for p in far:
        q_wait(2 * p + zl)
        q_wait(2 * p + 1 - zl)

    def e_copy(m, t):
        p = lax.rem(h + t, HEADS)
        dst = p * 2 + 1 - m
        cols = pl.ds(pl.multiple_of(p * HD, HD), HD)
        return (
            e_hbm.at[m, :, cols],
            ebuf.at[b],
            m * HEADS + t,
            dst,
        )

    @pl.when(s == 0)
    def _():
        for m in range(2):
            def e_start(t, _):
                src, dst_ref, i, dst = e_copy(m, t)
                rcopy(src, dst_ref, e_send.at[i], e_recv.at[b], (dst, s)).start()
                return 0
            lax.fori_loop(1, HEADS, e_start, 0)
            src, dst_ref, i, dst = e_copy(m, 0)

            @pl.when(zl == 1 - m)
            def _():
                pltpu.make_async_copy(src, dst_ref, e_recv.at[b]).start()

            @pl.when(zl == m)
            def _():
                rcopy(src, dst_ref, e_send.at[i], e_recv.at[b], (dst, s)).start()

    base0 = (b * 4 + s) * ROWS
    base1 = (b * 4 + s + 1 - 2 * c) * ROWS
    pos = pos_ref[pl.ds(c, 1), :]
    ids = lax.broadcasted_iota(jnp.int32, (ROWS, LAT), 0)
    scale = HD ** (-0.5)

    ids1 = ids + base1
    ids0 = ids + base0

    def scores(hh):
        cols = pl.ds(pl.multiple_of(hh * HD, HD), HD)
        qh = qbuf[:, :, cols].astype(f32).reshape(LAT, HD).astype(bf16)
        s0 = jnp.where(ids0 < pos, dot(kb[0, :, cols], qh, NT) * scale, masked)
        s1 = jnp.where(ids1 < pos, dot(kb[1, :, cols], qh, NT) * scale, masked)
        return s0, s1

    def weigh(s0, s1):
        top = jnp.maximum(jnp.max(jnp.maximum(s0, s1), axis=0, keepdims=True), 0.1 * masked)
        e0, e1 = jnp.exp(s0 - top), jnp.exp(s1 - top)
        total = jnp.sum(e0 + e1, axis=0, keepdims=True)
        return top, total, jnp.concatenate([e0.astype(bf16), e1.astype(bf16)], axis=0)

    order = far + [h]
    for g in range(0, HEADS, 2):
        group = order[g : g + 2]
        ss = [scores(hh) for hh in group]
        ws = [weigh(*v) for v in ss]
        for hh, (top, total, e) in zip(group, ws):
            ob[hh, 0:HD, :] = dot(vts[hh], e, NN).astype(bf16)
            ob[hh, HD:SR, :] = stat_rows(*split3(top), *split3(total))
        for i in range(g, g + 2):
            if i < HEADS - 1:
                hh = order[i]
                go(rcopy(ob.at[hh], r1.at[h], r1_send.at[i], r1_recv.at[h], (hh * 2 + zl, s)))

    for p in near[1:]:
        pltpu.make_async_copy(r2o, r1.at[p], r1_recv.at[p]).wait()
    r1[h] = ob[h]

    def combine(buf, n):
        st = [buf[i, HD:SR, :].astype(f32) for i in range(n)]
        tops = [stat3(v, 0) for v in st]
        top = tops[0]
        for v in tops[1:]:
            top = jnp.maximum(top, v)
        total = jnp.zeros((1, LAT), f32)
        acc = jnp.zeros((HD, LAT), f32)
        for i in range(n):
            w = jnp.exp(tops[i] - top)
            total = total + w * stat3(st[i], 3)
            acc = acc + w * buf[i, 0:HD, :].astype(f32)
        return acc, top, total

    acc, top, total = combine(r1, HEADS)
    r2o[0:HD, :] = acc.astype(bf16)
    r2o[HD:SR, :] = stat_rows(*split3(top), *split3(total))
    z = zh * 2 + zl
    r2_home = (s == 0) & (zl == 1 - c)
    r2_dst = (2 * h + 1 - c, 0)

    @pl.when(r2_home)
    def _():
        pltpu.make_async_copy(r2o, r2.at[z], r2_recv.at[z]).start()

    @pl.when(jnp.logical_not(r2_home))
    def _():
        rcopy(r2o, r2.at[z], r2_sem.at[0], r2_recv.at[z], r2_dst).start()

    wox = rcopy(wo_hbm, wob.at[half, :], w_send.at[1], w_recv.at[1], zpart)
    wox.start()

    gx.wait_recv()
    my_cols = pl.ds(pl.multiple_of(h * HD, HD), HD)

    def column(ref):
        return jnp.broadcast_to(ref[:, my_cols], (HD, LAT)).T

    def pack_x(x, gain):
        xs[0:HD, :] = (x * gain).astype(bf16)
        xs[HD:SR, :] = stat_rows(*split3(jnp.sum(x * x, axis=0, keepdims=True)))

    @pl.when(c == 0)
    def _():
        @pl.when(s == 0)
        def _():
            def e_wait(i, _):
                pltpu.make_async_copy(e_hbm.at[0, :, pl.ds(0, HD)], ebuf.at[i], e_recv.at[i]).wait()
                return 0

            lax.fori_loop(0, NB, e_wait, 0)
            for i in range(4):
                pltpu.make_async_copy(r2o, r2.at[i], r2_recv.at[i]).wait()
            acc, top, total = combine(r2, 4)
            emb = ebuf[...].astype(f32).reshape(LAT, HD).T
            xr[...] = emb + acc / total

        @pl.when(s == 2)
        def _():
            pltpu.make_async_copy(xn, xr, xr_recv.at[0]).wait()

        pack_x(xr[...], column(gain_ref))

        for i, p in enumerate(far):
            rcopy(xs, xb.at[h], x_send.at[i], x_recv.at[h], (p * 2 + zl, s)).start()
        pltpu.make_async_copy(xs, xb.at[h], x_recv.at[h]).start()

    loc[2].wait()
    wx.wait_recv()
    qkv = jnp.zeros((3 * HD, LAT), f32)
    ss = jnp.zeros((1, LAT), f32)
    for j in range(0, HEADS, 2):
        pair = near[j : j + 2]
        for p in pair:
            pltpu.make_async_copy(xs, xb.at[p], x_recv.at[p]).wait()
        w2 = [wt[:, :, pl.ds(pl.multiple_of(p * HD, HD), HD)].reshape(3 * HD, HD) for p in pair]
        x2 = [xb[p, 0:HD, :] for p in pair]
        qkv = qkv + dot(jnp.concatenate(w2, axis=1), jnp.concatenate(x2, axis=0), NN)
        for p in pair:
            ss = ss + stat3(xb[p, HD:SR, :].astype(f32), 0)
    loc[3].wait()
    wox.wait_recv()
    for j in range(HEADS):
        wot[j] = wob[:, j * HD : (j + 1) * HD].T
    factor = lax.rsqrt(ss * (1.0 / D) + epsilon)
    qkv = (qkv * factor).astype(bf16)
    qt, kt, vt = qkv[0:HD], qkv[HD : 2 * HD], qkv[2 * HD :]
    sc = dot(kt, qt, TN) * scale
    jj = lax.broadcasted_iota(jnp.int32, (LAT, LAT), 0)
    ii = lax.broadcasted_iota(jnp.int32, (LAT, LAT), 1)
    sc = jnp.where(jj <= ii, sc, masked)
    e = jnp.exp(sc - jnp.max(sc, axis=0, keepdims=True))
    soft = (e / jnp.sum(e, axis=0, keepdims=True)).astype(bf16)
    att = dot(vt, soft, NN).astype(bf16)

    for g in range(0, HEADS - 1, 5):
        us = [dot(wot[p], att, NN).astype(bf16) for p in far[g : g + 5]]
        for p, u in zip(far[g : g + 5], us):
            ub[p] = u
        for i, p in enumerate(far[g : g + 5], g):
            go(rcopy(ub.at[p], rb.at[h], u_send.at[i], u_recv.at[h], (p * 2 + zl, s)))
    own = dot(wot[h], att, NN)

    @pl.when(c == 1)
    def _():
        pltpu.make_async_copy(xn, xr, xr_recv.at[0]).wait()

    x = xr[...] + own
    for p in near[1:]:
        pltpu.make_async_copy(ub.at[p], rb.at[p], u_recv.at[p]).wait()
        x = x + rb[p].astype(f32)
    xn[...] = x

    @pl.when(c == 0)
    def _():
        for i in range(HEADS - 1):
            pltpu.make_async_copy(xs, xb.at[0], x_send.at[i]).wait()
        pack_x(xn[...], column(gain2))

        for i, p in enumerate(far + [h]):
            rcopy(xs, xb.at[h], x_send.at[i], x_recv.at[h], (p * 2 + zl, s + 1)).start()
        up = rcopy(xn, xr, xr_send.at[0], xr_recv.at[0], sib)
        up.start()
        for i in range(HEADS):
            pltpu.make_async_copy(xs, xb.at[0], x_send.at[i]).wait()
        up.wait_send()

    @pl.when(s == 1)
    def _():
        up = rcopy(xn, xr, xr_send.at[0], xr_recv.at[0], (b + 1 - 2 * zl, 2))
        up.start()
        up.wait_send()

    seg = h // 4
    f_cols = pl.ds(pl.multiple_of(lax.rem(h, 4) * HD, HD), HD)

    @pl.when(s == 3)
    def _():
        fb[...] = xn[...].T.reshape(NB, 4, HD)

        dst = out_ref.at[zl, :, f_cols]
        sem = f_recv.at[zl * 4 + lax.rem(h, 4)]
        for i, p in enumerate(far):
            for dz in range(2):
                rcopy(fb.at[2 * p + dz], dst, f_send.at[2 * i + dz], sem, (2 * p + dz, seg)).start()
        rcopy(fb.at[other], dst, f_send.at[30], sem, (other, seg)).start()

        @pl.when(seg != s)
        def _():
            rcopy(fb.at[b], dst, f_send.at[31], sem, (b, seg)).start()

        @pl.when(seg == s)
        def _():
            pltpu.make_async_copy(fb.at[b], dst, sem).start()

        for i in range(31):
            pltpu.make_async_copy(fb.at[i], fb.at[i], f_send.at[i]).wait()

        @pl.when(seg != s)
        def _():
            pltpu.make_async_copy(fb.at[0], fb.at[0], f_send.at[31]).wait()

    q1.wait_send()
    kx.wait_send()
    vx.wait_send()
    gx.wait_send()
    wx.wait_send()
    wox.wait_send()

    for cp in sent:
        cp.wait_send()

    @pl.when(jnp.logical_not(r2_home))
    def _():
        rcopy(r2o, r2.at[z], r2_sem.at[0], r2_recv.at[z], r2_dst).wait_send()

    @pl.when(s == 0)
    def _():
        for m in range(2):
            def e_drain(t, _):
                src, dst_ref, i, dst = e_copy(m, t)
                pltpu.make_async_copy(src, dst_ref, e_send.at[i]).wait()
                return 0

            lax.fori_loop(1, HEADS, e_drain, 0)

            @pl.when(zl == m)
            def _():
                src, dst_ref, i, dst = e_copy(m, 0)
                pltpu.make_async_copy(src, dst_ref, e_send.at[i]).wait()

    for m in range(2):
        for i in range(4):
            pltpu.make_async_copy(
                fb.at[0], out_ref.at[m, :, i * HD : (i + 1) * HD], f_recv.at[m * 4 + i]
            ).wait()


def on_device(
    latent_queries, latent_embed, history_keys, history_values, latent_pos, norm_gain, w_qkv, w_out
):
    wt = jnp.transpose(w_qkv[0], (1, 2, 0))
    hbm = pl.BlockSpec(memory_space=pl.ANY)
    vmem = pl.BlockSpec(memory_space=pltpu.VMEM)
    dma = pltpu.SemaphoreType.DMA
    return pl.pallas_call(
        kernel,
        out_shape=jax.ShapeDtypeStruct((2, 4, 512), f32),
        in_specs=[hbm, hbm, hbm, hbm, vmem, vmem, hbm, hbm],
        out_specs=vmem,
        scratch_shapes=[
            pltpu.VMEM((NB, 4, D), bf16),
            pltpu.VMEM((2, ROWS, D), bf16),
            pltpu.VMEM((2, ROWS, D), bf16),
            pltpu.VMEM((HEADS, HD, 2 * ROWS), bf16),
            pltpu.VMEM((3, HD, D), bf16),
            pltpu.VMEM((HD, D), bf16),
            pltpu.VMEM((HEADS, HD, HD), bf16),
            pltpu.VMEM((1, D), f32),
            pltpu.VMEM((HEADS, SR, LAT), bf16),
            pltpu.VMEM((HEADS, SR, LAT), bf16),
            pltpu.VMEM((SR, LAT), bf16),
            pltpu.VMEM((4, SR, LAT), bf16),
            pltpu.VMEM((NB, 4, HD), bf16),
            pltpu.VMEM((SR, LAT), bf16),
            pltpu.VMEM((HEADS, SR, LAT), bf16),
            pltpu.VMEM((HD, LAT), f32),
            pltpu.VMEM((HD, LAT), f32),
            pltpu.VMEM((HEADS, HD, LAT), bf16),
            pltpu.VMEM((HEADS, HD, LAT), bf16),
            pltpu.VMEM((NB, 4, HD), f32),
            dma((5,)), dma((2,)), dma((2,)), dma((2,)), dma((2,)), dma((2,)), dma((2,)),
            dma((NB,)), dma((NB,)), dma((HEADS,)), dma((HEADS,)), dma((1,)), dma((4,)),
            dma((2 * HEADS,)), dma((NB,)), dma((HEADS,)), dma((HEADS,)), dma((HEADS,)), dma((HEADS,)),
            dma((1,)), dma((1,)), dma((NB,)), dma((8,)),
        ],
        compiler_params=pltpu.CompilerParams(
            collective_id=0, has_side_effects=True, vmem_limit_bytes=67043328
        ),
        name="ar_step",
    )(latent_queries, latent_embed, history_keys, history_values, latent_pos, norm_gain, wt, w_out[0])


def solution(mesh):
    return jax.shard_map(
        on_device,
        mesh=mesh,
        in_specs=(
            P(None, "blk", None),
            P(None, "blk", None),
            P(None, ("blk", "segment"), None),
            P(None, ("blk", "segment"), None),
            P(),
            P("segment", None),
            P("segment", None, None, "blk"),
            P("segment", "blk", None),
        ),
        out_specs=P(None, "blk", "segment"),
        check_vma=False,
    )
```

```python
import jax
import jax.numpy as jnp
from jax import lax
from jax.experimental import pallas as pl
from jax.experimental.pallas import tpu as pltpu
from jax.sharding import PartitionSpec as P

HEADS = 16
HD = 128
LAT = 128
D = 2048
ROWS = 256
NB = 32
SR = 144
epsilon = 1e-06
masked = -1e30
MESH = pl.DeviceIdType.MESH
f32, bf16 = jnp.float32, jnp.bfloat16
NN = (((1,), (0,)), ((), ()))
NT = (((1,), (1,)), ((), ()))
TN = (((0,), (0,)), ((), ()))
FAR = sorted(
    ((dx, dy) for dx in range(4) for dy in range(4) if dx or dy),
    key=lambda o: -min(o[0], 4 - o[0]) - min(o[1], 4 - o[1]),
)


def dot(a, b, dims):
    return lax.dot_general(a, b, dims, preferred_element_type=f32)


def split3(v):
    hi = v.astype(bf16).astype(f32)
    mid = (v - hi).astype(bf16).astype(f32)
    return hi, mid, v - hi - mid


def stat_rows(*rows):
    ids = lax.broadcasted_iota(jnp.int32, (16, LAT), 0)
    out = jnp.zeros((16, LAT), f32)
    for i, r in enumerate(rows):
        out = jnp.where(ids == i, jnp.broadcast_to(r, (16, LAT)), out)
    return out.astype(bf16)


def stat3(st, i):
    return st[i : i + 1] + st[i + 1 : i + 2] + st[i + 2 : i + 3]


def kernel(
    q_hbm, e_hbm, k_hbm, v_hbm, pos_ref, gain_ref, wt_hbm, wo_hbm, out_ref,
    qbuf, kb, vb, vts, wt, wob, wot, gain2, ob, r1, r2o, r2, ebuf, xs, xb, xr, xn, ub, rb, fb, fx, uf, fu,
    loc_sem, kv_send, kv_recv, w_send, w_recv, g_sem, q_send, q_recv,
    r1_sem, r2_sem, e_sem, x_send, x_recv, u_send, u_recv, xr_sem, f_send, f_recv,
):
    b = lax.axis_index("blk")
    s = lax.axis_index("segment")
    h = b // 2
    zl = b % 2
    zh = s // 2
    c = s % 2
    sib = (b, s + 1 - 2 * c)
    zpart = (b + 1 - 2 * zl, s)

    def rcopy(src, dst, ss, rs, dev):
        return pltpu.make_async_remote_copy(
            src_ref=src, dst_ref=dst, send_sem=ss, recv_sem=rs, device_id=dev, device_id_type=MESH
        )

    def bytes_of(ref, sem):
        pltpu.make_async_copy(ref, ref, sem).wait()

    hx, hy = h // 4, lax.rem(h, 4)

    def chip(dx, dy):
        return lax.rem(hx + dx, 4) * 4 + lax.rem(hy + dy, 4)

    far = [chip(*o) for o in FAR]
    near = [h] + far[::-1]

    half = pl.ds(pl.multiple_of(64 * zl, 64), 64)
    loc = [
        pltpu.make_async_copy(k_hbm.at[c], kb.at[0], loc_sem.at[0]),
        pltpu.make_async_copy(v_hbm.at[c], vb.at[0], loc_sem.at[1]),
        pltpu.make_async_copy(q_hbm.at[c], qbuf.at[b], loc_sem.at[2]),
    ]
    for cp in (loc[2], loc[1], loc[0]):
        cp.start()

    barrier = pltpu.get_barrier_semaphore()
    for dz in range(2):
        for ds in range(4):
            if dz + ds:
                pl.semaphore_signal(
                    barrier, inc=1, device_id=(2 * h + (zl + dz) % 2, (s + ds) % 4), device_id_type=MESH
                )

    for p in far:
        pl.semaphore_signal(barrier, inc=1, device_id=(p * 2 + zl, s), device_id_type=MESH)
    pl.semaphore_wait(barrier, HEADS + 6)

    other = b + 1 - 2 * zl
    q1 = rcopy(q_hbm.at[c], qbuf.at[b], q_send.at[0], q_recv.at[0], zpart)
    q1.start()
    w_to = [
        (wt_hbm, wt.at[c, :, half, :], w_send.at[0], w_recv.at[2 * c + zl]),
        (wo_hbm, wob.at[c, half, :], w_send.at[1], w_recv.at[4 + 2 * c + zl]),
    ]
    w_away = [rcopy(*w, (other, 2 * zh + 1)) for w in w_to]

    @pl.when(c == 0)
    def _():
        for cp in w_away:
            cp.start()

    for p in far:
        rcopy(q_hbm.at[c], qbuf.at[b], q_send.at[0], q_recv.at[1], (p * 2 + zl, s)).start()
    kx = rcopy(k_hbm.at[1 - c], kb.at[1], kv_send.at[0], kv_recv.at[0], sib)
    vx = rcopy(v_hbm.at[1 - c], vb.at[1], kv_send.at[1], kv_recv.at[1], sib)
    gx = rcopy(gain_ref, gain2, g_sem.at[0], g_sem.at[1], sib)
    kx.start()
    vx.start()
    gx.start()
    w_sib = [rcopy(src, dst, w_send.at[2 + i], rs, sib) for i, (src, dst, _, rs) in enumerate(w_to)]
    w_here = [pltpu.make_async_copy(src, dst, rs) for src, dst, _, rs in w_to]

    @pl.when(c == 0)
    def _():
        for cp in w_sib:
            cp.start()

    @pl.when(c == 1)
    def _():
        for cp in w_here:
            cp.start()

    q1.wait_recv()
    for p in far:
        rcopy(qbuf.at[other], qbuf.at[other], q_send.at[0], q_recv.at[1], (p * 2 + zl, s)).start()

    loc[1].wait()
    for j in range(HEADS):
        vts[j, :, 0:ROWS] = vb[0, :, j * HD : (j + 1) * HD].T
    vx.wait_recv()
    for j in range(HEADS):
        vts[j, :, ROWS : 2 * ROWS] = vb[1, :, j * HD : (j + 1) * HD].T
    loc[0].wait()
    kx.wait_recv()
    loc[2].wait()
    bytes_of(qbuf.at[0:30], q_recv.at[1])

    def e_copy(m, t):
        p = lax.rem(h + t, HEADS)
        dst = p * 2 + 1 - m
        cols = pl.ds(pl.multiple_of(p * HD, HD), HD)
        return (
            e_hbm.at[m, :, cols],
            ebuf.at[b],
            dst,
        )

    @pl.when(s == 1)
    def _():
        for m in range(2):
            def e_start(t, _):
                src, dst_ref, dst = e_copy(m, t)
                rcopy(src, dst_ref, e_sem.at[0], e_sem.at[1], (dst, s)).start()
                return 0
            lax.fori_loop(1, HEADS, e_start, 0)
            src, dst_ref, dst = e_copy(m, 0)

            @pl.when(zl == 1 - m)
            def _():
                pltpu.make_async_copy(src, dst_ref, e_sem.at[1]).start()

            @pl.when(zl == m)
            def _():
                rcopy(src, dst_ref, e_sem.at[0], e_sem.at[1], (dst, s)).start()

    base0 = (b * 4 + s) * ROWS
    base1 = (b * 4 + s + 1 - 2 * c) * ROWS
    pos = pos_ref[pl.ds(c, 1), :]
    ids = lax.broadcasted_iota(jnp.int32, (ROWS, LAT), 0)
    scale = HD ** (-0.5)

    ids1 = ids + base1
    ids0 = ids + base0

    def scores(hh):
        cols = pl.ds(pl.multiple_of(hh * HD, HD), HD)
        qh = qbuf[:, :, cols].astype(f32).reshape(LAT, HD).astype(bf16)
        s0 = jnp.where(ids0 < pos, dot(kb[0, :, cols], qh, NT) * scale, masked)
        s1 = jnp.where(ids1 < pos, dot(kb[1, :, cols], qh, NT) * scale, masked)
        return s0, s1

    def weigh(s0, s1):
        top = jnp.maximum(jnp.max(jnp.maximum(s0, s1), axis=0, keepdims=True), 0.1 * masked)
        e0, e1 = jnp.exp(s0 - top), jnp.exp(s1 - top)
        total = jnp.sum(e0 + e1, axis=0, keepdims=True)
        return top, total, jnp.concatenate([e0.astype(bf16), e1.astype(bf16)], axis=0)

    order = far + [h]
    for g in range(0, HEADS, 2):
        group = order[g : g + 2]
        ss = [scores(hh) for hh in group]
        ws = [weigh(*v) for v in ss]
        for hh, (top, total, e) in zip(group, ws):
            ob[hh, 0:HD, :] = dot(vts[hh], e, NN).astype(bf16)
            ob[hh, HD:SR, :] = stat_rows(*split3(top), *split3(total))
        for i in range(g, g + 2):
            if i < HEADS - 1:
                hh = order[i]
                rcopy(ob.at[hh], r1.at[h], r1_sem.at[0], r1_sem.at[1], (hh * 2 + zl, s)).start()

    bytes_of(r1.at[0:15], r1_sem.at[1])
    r1[h] = ob[h]

    def combine(buf, n):
        st = [buf[i, HD:SR, :].astype(f32) for i in range(n)]
        tops = [stat3(v, 0) for v in st]
        top = tops[0]
        for v in tops[1:]:
            top = jnp.maximum(top, v)
        total = jnp.zeros((1, LAT), f32)
        acc = jnp.zeros((HD, LAT), f32)
        for i in range(n):
            w = jnp.exp(tops[i] - top)
            total = total + w * stat3(st[i], 3)
            acc = acc + w * buf[i, 0:HD, :].astype(f32)
        return acc, top, total

    acc, top, total = combine(r1, HEADS)
    r2o[0:HD, :] = acc.astype(bf16)
    r2o[HD:SR, :] = stat_rows(*split3(top), *split3(total))
    z = zh * 2 + zl
    r2_home = (s == 1) & (zl == 1 - c)
    r2_dst = (2 * h + 1 - c, 1)
    r2_copy = rcopy(r2o, r2.at[z], r2_sem.at[0], r2_sem.at[1], r2_dst)

    @pl.when(r2_home)
    def _():
        pltpu.make_async_copy(r2o, r2.at[z], r2_sem.at[1]).start()

    @pl.when(jnp.logical_not(r2_home))
    def _():
        r2_copy.start()

    @pl.when(c == 1)
    def _():
        for cp in w_away:
            cp.start()

    gx.wait_recv()
    my_cols = pl.ds(pl.multiple_of(h * HD, HD), HD)

    def column(ref):
        return jnp.broadcast_to(ref[:, my_cols], (HD, LAT)).T

    seg = h // 4
    jj = lax.broadcasted_iota(jnp.int32, (LAT, LAT), 0)
    ii = lax.broadcasted_iota(jnp.int32, (LAT, LAT), 1)

    def layer(k):
        for p in far:
            rcopy(xs.at[k], xb.at[k, h], x_send.at[k], x_recv.at[k, h], (p * 2 + zl, s)).start()
        pltpu.make_async_copy(xs.at[k], xb.at[k, h], x_recv.at[k, h]).start()
        for i in range(2):
            pltpu.make_async_copy(wt_hbm, wt.at[k, :, 0:64, :], w_recv.at[2 * k + i]).wait()
            pltpu.make_async_copy(wo_hbm, wob.at[k, 0:64, :], w_recv.at[4 + 2 * k + i]).wait()
        for j in range(HEADS):
            wot[k, j] = wob[k, :, j * HD : (j + 1) * HD].T
        if k == 1:

            @pl.when(s == 3)
            def _():
                fb[...] = xn[...].T.reshape(NB, 4, HD)
                sem = f_recv.at[0]
                dst = fx.at[zl, lax.rem(h, 4)]
                for p in far:
                    for dz in range(2):
                        rcopy(fb.at[2 * p + dz], dst, f_send.at[0], sem, (2 * p + dz, seg)).start()
                rcopy(fb.at[other], dst, f_send.at[0], sem, (other, seg)).start()

                @pl.when(seg != s)
                def _():
                    rcopy(fb.at[b], dst, f_send.at[0], sem, (b, seg)).start()

                @pl.when(seg == s)
                def _():
                    pltpu.make_async_copy(fb.at[b], dst, sem).start()

        qkv = jnp.zeros((3 * HD, LAT), f32)
        ss = jnp.zeros((1, LAT), f32)
        for j in range(0, HEADS, 2):
            pair = near[j : j + 2]
            for p in pair:
                pltpu.make_async_copy(xs.at[k], xb.at[k, p], x_recv.at[k, p]).wait()
            w2 = [wt[k, :, :, pl.ds(pl.multiple_of(p * HD, HD), HD)].reshape(3 * HD, HD) for p in pair]
            x2 = [xb[k, p, 0:HD, :] for p in pair]
            qkv = qkv + dot(jnp.concatenate(w2, axis=1), jnp.concatenate(x2, axis=0), NN)
            for p in pair:
                ss = ss + stat3(xb[k, p, HD:SR, :].astype(f32), 0)
        factor = lax.rsqrt(ss * (1.0 / D) + epsilon)
        qkv = (qkv * factor).astype(bf16)
        qt, kt, vt = qkv[0:HD], qkv[HD : 2 * HD], qkv[2 * HD :]
        sc = dot(kt, qt, TN) * scale
        sc = jnp.where(jj <= ii, sc, masked)
        e = jnp.exp(sc - jnp.max(sc, axis=0, keepdims=True))
        soft = (e / jnp.sum(e, axis=0, keepdims=True)).astype(bf16)
        return dot(vt, soft, NN).astype(bf16)

    def exchange(k, att, x0):
        for g in range(0, HEADS - 1, 5):
            us = [dot(wot[k, p], att, NN).astype(bf16) for p in far[g : g + 5]]
            for p, u in zip(far[g : g + 5], us):
                ub[k, p] = u
            for p in far[g : g + 5]:
                rcopy(ub.at[k, p], rb.at[k, h], u_send.at[k], u_recv.at[k], (p * 2 + zl, s)).start()
        x = x0 + dot(wot[k, h], att, NN)
        bytes_of(rb.at[k, 0:15], u_recv.at[k])
        for p in near[1:]:
            x = x + rb[k, p].astype(f32)
        return x

    def pack_x(k, x, gain):
        xs[k, 0:HD, :] = (x * gain).astype(bf16)
        xs[k, HD:SR, :] = stat_rows(*split3(jnp.sum(x * x, axis=0, keepdims=True)))

    @pl.when(c == 1)
    def _():
        @pl.when(s == 1)
        def _():
            bytes_of(ebuf, e_sem.at[1])
            emb = ebuf[...].astype(f32).reshape(LAT, HD).T
            bytes_of(r2, r2_sem.at[1])
            acc, top, total = combine(r2, 4)
            xr[...] = emb + acc / total

        @pl.when(s == 3)
        def _():
            pltpu.make_async_copy(xn, xr, xr_sem.at[1]).wait()

        pack_x(0, xr[...], column(gain2))
        x = exchange(0, layer(0), xr[...])
        xn[...] = x
        pack_x(1, x, column(gain_ref))
        att = layer(1)

        @pl.when(s == 1)
        def _():
            x = exchange(1, att, xn[...])
            fb2 = xr
            fb2[...] = x
            up = rcopy(fb2, xr, xr_sem.at[0], xr_sem.at[1], (other, 3))
            up.start()
            bytes_of(ub.at[1, 0:15], u_send.at[1])
            up.wait_send()

        @pl.when(s == 3)
        def _():
            att_r = att.T
            for n in range(4):
                u = dot(att_r, wob[1, :, n * 512 : (n + 1) * 512], NN)
                uf[n * NB : (n + 1) * NB] = u.reshape(NB, 4, 512).astype(bf16)
            sem = f_recv.at[1]
            dst = fu.at[zl, h]
            for p in far:
                for dz in range(2):
                    for n in range(4):
                        i = 2 * p + dz
                        rcopy(uf.at[n * NB + i], dst, f_send.at[1], sem, (i, n)).start()
            for n in range(4):
                rcopy(uf.at[n * NB + other], dst, f_send.at[1], sem, (other, n)).start()
            for n in range(3):
                rcopy(uf.at[n * NB + b], dst, f_send.at[1], sem, (b, n)).start()
            pltpu.make_async_copy(uf.at[3 * NB + b], dst, sem).start()
            bytes_of(uf.at[0:127], f_send.at[1])

            @pl.when(seg == s)
            def _():
                bytes_of(fb.at[0:31], f_send.at[0])

            @pl.when(seg != s)
            def _():
                bytes_of(fb, f_send.at[0])

        bytes_of(ub.at[0, 0:15], u_send.at[0])
        for k in range(2):
            bytes_of(xb.at[k, 0:15], x_send.at[k])

    bytes_of(qbuf.at[0:31], q_send.at[0])
    bytes_of(ob.at[0:15], r1_sem.at[0])
    for cp in [kx, vx, gx] + w_away:
        cp.wait_send()

    @pl.when(c == 0)
    def _():
        for cp in w_sib:
            cp.wait_send()

    @pl.when(jnp.logical_not(r2_home))
    def _():
        r2_copy.wait_send()

    @pl.when(s == 1)
    def _():
        bytes_of(ebuf.at[0:31], e_sem.at[0])

    bytes_of(fx, f_recv.at[0])
    bytes_of(fu, f_recv.at[1])
    for m in range(2):
        acc = jnp.concatenate([fx[m, i] for i in range(4)], axis=1)
        for i in range(HEADS):
            acc = acc + fu[m, i].astype(f32)
        out_ref[m] = acc


def on_device(
    latent_queries, latent_embed, history_keys, history_values, latent_pos, norm_gain, w_qkv, w_out
):
    wt = jnp.transpose(w_qkv[0], (1, 2, 0))
    hbm = pl.BlockSpec(memory_space=pl.ANY)
    vmem = pl.BlockSpec(memory_space=pltpu.VMEM)
    dma = pltpu.SemaphoreType.DMA
    return pl.pallas_call(
        kernel,
        out_shape=jax.ShapeDtypeStruct((2, 4, 512), f32),
        in_specs=[hbm, hbm, hbm, hbm, vmem, vmem, hbm, hbm],
        out_specs=vmem,
        scratch_shapes=[
            pltpu.VMEM((NB, 4, D), bf16),
            pltpu.VMEM((2, ROWS, D), bf16),
            pltpu.VMEM((2, ROWS, D), bf16),
            pltpu.VMEM((HEADS, HD, 2 * ROWS), bf16),
            pltpu.VMEM((2, 3, HD, D), bf16),
            pltpu.VMEM((2, HD, D), bf16),
            pltpu.VMEM((2, HEADS, HD, HD), bf16),
            pltpu.VMEM((1, D), f32),
            pltpu.VMEM((HEADS, SR, LAT), bf16),
            pltpu.VMEM((HEADS, SR, LAT), bf16),
            pltpu.VMEM((SR, LAT), bf16),
            pltpu.VMEM((4, SR, LAT), bf16),
            pltpu.VMEM((NB, 4, HD), bf16),
            pltpu.VMEM((2, SR, LAT), bf16),
            pltpu.VMEM((2, HEADS, SR, LAT), bf16),
            pltpu.VMEM((HD, LAT), f32),
            pltpu.VMEM((HD, LAT), f32),
            pltpu.VMEM((2, HEADS, HD, LAT), bf16),
            pltpu.VMEM((2, HEADS, HD, LAT), bf16),
            pltpu.VMEM((NB, 4, HD), f32),
            pltpu.VMEM((2, 4, 4, HD), f32),
            pltpu.VMEM((4 * NB, 4, 512), bf16),
            pltpu.VMEM((2, HEADS, 4, 512), bf16),
            dma((3,)), dma((2,)), dma((2,)), dma((4,)), dma((8,)), dma((2,)), dma((1,)), dma((2,)),
            dma((2,)), dma((2,)), dma((2,)), dma((2,)), dma((2, HEADS)), dma((2,)), dma((2,)), dma((2,)), dma((2,)), dma((2,)),
        ],
        compiler_params=pltpu.CompilerParams(
            collective_id=0, has_side_effects=True, vmem_limit_bytes=67043328
        ),
        name="ar_step",
    )(latent_queries, latent_embed, history_keys, history_values, latent_pos, norm_gain, wt, w_out[0])


def solution(mesh):
    return jax.shard_map(
        on_device,
        mesh=mesh,
        in_specs=(
            P(None, "blk", None),
            P(None, "blk", None),
            P(None, ("blk", "segment"), None),
            P(None, ("blk", "segment"), None),
            P(),
            P("segment", None),
            P("segment", None, None, "blk"),
            P("segment", "blk", None),
        ),
        out_specs=P(None, "blk", "segment"),
        check_vma=False,
    )
```

```python
import jax
import jax.numpy as jnp
from jax import lax
from jax.experimental import pallas as pl
from jax.experimental.pallas import tpu as pltpu
from jax.sharding import PartitionSpec as P

HEADS = 16
HD = 128
LAT = 128
D = 2048
ROWS = 256
NB = 32
SR = 144
epsilon = 1e-06
masked = -1e30
MESH = pl.DeviceIdType.MESH
f32, bf16 = jnp.float32, jnp.bfloat16
NN = (((1,), (0,)), ((), ()))
NT = (((1,), (1,)), ((), ()))
TN = (((0,), (0,)), ((), ()))


def hops(o):
    return sum(min(v, 4 - v) for v in o)


FAR = sorted(((dx, dy) for dx in range(4) for dy in range(4) if dx or dy), key=lambda o: -hops(o))
FAR3 = sorted(
    ((dx, dy, dz) for dx in range(4) for dy in range(4) for dz in range(2) if dx or dy or dz),
    key=lambda o: -hops(o),
)
HALVES = [
    sorted(((dx, dy) for dx in steps for dy in range(4)), key=lambda o: -hops(o)) for steps in ((2, 1), (3, 0))
]
NEAR = 10


def dot(a, b, dims):
    return lax.dot_general(a, b, dims, preferred_element_type=f32)


def split3(v):
    hi = v.astype(bf16).astype(f32)
    mid = (v - hi).astype(bf16).astype(f32)
    return hi, mid, v - hi - mid


def stat_rows(*rows):
    ids = lax.broadcasted_iota(jnp.int32, (16, LAT), 0)
    out = jnp.zeros((16, LAT), f32)
    for i, r in enumerate(rows):
        out = jnp.where(ids == i, jnp.broadcast_to(r, (16, LAT)), out)
    return out.astype(bf16)


def stat3(st, i):
    return st[i : i + 1] + st[i + 1 : i + 2] + st[i + 2 : i + 3]


def kernel(
    q_hbm, e_hbm, k_hbm, v_hbm, pos_hbm, gain_hbm, wt_hbm, wo_hbm, out_ref,
    pos_ref, gain_ref, qbuf, kb, vb, vts, wt, wob, wot, gain2, gain3, ob, r1, r2o, r2, ebuf, xs, xb, xr, xn, ub, rb, fb, fx, uf, fu,
    loc_sem, kv_send, kv_recv, w_send, w_recv, g_sem, q_send, q_recv,
    r1_sem, r2_sem, e_sem, x_send, x_recv, u_send, u_recv, xr_sem, f_send, f_recv,
):
    b = lax.axis_index("blk")
    s = lax.axis_index("segment")
    h = b // 2
    zl = b % 2
    zh = s // 2
    c = s % 2
    sib = (b, s + 1 - 2 * c)
    zpart = (b + 1 - 2 * zl, s)

    def rcopy(src, dst, ss, rs, dev):
        return pltpu.make_async_remote_copy(
            src_ref=src, dst_ref=dst, send_sem=ss, recv_sem=rs, device_id=dev, device_id_type=MESH
        )

    def bytes_of(ref, sem):
        pltpu.make_async_copy(ref, ref, sem).wait()

    hx, hy = h // 4, lax.rem(h, 4)

    def chip(dx, dy):
        return lax.rem(hx + dx, 4) * 4 + lax.rem(hy + dy, 4)

    far = [chip(*o) for o in FAR]
    near = [h] + far[::-1]

    half = pl.ds(pl.multiple_of(64 * zl, 64), 64)
    loc = [
        pltpu.make_async_copy(k_hbm.at[c], kb.at[0], loc_sem.at[0]),
        pltpu.make_async_copy(v_hbm.at[c], vb.at[0], loc_sem.at[1]),
        pltpu.make_async_copy(q_hbm.at[c], qbuf.at[b], loc_sem.at[2]),
        pltpu.make_async_copy(pos_hbm, pos_ref, loc_sem.at[3]),
        pltpu.make_async_copy(gain_hbm, gain_ref, loc_sem.at[4]),
    ]
    barrier = pltpu.get_barrier_semaphore()
    other = b + 1 - 2 * zl

    def pair_dev(dx, dy, dz):
        return chip(dx, dy) * 2 + (1 - zl if dz else zl)

    for o in FAR3:
        pl.semaphore_signal(barrier, inc=1, device_id=(pair_dev(*o), s), device_id_type=MESH)
    for blk in (b, other):
        for ds in range(1, 4):
            pl.semaphore_signal(barrier, inc=1, device_id=(blk, (s + ds) % 4), device_id_type=MESH)
    for cp in (loc[2], loc[1], loc[0], loc[3], loc[4]):
        cp.start()

    pl.semaphore_wait(barrier, 37)

    kx = rcopy(k_hbm.at[1 - c], kb.at[1], kv_send.at[0], kv_recv.at[0], sib)
    vx = rcopy(v_hbm.at[1 - c], vb.at[1], kv_send.at[1], kv_recv.at[1], sib)
    kx.start()
    vx.start()

    def q_start(half_no):
        for dx, dy, dz in FAR3:
            for step in ((2, 1), (3, 0))[half_no]:
                cols = pl.ds(pl.multiple_of(lax.rem(hx + dx + step, 4) * 512, 512), 512)
                rcopy(
                    q_hbm.at[c, :, cols], qbuf.at[b, :, cols], q_send.at[0], q_recv.at[half_no],
                    (pair_dev(dx, dy, dz), s),
                ).start()

    q_start(0)
    q_start(1)
    w_to = [
        (wt_hbm, wt.at[c, :, half, :], w_send.at[0], w_recv.at[2 * c + zl]),
        (wo_hbm, wob.at[c, half, :], w_send.at[1], w_recv.at[4 + 2 * c + zl]),
    ]
    w_away = [rcopy(*w, (other, 2 * zh + 1)) for w in w_to]

    @pl.when(c == 0)
    def _():
        w_away[0].start()

    gx = rcopy(gain_hbm, gain2, g_sem.at[0], g_sem.at[1], sib)
    gx.start()
    g3 = rcopy(gain_hbm, gain3, g_sem.at[2], g_sem.at[3], (other, 1))

    @pl.when(s == 2)
    def _():
        g3.start()

    w_sib = [rcopy(src, dst, w_send.at[2 + i], rs, sib) for i, (src, dst, _, rs) in enumerate(w_to)]
    w_here = [pltpu.make_async_copy(src, dst, rs) for src, dst, _, rs in w_to]

    @pl.when(c == 0)
    def _():
        for cp in w_sib:
            cp.start()

    @pl.when(c == 1)
    def _():
        for cp in w_here:
            cp.start()

    loc[1].wait()
    for j in range(HEADS):
        vts[j] = vb[0, :, j * HD : (j + 1) * HD].T
    loc[0].wait()
    kx.wait_recv()
    for cp in loc[2:]:
        cp.wait()
    bytes_of(qbuf.at[0:31, :, 0:1024], q_recv.at[0])

    def e_copy(m, t):
        p = lax.rem(h + t, HEADS)
        dst = p * 2 + 1 - m
        cols = pl.ds(pl.multiple_of(p * HD, HD), HD)
        return (
            e_hbm.at[m, :, cols],
            ebuf.at[b],
            dst,
        )

    @pl.when(s == 1)
    def _():
        for m in range(2):
            def e_start(t, _):
                src, dst_ref, dst = e_copy(m, t)
                rcopy(src, dst_ref, e_sem.at[0], e_sem.at[1], (dst, s)).start()
                return 0
            lax.fori_loop(1, HEADS, e_start, 0)
            src, dst_ref, dst = e_copy(m, 0)

            @pl.when(zl == 1 - m)
            def _():
                pltpu.make_async_copy(src, dst_ref, e_sem.at[1]).start()

            @pl.when(zl == m)
            def _():
                rcopy(src, dst_ref, e_sem.at[0], e_sem.at[1], (dst, s)).start()

    base0 = (b * 4 + s) * ROWS
    base1 = (b * 4 + s + 1 - 2 * c) * ROWS
    pos = pos_ref[pl.ds(c, 1), :]
    ids = lax.broadcasted_iota(jnp.int32, (ROWS, LAT), 0)
    scale = HD ** (-0.5)

    ids1 = ids + base1
    ids0 = ids + base0

    def scores(hh):
        cols = pl.ds(pl.multiple_of(hh * HD, HD), HD)
        qh = qbuf[:, :, cols].astype(f32).reshape(LAT, HD).astype(bf16)
        s0 = jnp.where(ids0 < pos, dot(kb[0, :, cols], qh, NT) * scale, masked)
        s1 = jnp.where(ids1 < pos, dot(kb[1, :, cols], qh, NT) * scale, masked)
        return s0, s1

    def weigh(s0, s1):
        top = jnp.maximum(jnp.max(jnp.maximum(s0, s1), axis=0, keepdims=True), 0.1 * masked)
        e0, e1 = jnp.exp(s0 - top), jnp.exp(s1 - top)
        total = jnp.sum(e0 + e1, axis=0, keepdims=True)
        return top, total, e0.astype(bf16), e1.astype(bf16)

    order = [chip(*o) for o in HALVES[0] + HALVES[1]]
    for g in range(0, HEADS, 2):
        if g == HEADS // 2:
            bytes_of(qbuf.at[0:31, :, 0:1024], q_recv.at[1])
        group = order[g : g + 2]
        ss = [scores(hh) for hh in group]
        ws = [weigh(*v) for v in ss]
        if g == 0:
            vx.wait_recv()
        for hh, (top, total, e0, e1) in zip(group, ws):
            cols = pl.ds(pl.multiple_of(hh * HD, HD), HD)
            ob[hh, 0:HD, :] = (dot(vts[hh], e0, NN) + dot(vb[1, :, cols].T, e1, NN)).astype(bf16)
            ob[hh, HD:SR, :] = stat_rows(*split3(top), *split3(total))
        for i in range(g, g + 2):
            if i < HEADS - 1:
                hh = order[i]
                rcopy(ob.at[hh], r1.at[h], r1_sem.at[0], r1_sem.at[1], (hh * 2 + zl, s)).start()

    bytes_of(r1.at[0:15], r1_sem.at[1])
    r1[h] = ob[h]

    def combine(buf, n):
        st = [buf[i, HD:SR, :].astype(f32) for i in range(n)]
        tops = [stat3(v, 0) for v in st]
        top = tops[0]
        for v in tops[1:]:
            top = jnp.maximum(top, v)
        total = jnp.zeros((1, LAT), f32)
        acc = jnp.zeros((HD, LAT), f32)
        for i in range(n):
            w = jnp.exp(tops[i] - top)
            total = total + w * stat3(st[i], 3)
            acc = acc + w * buf[i, 0:HD, :].astype(f32)
        return acc, top, total

    acc, top, total = combine(r1, HEADS)
    r2o[0:HD, :] = acc.astype(bf16)
    r2o[HD:SR, :] = stat_rows(*split3(top), *split3(total))
    z = zh * 2 + zl
    r2_home = (s == 1) & (zl == 1 - c)
    r2_dst = (2 * h + 1 - c, 1)
    r2_copy = rcopy(r2o, r2.at[z], r2_sem.at[0], r2_sem.at[1], r2_dst)

    @pl.when(r2_home)
    def _():
        pltpu.make_async_copy(r2o, r2.at[z], r2_sem.at[1]).start()

    @pl.when(jnp.logical_not(r2_home))
    def _():
        r2_copy.start()

    @pl.when(c == 1)
    def _():
        w_away[0].start()

    w_away[1].start()

    gx.wait_recv()
    my_cols = pl.ds(pl.multiple_of(h * HD, HD), HD)

    def column(ref):
        return jnp.broadcast_to(ref[:, my_cols], (HD, LAT)).T

    seg = h // 4
    jj = lax.broadcasted_iota(jnp.int32, (LAT, LAT), 0)
    ii = lax.broadcasted_iota(jnp.int32, (LAT, LAT), 1)

    halves = (slice(0, 64), slice(64, SR))

    def pack_x(k, i, x, gain, before):
        xs[k, 64 * i : 64 * i + 64, :] = (x * gain[64 * i : 64 * i + 64]).astype(bf16)
        ss = before + jnp.sum(x * x, axis=0, keepdims=True)
        if i:
            xs[k, HD:SR, :] = stat_rows(*split3(ss))
        return ss

    def gather(k, i):
        rows = halves[i]
        for n, p in enumerate(far):
            late = 1 if n < HEADS - NEAR else 0
            rcopy(
                xs.at[k, rows], xb.at[k, h, rows], x_send.at[k], x_recv.at[k, late], (p * 2 + zl, s)
            ).start()
        pltpu.make_async_copy(xs.at[k, rows], xb.at[k, h, rows], x_recv.at[k, 0]).start()

    def attend(k):
        for i in range(2):
            pltpu.make_async_copy(wt_hbm, wt.at[k, :, 0:64, :], w_recv.at[2 * k + i]).wait()
        if k == 1:

            @pl.when(s == 3)
            def _():
                fb[...] = xn[...].T.reshape(NB, 4, HD)
                sem = f_recv.at[0]
                dst = fx.at[zl, lax.rem(h, 4)]
                for p in far:
                    for dz in range(2):
                        rcopy(fb.at[2 * p + dz], dst, f_send.at[0], sem, (2 * p + dz, seg)).start()
                rcopy(fb.at[other], dst, f_send.at[0], sem, (other, seg)).start()

                @pl.when(seg != s)
                def _():
                    rcopy(fb.at[b], dst, f_send.at[0], sem, (b, seg)).start()

                @pl.when(seg == s)
                def _():
                    pltpu.make_async_copy(fb.at[b], dst, sem).start()

        qkv = jnp.zeros((3 * HD, LAT), f32)
        ss = jnp.zeros((1, LAT), f32)
        for j in range(0, HEADS, 2):
            pair = near[j : j + 2]
            if j == 0:
                bytes_of(xb.at[k, 0:NEAR], x_recv.at[k, 0])
            if j == NEAR:
                for i in range(2):
                    pltpu.make_async_copy(wo_hbm, wob.at[k, 0:64, :], w_recv.at[4 + 2 * k + i]).wait()
                for i in range(HEADS):
                    wot[k, i] = wob[k, :, i * HD : (i + 1) * HD].T
                bytes_of(xb.at[k, 0 : HEADS - NEAR], x_recv.at[k, 1])
            w2 = [wt[k, :, :, pl.ds(pl.multiple_of(p * HD, HD), HD)].reshape(3 * HD, HD) for p in pair]
            x2 = [xb[k, p, 0:HD, :] for p in pair]
            qkv = qkv + dot(jnp.concatenate(w2, axis=1), jnp.concatenate(x2, axis=0), NN)
            for p in pair:
                ss = ss + stat3(xb[k, p, HD:SR, :].astype(f32), 0)
        factor = lax.rsqrt(ss * (1.0 / D) + epsilon)
        qkv = (qkv * factor).astype(bf16)
        qt, kt, vt = qkv[0:HD], qkv[HD : 2 * HD], qkv[2 * HD :]
        sc = dot(kt, qt, TN) * scale
        sc = jnp.where(jj <= ii, sc, masked)
        e = jnp.exp(sc - jnp.max(sc, axis=0, keepdims=True))
        soft = (e / jnp.sum(e, axis=0, keepdims=True)).astype(bf16)
        return dot(vt, soft, NN).astype(bf16)

    def exchange(k, att, x_ref, done):
        for i in range(2):
            rows = slice(64 * i, 64 * i + 64)
            for g in range(0, HEADS - 1, 5):
                us = [dot(wot[k, p, rows, :], att, NN).astype(bf16) for p in far[g : g + 5]]
                for p, u in zip(far[g : g + 5], us):
                    ub[k, p, rows, :] = u
                for p in far[g : g + 5]:
                    rcopy(
                        ub.at[k, p, rows], rb.at[k, h, rows], u_send.at[k], u_recv.at[k, i], (p * 2 + zl, s)
                    ).start()
        own = dot(wot[k, h], att, NN)
        ss = jnp.zeros((1, LAT), f32)
        for i in range(2):
            rows = slice(64 * i, 64 * i + 64)
            x = x_ref[rows, :] + own[rows]
            bytes_of(rb.at[k, 0:15, rows], u_recv.at[k, i])
            for p in near[1:]:
                x = x + rb[k, p, rows, :].astype(f32)
            ss = done(i, x, ss)

    @pl.when(c == 1)
    def _():
        @pl.when(s == 1)
        def _():
            bytes_of(ebuf, e_sem.at[1])
            emb = ebuf[...].astype(f32).reshape(LAT, HD).T
            bytes_of(r2, r2_sem.at[1])
            acc, top, total = combine(r2, 4)
            xr[...] = emb + acc / total
            ss = jnp.zeros((1, LAT), f32)
            for i in range(2):
                ss = pack_x(0, i, xr[64 * i : 64 * i + 64, :], column(gain2), ss)
                gather(0, i)

        @pl.when(s == 3)
        def _():
            for i in range(2):
                bytes_of(xs.at[0, halves[i]], xr_sem.at[3 + i])
                gather(0, i)

        att = attend(0)

        @pl.when(s == 3)
        def _():
            bytes_of(xr, xr_sem.at[1])

        def to_next(i, x, ss):
            xn[64 * i : 64 * i + 64, :] = x
            ss = pack_x(1, i, x, column(gain_ref), ss)
            gather(1, i)
            return ss

        exchange(0, att, xr, to_next)
        att = attend(1)

        @pl.when(s == 1)
        def _():
            bytes_of(gain3, g_sem.at[3])

            def over(i):
                rows = halves[i]
                return rcopy(xs.at[2, rows], xs.at[0, rows], xr_sem.at[2], xr_sem.at[3 + i], (other, 3))

            def to_plane(i, x, ss):
                xr[64 * i : 64 * i + 64, :] = x
                ss = pack_x(2, i, x, column(gain3), ss)
                over(i).start()
                return ss

            exchange(1, att, xn, to_plane)
            up = rcopy(xr, xr, xr_sem.at[0], xr_sem.at[1], (other, 3))
            up.start()
            bytes_of(xs.at[2], xr_sem.at[2])
            bytes_of(ub.at[1, 0:15], u_send.at[1])
            up.wait_send()

        @pl.when(s == 3)
        def _():
            att_r = att.T
            for n in range(4):
                u = dot(att_r, wob[1, :, n * 512 : (n + 1) * 512], NN)
                uf[n * NB : (n + 1) * NB] = u.reshape(NB, 4, 512).astype(bf16)
            sem = f_recv.at[1]
            dst = fu.at[zl, h]
            for p in far:
                for dz in range(2):
                    for n in range(4):
                        i = 2 * p + dz
                        rcopy(uf.at[n * NB + i], dst, f_send.at[1], sem, (i, n)).start()
            for n in range(4):
                rcopy(uf.at[n * NB + other], dst, f_send.at[1], sem, (other, n)).start()
            for n in range(3):
                rcopy(uf.at[n * NB + b], dst, f_send.at[1], sem, (b, n)).start()
            pltpu.make_async_copy(uf.at[3 * NB + b], dst, sem).start()
            bytes_of(uf.at[0:127], f_send.at[1])

            @pl.when(seg == s)
            def _():
                bytes_of(fb.at[0:31], f_send.at[0])

            @pl.when(seg != s)
            def _():
                bytes_of(fb, f_send.at[0])

        bytes_of(ub.at[0, 0:15], u_send.at[0])
        for k in range(2):
            bytes_of(xb.at[k, 0:15], x_send.at[k])

    bytes_of(qbuf.at[0:31], q_send.at[0])
    bytes_of(ob.at[0:15], r1_sem.at[0])
    for cp in [kx, vx, gx] + w_away:
        cp.wait_send()

    @pl.when(c == 0)
    def _():
        for cp in w_sib:
            cp.wait_send()

    @pl.when(s == 2)
    def _():
        g3.wait_send()

    @pl.when(jnp.logical_not(r2_home))
    def _():
        r2_copy.wait_send()

    @pl.when(s == 1)
    def _():
        bytes_of(ebuf.at[0:31], e_sem.at[0])

    bytes_of(fx, f_recv.at[0])
    bytes_of(fu, f_recv.at[1])
    for m in range(2):
        acc = jnp.concatenate([fx[m, i] for i in range(4)], axis=1)
        for i in range(HEADS):
            acc = acc + fu[m, i].astype(f32)
        out_ref[m] = acc


def on_device(
    latent_queries, latent_embed, history_keys, history_values, latent_pos, norm_gain, w_qkv, w_out
):
    wt = jnp.transpose(w_qkv[0], (1, 2, 0))
    hbm = pl.BlockSpec(memory_space=pl.ANY)
    vmem = pl.BlockSpec(memory_space=pltpu.VMEM)
    dma = pltpu.SemaphoreType.DMA
    return pl.pallas_call(
        kernel,
        out_shape=jax.ShapeDtypeStruct((2, 4, 512), f32),
        in_specs=[hbm] * 8,
        out_specs=vmem,
        scratch_shapes=[
            pltpu.VMEM((2, LAT), jnp.int32),
            pltpu.VMEM((1, D), f32),
            pltpu.VMEM((NB, 4, D), bf16),
            pltpu.VMEM((2, ROWS, D), bf16),
            pltpu.VMEM((2, ROWS, D), bf16),
            pltpu.VMEM((HEADS, HD, ROWS), bf16),
            pltpu.VMEM((2, 3, HD, D), bf16),
            pltpu.VMEM((2, HD, D), bf16),
            pltpu.VMEM((2, HEADS, HD, HD), bf16),
            pltpu.VMEM((1, D), f32),
            pltpu.VMEM((1, D), f32),
            pltpu.VMEM((HEADS, SR, LAT), bf16),
            pltpu.VMEM((HEADS, SR, LAT), bf16),
            pltpu.VMEM((SR, LAT), bf16),
            pltpu.VMEM((4, SR, LAT), bf16),
            pltpu.VMEM((NB, 4, HD), bf16),
            pltpu.VMEM((3, SR, LAT), bf16),
            pltpu.VMEM((2, HEADS, SR, LAT), bf16),
            pltpu.VMEM((HD, LAT), f32),
            pltpu.VMEM((HD, LAT), f32),
            pltpu.VMEM((2, HEADS, HD, LAT), bf16),
            pltpu.VMEM((2, HEADS, HD, LAT), bf16),
            pltpu.VMEM((NB, 4, HD), f32),
            pltpu.VMEM((2, 4, 4, HD), f32),
            pltpu.VMEM((4 * NB, 4, 512), bf16),
            pltpu.VMEM((2, HEADS, 4, 512), bf16),
            dma((5,)), dma((2,)), dma((2,)), dma((4,)), dma((8,)), dma((4,)), dma((1,)), dma((2,)),
            dma((2,)), dma((2,)), dma((2,)), dma((2,)), dma((2, 2)), dma((2,)), dma((2, 2)), dma((5,)), dma((2,)), dma((2,)),
        ],
        compiler_params=pltpu.CompilerParams(
            collective_id=0, has_side_effects=True, vmem_limit_bytes=67043328
        ),
        name="ar_step",
    )(latent_queries, latent_embed, history_keys, history_values, latent_pos, norm_gain, wt, w_out[0])


def solution(mesh):
    return jax.shard_map(
        on_device,
        mesh=mesh,
        in_specs=(
            P(None, "blk", None),
            P(None, "blk", None),
            P(None, ("blk", "segment"), None),
            P(None, ("blk", "segment"), None),
            P(),
            P("segment", None),
            P("segment", None, None, "blk"),
            P("segment", "blk", None),
        ),
        out_specs=P(None, "blk", "segment"),
        check_vma=False,
    )
```

```python
import jax
import jax.numpy as jnp
from jax import lax
from jax.experimental import pallas as pl
from jax.experimental.pallas import tpu as pltpu
from jax.sharding import PartitionSpec as P

HEADS = 16
HD = 128
LAT = 128
D = 2048
ROWS = 256
NB = 32
SR = 144
epsilon = 1e-06
masked = -1e30
MESH = pl.DeviceIdType.MESH
f32, bf16 = jnp.float32, jnp.bfloat16
NN = (((1,), (0,)), ((), ()))
NT = (((1,), (1,)), ((), ()))
TN = (((0,), (0,)), ((), ()))


def hops(o):
    return sum(min(v, 4 - v) for v in o)


FAR = sorted(((dx, dy) for dx in range(4) for dy in range(4) if dx or dy), key=lambda o: -hops(o))
FAR3 = sorted(
    ((dx, dy, dz) for dx in range(4) for dy in range(4) for dz in range(2) if dx or dy or dz),
    key=lambda o: -hops(o),
)
HALVES = [
    sorted(((dx, dy) for dx in steps for dy in range(4)), key=lambda o: -hops(o)) for steps in ((2, 1), (3, 0))
]
NEAR = 10


def dot(a, b, dims):
    return lax.dot_general(a, b, dims, preferred_element_type=f32)


def split3(v):
    hi = v.astype(bf16).astype(f32)
    mid = (v - hi).astype(bf16).astype(f32)
    return hi, mid, v - hi - mid


def stat_rows(*rows):
    ids = lax.broadcasted_iota(jnp.int32, (16, LAT), 0)
    out = jnp.zeros((16, LAT), f32)
    for i, r in enumerate(rows):
        out = jnp.where(ids == i, jnp.broadcast_to(r, (16, LAT)), out)
    return out.astype(bf16)


def stat3(st, i):
    return st[i : i + 1] + st[i + 1 : i + 2] + st[i + 2 : i + 3]


def kernel(
    q_hbm, e_hbm, k_hbm, v_hbm, pos_hbm, gain_hbm, wt_hbm, wo_hbm, out_ref,
    pos_ref, gains, qbuf, kb, vb, vts, wt, wob, wot, ob, r1, r2o, r2, ebuf, xs, xb, xf, ub, rb, fb, fx, uf, fu,
    loc_sem, kv_send, kv_recv, w_send, w_recv, g_sem, q_send, q_recv,
    r1_sem, r2_sem, e_sem, x_send, x_recv, u_send, u_recv, f_send, f_recv, go_sem,
):
    b = lax.axis_index("blk")
    s = lax.axis_index("segment")
    h = b // 2
    zl = b % 2
    zh = s // 2
    c = s % 2
    sib = (b, s + 1 - 2 * c)
    zpart = (b + 1 - 2 * zl, s)

    def rcopy(src, dst, ss, rs, dev):
        return pltpu.make_async_remote_copy(
            src_ref=src, dst_ref=dst, send_sem=ss, recv_sem=rs, device_id=dev, device_id_type=MESH
        )

    def bytes_of(ref, sem):
        pltpu.make_async_copy(ref, ref, sem).wait()

    hx, hy = h // 4, lax.rem(h, 4)

    def chip(dx, dy):
        return lax.rem(hx + dx, 4) * 4 + lax.rem(hy + dy, 4)

    far = [chip(*o) for o in FAR]
    near = [h] + far[::-1]

    half = pl.ds(pl.multiple_of(64 * zl, 64), 64)
    loc = [
        pltpu.make_async_copy(k_hbm.at[c], kb.at[0], loc_sem.at[0]),
        pltpu.make_async_copy(v_hbm.at[c], vb.at[0], loc_sem.at[1]),
        pltpu.make_async_copy(q_hbm.at[c], qbuf.at[b], loc_sem.at[2]),
        pltpu.make_async_copy(pos_hbm, pos_ref, loc_sem.at[3]),
    ]
    barrier = pltpu.get_barrier_semaphore()
    other = b + 1 - 2 * zl

    def pair_dev(dx, dy, dz):
        return chip(dx, dy) * 2 + (1 - zl if dz else zl)

    for o in FAR3:
        pl.semaphore_signal(barrier, inc=1, device_id=(pair_dev(*o), s), device_id_type=MESH)
    for blk in (b, other):
        for ds in range(1, 4):
            pl.semaphore_signal(barrier, inc=1, device_id=(blk, (s + ds) % 4), device_id_type=MESH)
    for cp in (loc[2], loc[1], loc[0], loc[3]):
        cp.start()

    pl.semaphore_wait(barrier, 37)

    kx = rcopy(k_hbm.at[1 - c], kb.at[1], kv_send.at[0], kv_recv.at[0], sib)
    vx = rcopy(v_hbm.at[1 - c], vb.at[1], kv_send.at[1], kv_recv.at[1], sib)
    kx.start()
    vx.start()

    def q_start(half_no):
        for dx, dy, dz in FAR3:
            for step in ((2, 1), (3, 0))[half_no]:
                cols = pl.ds(pl.multiple_of(lax.rem(hx + dx + step, 4) * 512, 512), 512)
                rcopy(
                    q_hbm.at[c, :, cols], qbuf.at[b, :, cols], q_send.at[0], q_recv.at[half_no],
                    (pair_dev(dx, dy, dz), s),
                ).start()

    q_start(0)
    q_start(1)
    w_to = [
        (wt_hbm, wt.at[s, :, half, :], w_recv.at[s]),
        (wo_hbm, wob.at[s, half, :], w_recv.at[4 + s]),
    ]
    w_away = [rcopy(src, dst, w_send.at[i], rs, (other, 1)) for i, (src, dst, rs) in enumerate(w_to)]
    w_same = [rcopy(src, dst, w_send.at[2 + i], rs, (b, 1)) for i, (src, dst, rs) in enumerate(w_to)]
    gx = rcopy(gain_hbm, gains.at[s], g_sem.at[0], g_sem.at[1], (b, 1))

    @pl.when(s == 1)
    def _():
        for src, dst, rs in w_to:
            pltpu.make_async_copy(src, dst, rs).start()
        pltpu.make_async_copy(gain_hbm, gains.at[s], g_sem.at[1]).start()

    @pl.when(s != 1)
    def _():
        gx.start()
        w_away[0].start()

    @pl.when(s == 0)
    def _():
        w_away[1].start()
        for cp in w_same:
            cp.start()

    loc[1].wait()
    for j in range(HEADS):
        vts[j] = vb[0, :, j * HD : (j + 1) * HD].T
    loc[0].wait()
    kx.wait_recv()
    for cp in loc[2:]:
        cp.wait()
    bytes_of(qbuf.at[0:31, :, 0:1024], q_recv.at[0])

    def e_copy(m, t):
        p = lax.rem(h + t, HEADS)
        dst = p * 2 + 1 - m
        cols = pl.ds(pl.multiple_of(p * HD, HD), HD)
        return (
            e_hbm.at[m, :, cols],
            ebuf.at[b],
            dst,
        )

    @pl.when(s == 1)
    def _():
        for m in range(2):
            def e_start(t, _):
                src, dst_ref, dst = e_copy(m, t)
                rcopy(src, dst_ref, e_sem.at[0], e_sem.at[1], (dst, s)).start()
                return 0
            lax.fori_loop(1, HEADS, e_start, 0)
            src, dst_ref, dst = e_copy(m, 0)

            @pl.when(zl == 1 - m)
            def _():
                pltpu.make_async_copy(src, dst_ref, e_sem.at[1]).start()

            @pl.when(zl == m)
            def _():
                rcopy(src, dst_ref, e_sem.at[0], e_sem.at[1], (dst, s)).start()

    base0 = (b * 4 + s) * ROWS
    base1 = (b * 4 + s + 1 - 2 * c) * ROWS
    pos = pos_ref[pl.ds(c, 1), :]
    ids = lax.broadcasted_iota(jnp.int32, (ROWS, LAT), 0)
    scale = HD ** (-0.5)

    ids1 = ids + base1
    ids0 = ids + base0

    def scores(hh):
        cols = pl.ds(pl.multiple_of(hh * HD, HD), HD)
        qh = qbuf[:, :, cols].astype(f32).reshape(LAT, HD).astype(bf16)
        s0 = jnp.where(ids0 < pos, dot(kb[0, :, cols], qh, NT) * scale, masked)
        s1 = jnp.where(ids1 < pos, dot(kb[1, :, cols], qh, NT) * scale, masked)
        return s0, s1

    def weigh(s0, s1):
        top = jnp.maximum(jnp.max(jnp.maximum(s0, s1), axis=0, keepdims=True), 0.1 * masked)
        e0, e1 = jnp.exp(s0 - top), jnp.exp(s1 - top)
        total = jnp.sum(e0 + e1, axis=0, keepdims=True)
        return top, total, e0.astype(bf16), e1.astype(bf16)

    order = [chip(*o) for o in HALVES[0] + HALVES[1]]
    for g in range(0, HEADS, 2):
        if g == HEADS // 2:
            bytes_of(qbuf.at[0:31, :, 0:1024], q_recv.at[1])
        group = order[g : g + 2]
        ss = [scores(hh) for hh in group]
        ws = [weigh(*v) for v in ss]
        if g == 0:
            vx.wait_recv()
        for hh, (top, total, e0, e1) in zip(group, ws):
            cols = pl.ds(pl.multiple_of(hh * HD, HD), HD)
            ob[hh, 0:HD, :] = (dot(vts[hh], e0, NN) + dot(vb[1, :, cols].T, e1, NN)).astype(bf16)
            ob[hh, HD:SR, :] = stat_rows(*split3(top), *split3(total))
        for i in range(g, g + 2):
            if i < HEADS - 1:
                hh = order[i]
                rcopy(ob.at[hh], r1.at[h], r1_sem.at[0], r1_sem.at[1], (hh * 2 + zl, s)).start()

    bytes_of(r1.at[0:15], r1_sem.at[1])
    r1[h] = ob[h]

    def combine(buf, n):
        st = [buf[i, HD:SR, :].astype(f32) for i in range(n)]
        tops = [stat3(v, 0) for v in st]
        top = tops[0]
        for v in tops[1:]:
            top = jnp.maximum(top, v)
        total = jnp.zeros((1, LAT), f32)
        acc = jnp.zeros((HD, LAT), f32)
        for i in range(n):
            w = jnp.exp(tops[i] - top)
            total = total + w * stat3(st[i], 3)
            acc = acc + w * buf[i, 0:HD, :].astype(f32)
        return acc, top, total

    acc, top, total = combine(r1, HEADS)
    r2o[0:HD, :] = acc.astype(bf16)
    r2o[HD:SR, :] = stat_rows(*split3(top), *split3(total))
    z = zh * 2 + zl
    r2_home = (s == 1) & (zl == 1 - c)
    r2_dst = (2 * h + 1 - c, 1)
    r2_copy = rcopy(r2o, r2.at[z], r2_sem.at[0], r2_sem.at[1], r2_dst)

    @pl.when(r2_home)
    def _():
        pltpu.make_async_copy(r2o, r2.at[z], r2_sem.at[1]).start()

    @pl.when(jnp.logical_not(r2_home))
    def _():
        r2_copy.start()

    @pl.when(zh == 1)
    def _():
        pl.semaphore_wait(go_sem, 2)
        for cp in [w_away[1]] + w_same:
            cp.start()

    my_cols = pl.ds(pl.multiple_of(h * HD, HD), HD)

    def column(k):
        return jnp.broadcast_to(gains[k, :, my_cols], (HD, LAT)).T

    seg = h // 4
    jj = lax.broadcasted_iota(jnp.int32, (LAT, LAT), 0)
    ii = lax.broadcasted_iota(jnp.int32, (LAT, LAT), 1)

    halves = (slice(0, 64), slice(64, SR))

    def pack_x(k, i, x, gain, before):
        xs[k, 64 * i : 64 * i + 64, :] = (x * gain[64 * i : 64 * i + 64]).astype(bf16)
        ss = before + jnp.sum(x * x, axis=0, keepdims=True)
        if i:
            xs[k, HD:SR, :] = stat_rows(*split3(ss))
        return ss

    def gather(k, i):
        rows = halves[i]
        for n, p in enumerate(far):
            late = 1 if n < HEADS - NEAR else 0
            rcopy(
                xs.at[k, rows], xb.at[k, h, rows], x_send.at[0], x_recv.at[k, late], (p * 2 + zl, s)
            ).start()
        pltpu.make_async_copy(xs.at[k, rows], xb.at[k, h, rows], x_recv.at[k, 0]).start()

    def attend(k):
        bytes_of(wt.at[k], w_recv.at[k])
        if k == 3:
            fb[...] = xf[k].T.reshape(NB, 4, HD)
            sem = f_recv.at[0]
            dst = fx.at[1 - zl, lax.rem(h, 4)]
            for p in far:
                for dz in range(2):
                    rcopy(fb.at[2 * p + dz], dst, f_send.at[0], sem, (2 * p + dz, seg)).start()
            rcopy(fb.at[other], dst, f_send.at[0], sem, (other, seg)).start()

            @pl.when(seg != s)
            def _():
                rcopy(fb.at[b], dst, f_send.at[0], sem, (b, seg)).start()

            @pl.when(seg == s)
            def _():
                pltpu.make_async_copy(fb.at[b], dst, sem).start()

        qkv = jnp.zeros((3 * HD, LAT), f32)
        ss = jnp.zeros((1, LAT), f32)
        for j in range(0, HEADS, 2):
            pair = near[j : j + 2]
            if j == 0:
                bytes_of(xb.at[k, 0:NEAR], x_recv.at[k, 0])
            if j == NEAR:
                bytes_of(wob.at[k], w_recv.at[4 + k])
                for i in range(HEADS if k < 3 else 0):
                    wot[k, i] = wob[k, :, i * HD : (i + 1) * HD].T
                bytes_of(xb.at[k, 0 : HEADS - NEAR], x_recv.at[k, 1])
            w2 = [wt[k, :, :, pl.ds(pl.multiple_of(p * HD, HD), HD)].reshape(3 * HD, HD) for p in pair]
            x2 = [xb[k, p, 0:HD, :] for p in pair]
            qkv = qkv + dot(jnp.concatenate(w2, axis=1), jnp.concatenate(x2, axis=0), NN)
            for p in pair:
                ss = ss + stat3(xb[k, p, HD:SR, :].astype(f32), 0)
        factor = lax.rsqrt(ss * (1.0 / D) + epsilon)
        qkv = (qkv * factor).astype(bf16)
        qt, kt, vt = qkv[0:HD], qkv[HD : 2 * HD], qkv[2 * HD :]
        sc = dot(kt, qt, TN) * scale
        sc = jnp.where(jj <= ii, sc, masked)
        e = jnp.exp(sc - jnp.max(sc, axis=0, keepdims=True))
        soft = (e / jnp.sum(e, axis=0, keepdims=True)).astype(bf16)
        return dot(vt, soft, NN).astype(bf16)

    def exchange(k, att):
        for i in range(2):
            rows = slice(64 * i, 64 * i + 64)
            for group in (far[0:5], far[5:15]) if i == 0 else (far,):
                us = [dot(wot[k, p, rows, :], att, NN).astype(bf16) for p in group]
                for p, u in zip(group, us):
                    ub[k, p, rows, :] = u
                for p in group:
                    rcopy(
                        ub.at[k, p, rows], rb.at[k, h, rows], u_send.at[0], u_recv.at[k, i], (p * 2 + zl, s)
                    ).start()
        own = dot(wot[k, h], att, NN)
        ss = jnp.zeros((1, LAT), f32)
        for i in range(2):
            rows = slice(64 * i, 64 * i + 64)
            x = xf[k, rows, :] + own[rows]
            bytes_of(rb.at[k, 0:15, rows], u_recv.at[k, i])
            for p in near[1:]:
                x = x + rb[k, p, rows, :].astype(f32)
            xf[k + 1, rows, :] = x
            ss = pack_x(k + 1, i, x, column(k + 1), ss)
            gather(k + 1, i)

    @pl.when(s == 1)
    def _():
        bytes_of(gains, g_sem.at[1])
        bytes_of(ebuf, e_sem.at[1])
        emb = ebuf[...].astype(f32).reshape(LAT, HD).T
        bytes_of(r2, r2_sem.at[1])
        acc, top, total = combine(r2, 4)
        x0 = emb + acc / total
        xf[0] = x0
        ss = jnp.zeros((1, LAT), f32)
        for i in range(2):
            ss = pack_x(0, i, x0[64 * i : 64 * i + 64], column(0), ss)
            gather(0, i)

        def signal(dev):
            pl.semaphore_signal(go_sem, inc=1, device_id=dev, device_id_type=MESH)

        signal((other, 1))
        signal((b, 2))
        signal((other, 2))
        pl.semaphore_wait(go_sem, 1)
        for cp in w_away:
            cp.start()
        exchange(0, attend(0))
        signal((b, 3))
        signal((other, 3))
        for k in range(1, 3):
            exchange(k, attend(k))
        att = attend(3)
        att_r = att.T
        sem = f_recv.at[1]
        dst = fu.at[1 - zl, h]
        for n in range(4):
            u = dot(att_r, wob[3, :, n * 512 : (n + 1) * 512], NN)
            uf[n * NB : (n + 1) * NB] = u.reshape(NB, 4, 512).astype(bf16)
        for p in far:
            for dz in range(2):
                for n in range(4):
                    i = 2 * p + dz
                    rcopy(uf.at[n * NB + i], dst, f_send.at[1], sem, (i, n)).start()
        for n in range(4):
            rcopy(uf.at[n * NB + other], dst, f_send.at[1], sem, (other, n)).start()
        for n in (0, 2, 3):
            rcopy(uf.at[n * NB + b], dst, f_send.at[1], sem, (b, n)).start()
        pltpu.make_async_copy(uf.at[NB + b], dst, sem).start()
        bytes_of(uf.at[0:127], f_send.at[1])

        @pl.when(seg == s)
        def _():
            bytes_of(fb.at[0:31], f_send.at[0])

        @pl.when(seg != s)
        def _():
            bytes_of(fb, f_send.at[0])

        bytes_of(ub.at[:, 0:15], u_send.at[0])
        bytes_of(xb.at[:, 0:15], x_send.at[0])

    bytes_of(qbuf.at[0:31], q_send.at[0])
    bytes_of(ob.at[0:15], r1_sem.at[0])
    for cp in [kx, vx] + w_away:
        cp.wait_send()

    @pl.when(s != 1)
    def _():
        for cp in [gx] + w_same:
            cp.wait_send()

    @pl.when(jnp.logical_not(r2_home))
    def _():
        r2_copy.wait_send()

    @pl.when(s == 1)
    def _():
        bytes_of(ebuf.at[0:31], e_sem.at[0])

    bytes_of(fx, f_recv.at[0])
    bytes_of(fu, f_recv.at[1])
    for m in range(2):
        acc = jnp.concatenate([fx[m, i] for i in range(4)], axis=1)
        for i in range(HEADS):
            acc = acc + fu[m, i].astype(f32)
        out_ref[m] = acc


def on_device(
    latent_queries, latent_embed, history_keys, history_values, latent_pos, norm_gain, w_qkv, w_out
):
    wt = jnp.transpose(w_qkv[0], (1, 2, 0))
    hbm = pl.BlockSpec(memory_space=pl.ANY)
    vmem = pl.BlockSpec(memory_space=pltpu.VMEM)
    dma = pltpu.SemaphoreType.DMA
    return pl.pallas_call(
        kernel,
        out_shape=jax.ShapeDtypeStruct((2, 4, 512), f32),
        in_specs=[hbm] * 8,
        out_specs=vmem,
        scratch_shapes=[
            pltpu.VMEM((2, LAT), jnp.int32),
            pltpu.VMEM((4, 1, D), f32),
            pltpu.VMEM((NB, 4, D), bf16),
            pltpu.VMEM((2, ROWS, D), bf16),
            pltpu.VMEM((2, ROWS, D), bf16),
            pltpu.VMEM((HEADS, HD, ROWS), bf16),
            pltpu.VMEM((4, 3, HD, D), bf16),
            pltpu.VMEM((4, HD, D), bf16),
            pltpu.VMEM((3, HEADS, HD, HD), bf16),
            pltpu.VMEM((HEADS, SR, LAT), bf16),
            pltpu.VMEM((HEADS, SR, LAT), bf16),
            pltpu.VMEM((SR, LAT), bf16),
            pltpu.VMEM((4, SR, LAT), bf16),
            pltpu.VMEM((NB, 4, HD), bf16),
            pltpu.VMEM((4, SR, LAT), bf16),
            pltpu.VMEM((4, HEADS, SR, LAT), bf16),
            pltpu.VMEM((4, HD, LAT), f32),
            pltpu.VMEM((3, HEADS, HD, LAT), bf16),
            pltpu.VMEM((3, HEADS, HD, LAT), bf16),
            pltpu.VMEM((NB, 4, HD), f32),
            pltpu.VMEM((2, 4, 4, HD), f32),
            pltpu.VMEM((4 * NB, 4, 512), bf16),
            pltpu.VMEM((2, HEADS, 4, 512), bf16),
            dma((4,)), dma((2,)), dma((2,)), dma((4,)), dma((8,)), dma((2,)), dma((1,)), dma((2,)),
            dma((2,)), dma((2,)), dma((2,)), dma((1,)), dma((4, 2)), dma((1,)), dma((3, 2)), dma((2,)), dma((2,)),
            pltpu.SemaphoreType.REGULAR,
        ],
        compiler_params=pltpu.CompilerParams(
            collective_id=0, has_side_effects=True, vmem_limit_bytes=67043328
        ),
        name="ar_step",
    )(latent_queries, latent_embed, history_keys, history_values, latent_pos, norm_gain, wt, w_out[0])


def solution(mesh):
    return jax.shard_map(
        on_device,
        mesh=mesh,
        in_specs=(
            P(None, "blk", None),
            P(None, "blk", None),
            P(None, ("blk", "segment"), None),
            P(None, ("blk", "segment"), None),
            P(),
            P("segment", None),
            P("segment", None, None, "blk"),
            P("segment", "blk", None),
        ),
        out_specs=P(None, "blk", "segment"),
        check_vma=False,
    )
```

```python
import jax
import jax.numpy as jnp
from jax import lax
from jax.experimental import pallas as pl
from jax.experimental.pallas import tpu as pltpu
from jax.sharding import PartitionSpec as P

HEADS = 16
HD = 128
LAT = 128
D = 2048
ROWS = 256
NB = 32
epsilon = 1e-06
masked = -1e30
MESH = pl.DeviceIdType.MESH
f32, bf16 = jnp.float32, jnp.bfloat16
NN = (((1,), (0,)), ((), ()))
NT = (((1,), (1,)), ((), ()))
TN = (((0,), (0,)), ((), ()))


def hops(o):
    return sum(min(v, 4 - v) for v in o)


FAR = [divmod(o, 10) for o in (22, 12, 32, 21, 23, 11, 13, 31, 33, 2, 20, 1, 3, 10, 30)]
FAR3 = sorted(
    ((dx, dy, dz) for dx in range(4) for dy in range(4) for dz in range(2) if dx or dy or dz),
    key=lambda o: -hops(o),
)
HALVES = [
    sorted(((dx, dy) for dx in steps for dy in range(4)), key=lambda o: -hops(o)) for steps in ((2, 1), (3, 0))
]
NEARS = [divmod(o, 10) for o in (1, 3, 10, 30, 2, 11, 13, 31, 33, 20, 12, 32, 21, 23, 22)]
NEAR = 10


def dot(a, b, dims):
    return lax.dot_general(a, b, dims, preferred_element_type=f32)


def kernel(
    q_hbm, e_hbm, k_hbm, v_hbm, pos_hbm, gain_hbm, wt_hbm, wo_hbm, out_ref,
    pos_ref, gains, qbuf, kb, vb, vts, wt, wob, wot, ob, obs, r1, r1s, r2o, r2os, r2, r2s, ebuf, xs, xss, xb, xbs, xf, ub, rb, fb, fx, uf, fu,
    loc_sem, kv_send, kv_recv, w_send, w_recv, g_sem, q_send, q_recv,
    r1_sem, r2_sem, e_sem, x_send, x_recv, u_send, u_recv, f_send, f_recv, go_sem,
):
    b = lax.axis_index("blk")
    s = lax.axis_index("segment")
    h = b // 2
    zl = b % 2
    zh = s // 2
    c = s % 2
    sib = (b, s + 1 - 2 * c)
    zpart = (b + 1 - 2 * zl, s)

    def rcopy(src, dst, ss, rs, dev):
        return pltpu.make_async_remote_copy(
            src_ref=src, dst_ref=dst, send_sem=ss, recv_sem=rs, device_id=dev, device_id_type=MESH
        )

    def bytes_of(ref, sem):
        pltpu.make_async_copy(ref, ref, sem).wait()

    hx, hy = h // 4, lax.rem(h, 4)

    def chip(dx, dy):
        return lax.rem(hx + dx, 4) * 4 + lax.rem(hy + dy, 4)

    far = [chip(*o) for o in FAR]
    near = [h] + [chip(*o) for o in NEARS]

    half = pl.ds(pl.multiple_of(64 * zl, 64), 64)
    loc = [
        pltpu.make_async_copy(k_hbm.at[c], kb.at[0], loc_sem.at[0]),
        pltpu.make_async_copy(v_hbm.at[c], vb.at[0], loc_sem.at[1]),
        pltpu.make_async_copy(q_hbm.at[c], qbuf.at[b], loc_sem.at[2]),
        pltpu.make_async_copy(pos_hbm, pos_ref, loc_sem.at[3]),
    ]
    barrier = pltpu.get_barrier_semaphore()
    other = b + 1 - 2 * zl

    def pair_dev(dx, dy, dz):
        return chip(dx, dy) * 2 + (1 - zl if dz else zl)

    for o in FAR3:
        pl.semaphore_signal(barrier, inc=1, device_id=(pair_dev(*o), s), device_id_type=MESH)
    for blk in (b, other):
        for ds in range(1, 4):
            pl.semaphore_signal(barrier, inc=1, device_id=(blk, (s + ds) % 4), device_id_type=MESH)
    for cp in (loc[2], loc[1], loc[0], loc[3]):
        cp.start()

    pl.semaphore_wait(barrier, 37)

    kx = rcopy(k_hbm.at[1 - c], kb.at[1], kv_send.at[0], kv_recv.at[0], sib)
    vx = rcopy(v_hbm.at[1 - c], vb.at[1], kv_send.at[1], kv_recv.at[1], sib)
    kx.start()
    vx.start()

    def q_start(half_no):
        for dx, dy, dz in FAR3:
            for step in ((2, 1), (3, 0))[half_no]:
                cols = pl.ds(pl.multiple_of(lax.rem(hx + dx + step, 4) * 512, 512), 512)
                rcopy(
                    q_hbm.at[c, :, cols], qbuf.at[b, :, cols], q_send.at[0], q_recv.at[half_no],
                    (pair_dev(dx, dy, dz), s),
                ).start()

    q_start(0)
    q_start(1)
    w_to = [
        (wt_hbm, wt.at[s, :, half, :], w_recv.at[s]),
        (wo_hbm, wob.at[s, half, :], w_recv.at[4 + s]),
    ]
    w_away = [rcopy(src, dst, w_send.at[i], rs, (other, 1)) for i, (src, dst, rs) in enumerate(w_to)]
    w_same = [rcopy(src, dst, w_send.at[2 + i], rs, (b, 1)) for i, (src, dst, rs) in enumerate(w_to)]
    gx = rcopy(gain_hbm, gains.at[s], g_sem.at[0], g_sem.at[1], (b, 1))

    @pl.when(s == 1)
    def _():
        for src, dst, rs in w_to:
            pltpu.make_async_copy(src, dst, rs).start()
        pltpu.make_async_copy(gain_hbm, gains.at[s], g_sem.at[1]).start()

    @pl.when(s != 1)
    def _():
        gx.start()

    @pl.when(c == 0)
    def _():
        w_away[0].start()

    @pl.when(s != 1)
    def _():
        w_away[1].start()

    @pl.when(s == 0)
    def _():
        for cp in w_same:
            cp.start()

    loc[1].wait()
    for j in range(HEADS):
        vts[j] = vb[0, :, j * HD : (j + 1) * HD].T
    loc[0].wait()
    kx.wait_recv()
    for cp in loc[2:]:
        cp.wait()
    bytes_of(qbuf.at[0:31, :, 0:1024], q_recv.at[0])

    def e_copy(m, t):
        p = lax.rem(h + t, HEADS)
        dst = p * 2 + 1 - m
        cols = pl.ds(pl.multiple_of(p * HD, HD), HD)
        return (
            e_hbm.at[m, :, cols],
            ebuf.at[b],
            dst,
        )

    @pl.when(s == 1)
    def _():
        for m in range(2):
            def e_start(t, _):
                src, dst_ref, dst = e_copy(m, t)
                rcopy(src, dst_ref, e_sem.at[0], e_sem.at[1], (dst, s)).start()
                return 0
            lax.fori_loop(1, HEADS, e_start, 0)
            src, dst_ref, dst = e_copy(m, 0)

            @pl.when(zl == 1 - m)
            def _():
                pltpu.make_async_copy(src, dst_ref, e_sem.at[1]).start()

            @pl.when(zl == m)
            def _():
                rcopy(src, dst_ref, e_sem.at[0], e_sem.at[1], (dst, s)).start()

    base0 = (b * 4 + s) * ROWS
    base1 = (b * 4 + s + 1 - 2 * c) * ROWS
    pos = pos_ref[pl.ds(c, 1), :]
    ids = lax.broadcasted_iota(jnp.int32, (ROWS, LAT), 0)
    scale = HD ** (-0.5)

    ids1 = ids + base1
    ids0 = ids + base0

    def scores(hh):
        cols = pl.ds(pl.multiple_of(hh * HD, HD), HD)
        qh = qbuf[:, :, cols].astype(f32).reshape(LAT, HD).astype(bf16)
        s0 = jnp.where(ids0 < pos, dot(kb[0, :, cols], qh, NT) * scale, masked)
        s1 = jnp.where(ids1 < pos, dot(kb[1, :, cols], qh, NT) * scale, masked)
        return s0, s1

    def weigh(s0, s1):
        top = jnp.maximum(jnp.max(jnp.maximum(s0, s1), axis=0, keepdims=True), 0.1 * masked)
        e0, e1 = jnp.exp(s0 - top), jnp.exp(s1 - top)
        total = jnp.sum(e0 + e1, axis=0, keepdims=True)
        return top, total, e0.astype(bf16), e1.astype(bf16)

    order = [chip(*o) for o in HALVES[0] + HALVES[1]]
    for g in range(0, HEADS, 4):
        if g == HEADS // 2:
            bytes_of(qbuf.at[0:31, :, 0:1024], q_recv.at[1])
        group = order[g : g + 4]
        ss = [scores(hh) for hh in group]
        ws = [weigh(*v) for v in ss]
        if g == 0:
            vx.wait_recv()
        for hh, (top, total, e0, e1) in zip(group, ws):
            cols = pl.ds(pl.multiple_of(hh * HD, HD), HD)
            ob[hh] = (dot(vts[hh], e0, NN) + dot(vb[1, :, cols].T, e1, NN)).astype(bf16)
            obs[hh, 0:1, :] = top
            obs[hh, 1:2, :] = total
        for i in range(g, g + 4):
            if i < HEADS - 1:
                hh = order[i]
                rcopy(obs.at[hh], r1s.at[h], r1_sem.at[2], r1_sem.at[3], (hh * 2 + zl, s)).start()
                rcopy(ob.at[hh], r1.at[h], r1_sem.at[0], r1_sem.at[1], (hh * 2 + zl, s)).start()

    bytes_of(r1.at[0:15], r1_sem.at[1])
    bytes_of(r1s.at[0:15], r1_sem.at[3])
    r1[h] = ob[h]
    r1s[h] = obs[h]

    def combine(buf, stats, n):
        top = stats[0, 0:1, :]
        for i in range(1, n):
            top = jnp.maximum(top, stats[i, 0:1, :])
        total = jnp.zeros((1, LAT), f32)
        acc = jnp.zeros((HD, LAT), f32)
        for i in range(n):
            w = jnp.exp(stats[i, 0:1, :] - top)
            total = total + w * stats[i, 1:2, :]
            acc = acc + w * buf[i].astype(f32)
        return acc, top, total

    acc, top, total = combine(r1, r1s, HEADS)
    r2o[...] = acc.astype(bf16)
    r2os[0:1, :] = top
    r2os[1:2, :] = total
    z = zh * 2 + zl
    r2_home = (s == 1) & (zl == 1 - c)
    r2_dst = (2 * h + 1 - c, 1)
    r2_copies = [
        rcopy(r2os, r2s.at[z], r2_sem.at[2], r2_sem.at[3], r2_dst),
        rcopy(r2o, r2.at[z], r2_sem.at[0], r2_sem.at[1], r2_dst),
    ]

    @pl.when(r2_home)
    def _():
        pltpu.make_async_copy(r2os, r2s.at[z], r2_sem.at[3]).start()
        pltpu.make_async_copy(r2o, r2.at[z], r2_sem.at[1]).start()

    @pl.when(jnp.logical_not(r2_home))
    def _():
        for cp in r2_copies:
            cp.start()

    @pl.when(s == 2)
    def _():
        pl.semaphore_wait(go_sem.at[0], 2)
        for cp in w_same:
            cp.start()

    @pl.when(s == 3)
    def _():
        pl.semaphore_wait(go_sem.at[0], 2)
        w_away[0].start()
        pl.semaphore_wait(go_sem.at[1], 2)
        for cp in w_same:
            cp.start()

    my_cols = pl.ds(pl.multiple_of(h * HD, HD), HD)

    def column(k):
        return jnp.broadcast_to(gains[k, :, my_cols], (HD, LAT)).T

    seg = h // 4
    jj = lax.broadcasted_iota(jnp.int32, (LAT, LAT), 0)
    ii = lax.broadcasted_iota(jnp.int32, (LAT, LAT), 1)

    halves = (slice(0, 64), slice(64, HD))

    def pack_x(k, i, x, gain, before):
        xs[k, 64 * i : 64 * i + 64, :] = (x * gain[64 * i : 64 * i + 64]).astype(bf16)
        ss = before + jnp.sum(x * x, axis=0, keepdims=True)
        if i:
            xss[k] = ss
        return ss

    def gather(k, i):
        rows = halves[i]
        if i:
            for p in far:
                rcopy(xss.at[k], xbs.at[k, h], x_send.at[1], x_recv.at[k, 2], (p * 2 + zl, s)).start()
            pltpu.make_async_copy(xss.at[k], xbs.at[k, h], x_recv.at[k, 2]).start()
        for n, p in enumerate(far):
            late = int(FAR[n] in NEARS[NEAR - 1 :])
            rcopy(
                xs.at[k, rows], xb.at[k, h, rows], x_send.at[0], x_recv.at[k, late], (p * 2 + zl, s)
            ).start()
        pltpu.make_async_copy(xs.at[k, rows], xb.at[k, h, rows], x_recv.at[k, 0]).start()

    def attend(k):
        bytes_of(wt.at[k], w_recv.at[k])
        if k == 3:
            fb[...] = xf[k].T.reshape(NB, 4, HD)
            sem = f_recv.at[0]
            dst = fx.at[1 - zl, lax.rem(h, 4)]
            for p in far:
                for dz in range(2):
                    rcopy(fb.at[2 * p + dz], dst, f_send.at[0], sem, (2 * p + dz, seg)).start()
            rcopy(fb.at[other], dst, f_send.at[0], sem, (other, seg)).start()

            @pl.when(seg != s)
            def _():
                rcopy(fb.at[b], dst, f_send.at[0], sem, (b, seg)).start()

            @pl.when(seg == s)
            def _():
                pltpu.make_async_copy(fb.at[b], dst, sem).start()

        qkv = jnp.zeros((3 * HD, LAT), f32)
        for j in range(0, HEADS, 2):
            pair = near[j : j + 2]
            if j == 0:
                bytes_of(xb.at[k, 0:NEAR], x_recv.at[k, 0])
            if j == NEAR:
                bytes_of(wob.at[k], w_recv.at[4 + k])
                for i in range(HEADS if k < 3 else 0):
                    wot[k, i] = wob[k, :, i * HD : (i + 1) * HD].T
                bytes_of(xb.at[k, 0 : HEADS - NEAR], x_recv.at[k, 1])
            w2 = [wt[k, :, :, pl.ds(pl.multiple_of(p * HD, HD), HD)].reshape(3 * HD, HD) for p in pair]
            x2 = [xb[k, p] for p in pair]
            qkv = qkv + dot(jnp.concatenate(w2, axis=1), jnp.concatenate(x2, axis=0), NN)
        bytes_of(xbs.at[k], x_recv.at[k, 2])
        factor = lax.rsqrt(jnp.sum(xbs[k], axis=0) * (1.0 / D) + epsilon)
        qkv = (qkv * factor).astype(bf16)
        qt, kt, vt = qkv[0:HD], qkv[HD : 2 * HD], qkv[2 * HD :]
        sc = dot(kt, qt, TN) * scale
        sc = jnp.where(jj <= ii, sc, masked)
        e = jnp.exp(sc - jnp.max(sc, axis=0, keepdims=True))
        soft = (e / jnp.sum(e, axis=0, keepdims=True)).astype(bf16)
        return dot(vt, soft, NN).astype(bf16)

    def exchange(k, att):
        for i in range(2):
            rows = slice(64 * i, 64 * i + 64)
            for group in (far[0:5], far[5:15]) if i == 0 else (far,):
                us = [dot(wot[k, p, rows, :], att, NN).astype(bf16) for p in group]
                for p, u in zip(group, us):
                    ub[k, p, rows, :] = u
                for p in group:
                    rcopy(
                        ub.at[k, p, rows], rb.at[k, h, rows], u_send.at[0], u_recv.at[k, i], (p * 2 + zl, s)
                    ).start()
        own = dot(wot[k, h], att, NN)
        ss = jnp.zeros((1, LAT), f32)
        for i in range(2):
            rows = slice(64 * i, 64 * i + 64)
            x = xf[k, rows, :] + own[rows]
            bytes_of(rb.at[k, 0:15, rows], u_recv.at[k, i])
            for p in near[1:]:
                x = x + rb[k, p, rows, :].astype(f32)
            xf[k + 1, rows, :] = x
            ss = pack_x(k + 1, i, x, column(k + 1), ss)
            gather(k + 1, i)

    @pl.when(s == 1)
    def _():
        bytes_of(gains, g_sem.at[1])
        bytes_of(ebuf, e_sem.at[1])
        emb = ebuf[...].astype(f32).reshape(LAT, HD).T
        bytes_of(r2, r2_sem.at[1])
        bytes_of(r2s, r2_sem.at[3])
        acc, top, total = combine(r2, r2s, 4)
        x0 = emb + acc / total
        xf[0] = x0
        ss = jnp.zeros((1, LAT), f32)
        for i in range(2):
            ss = pack_x(0, i, x0[64 * i : 64 * i + 64], column(0), ss)
            gather(0, i)

        def signal(dev, n=0):
            pl.semaphore_signal(go_sem.at[n], inc=1, device_id=dev, device_id_type=MESH)

        signal((other, 1))
        for n in (2, 3):
            signal((b, n))
            signal((other, n))
        pl.semaphore_wait(go_sem.at[0], 1)
        for cp in w_away:
            cp.start()
        exchange(0, attend(0))
        signal((b, 3), 1)
        signal((other, 3), 1)
        for k in range(1, 3):
            exchange(k, attend(k))
        att = attend(3)
        att_r = att.T
        sem = f_recv.at[1]
        dst = fu.at[1 - zl, h]
        for n in range(4):
            u = dot(att_r, wob[3, :, n * 512 : (n + 1) * 512], NN)
            uf[n * NB : (n + 1) * NB] = u.reshape(NB, 4, 512).astype(bf16)
        for p in far:
            for dz in range(2):
                for n in range(4):
                    i = 2 * p + dz
                    rcopy(uf.at[n * NB + i], dst, f_send.at[1], sem, (i, n)).start()
        for n in range(4):
            rcopy(uf.at[n * NB + other], dst, f_send.at[1], sem, (other, n)).start()
        for n in (0, 2, 3):
            rcopy(uf.at[n * NB + b], dst, f_send.at[1], sem, (b, n)).start()
        pltpu.make_async_copy(uf.at[NB + b], dst, sem).start()
        bytes_of(uf.at[0:127], f_send.at[1])

        @pl.when(seg == s)
        def _():
            bytes_of(fb.at[0:31], f_send.at[0])

        @pl.when(seg != s)
        def _():
            bytes_of(fb, f_send.at[0])

        bytes_of(ub.at[:, 0:15], u_send.at[0])
        bytes_of(xb.at[:, 0:15], x_send.at[0])
        bytes_of(xbs.at[:, 0:15], x_send.at[1])

    bytes_of(qbuf.at[0:31], q_send.at[0])
    bytes_of(ob.at[0:15], r1_sem.at[0])
    bytes_of(obs.at[0:15], r1_sem.at[2])
    for cp in [kx, vx] + w_away:
        cp.wait_send()

    @pl.when(s != 1)
    def _():
        for cp in [gx] + w_same:
            cp.wait_send()

    @pl.when(jnp.logical_not(r2_home))
    def _():
        for cp in r2_copies:
            cp.wait_send()

    @pl.when(s == 1)
    def _():
        bytes_of(ebuf.at[0:31], e_sem.at[0])

    bytes_of(fx, f_recv.at[0])
    bytes_of(fu, f_recv.at[1])
    for m in range(2):
        acc = jnp.concatenate([fx[m, i] for i in range(4)], axis=1)
        for i in range(HEADS):
            acc = acc + fu[m, i].astype(f32)
        out_ref[m] = acc


def on_device(
    latent_queries, latent_embed, history_keys, history_values, latent_pos, norm_gain, w_qkv, w_out
):
    wt = jnp.transpose(w_qkv[0], (1, 2, 0))
    hbm = pl.BlockSpec(memory_space=pl.ANY)
    vmem = pl.BlockSpec(memory_space=pltpu.VMEM)
    dma = pltpu.SemaphoreType.DMA
    return pl.pallas_call(
        kernel,
        out_shape=jax.ShapeDtypeStruct((2, 4, 512), f32),
        in_specs=[hbm] * 8,
        out_specs=vmem,
        scratch_shapes=[
            pltpu.VMEM((2, LAT), jnp.int32),
            pltpu.VMEM((4, 1, D), f32),
            pltpu.VMEM((NB, 4, D), bf16),
            pltpu.VMEM((2, ROWS, D), bf16),
            pltpu.VMEM((2, ROWS, D), bf16),
            pltpu.VMEM((HEADS, HD, ROWS), bf16),
            pltpu.VMEM((4, 3, HD, D), bf16),
            pltpu.VMEM((4, HD, D), bf16),
            pltpu.VMEM((3, HEADS, HD, HD), bf16),
            pltpu.VMEM((HEADS, HD, LAT), bf16),
            pltpu.VMEM((HEADS, 2, LAT), f32),
            pltpu.VMEM((HEADS, HD, LAT), bf16),
            pltpu.VMEM((HEADS, 2, LAT), f32),
            pltpu.VMEM((HD, LAT), bf16),
            pltpu.VMEM((2, LAT), f32),
            pltpu.VMEM((4, HD, LAT), bf16),
            pltpu.VMEM((4, 2, LAT), f32),
            pltpu.VMEM((NB, 4, HD), bf16),
            pltpu.VMEM((4, HD, LAT), bf16),
            pltpu.VMEM((4, 1, LAT), f32),
            pltpu.VMEM((4, HEADS, HD, LAT), bf16),
            pltpu.VMEM((4, HEADS, 1, LAT), f32),
            pltpu.VMEM((4, HD, LAT), f32),
            pltpu.VMEM((3, HEADS, HD, LAT), bf16),
            pltpu.VMEM((3, HEADS, HD, LAT), bf16),
            pltpu.VMEM((NB, 4, HD), f32),
            pltpu.VMEM((2, 4, 4, HD), f32),
            pltpu.VMEM((4 * NB, 4, 512), bf16),
            pltpu.VMEM((2, HEADS, 4, 512), bf16),
            dma((4,)), dma((2,)), dma((2,)), dma((4,)), dma((8,)), dma((2,)), dma((1,)), dma((2,)),
            dma((4,)), dma((4,)), dma((2,)), dma((2,)), dma((4, 3)), dma((1,)), dma((3, 2)), dma((2,)), dma((2,)),
            pltpu.SemaphoreType.REGULAR((2,)),
        ],
        compiler_params=pltpu.CompilerParams(
            collective_id=0, has_side_effects=True, vmem_limit_bytes=67043328
        ),
        name="ar_step",
    )(latent_queries, latent_embed, history_keys, history_values, latent_pos, norm_gain, wt, w_out[0])


def solution(mesh):
    return jax.shard_map(
        on_device,
        mesh=mesh,
        in_specs=(
            P(None, "blk", None),
            P(None, "blk", None),
            P(None, ("blk", "segment"), None),
            P(None, ("blk", "segment"), None),
            P(),
            P("segment", None),
            P("segment", None, None, "blk"),
            P("segment", "blk", None),
        ),
        out_specs=P(None, "blk", "segment"),
        check_vma=False,
    )
```

```python
import jax
import jax.numpy as jnp
from jax import lax
from jax.experimental import pallas as pl
from jax.experimental.pallas import tpu as pltpu
from jax.sharding import PartitionSpec as P

HEADS = 16
HD = 128
LAT = 128
D = 2048
ROWS = 256
NB = 32
epsilon = 1e-06
masked = -1e30
MESH = pl.DeviceIdType.MESH
f32, bf16 = jnp.float32, jnp.bfloat16
NN = (((1,), (0,)), ((), ()))
NT = (((1,), (1,)), ((), ()))
TN = (((0,), (0,)), ((), ()))


def hops(o):
    return sum(min(v, 4 - v) for v in o)


FAR = [divmod(o, 10) for o in (22, 12, 32, 21, 23, 11, 13, 31, 33, 2, 20, 1, 3, 10, 30)]
FAR3 = sorted(
    ((dx, dy, dz) for dx in range(4) for dy in range(4) for dz in range(2) if dx or dy or dz),
    key=lambda o: -hops(o),
)
HALVES = [
    sorted(((dx, dy) for dx in steps for dy in range(4)), key=lambda o: -hops(o)) for steps in ((2, 1), (3, 0))
]
NEARS = [divmod(o, 10) for o in (1, 3, 10, 30, 2, 11, 13, 31, 33, 20, 12, 32, 21, 23, 22)]
NEAR = 10
PIECES = 4
PR = HD // PIECES


def dot(a, b, dims):
    return lax.dot_general(a, b, dims, preferred_element_type=f32)


def kernel(
    q_hbm, e_hbm, k_hbm, v_hbm, pos_hbm, gain_hbm, wt_hbm, wo_hbm, out_ref,
    pos_ref, gains, qbuf, kb, vb, vts, wt, wob, wot, ob, obs, r1, r1s, r2o, r2os, r2, r2s, ebuf, xs, xss, xb, xbs, xf, ub, rb, fb, fx, uf, fu,
    loc_sem, kv_send, kv_recv, w_send, w_recv, g_sem, q_send, q_recv,
    r1_sem, r2_sem, e_sem, x_send, x_recv, u_send, u_recv, f_send, f_recv, go_sem,
):
    b = lax.axis_index("blk")
    s = lax.axis_index("segment")
    h = b // 2
    zl = b % 2
    zh = s // 2
    c = s % 2
    sib = (b, s + 1 - 2 * c)
    zpart = (b + 1 - 2 * zl, s)

    def rcopy(src, dst, ss, rs, dev):
        return pltpu.make_async_remote_copy(
            src_ref=src, dst_ref=dst, send_sem=ss, recv_sem=rs, device_id=dev, device_id_type=MESH
        )

    def bytes_of(ref, sem):
        pltpu.make_async_copy(ref, ref, sem).wait()

    hx, hy = h // 4, lax.rem(h, 4)

    def chip(dx, dy):
        return lax.rem(hx + dx, 4) * 4 + lax.rem(hy + dy, 4)

    far = [chip(*o) for o in FAR]
    near = [h] + [chip(*o) for o in NEARS]

    half = pl.ds(pl.multiple_of(64 * zl, 64), 64)
    loc = [
        pltpu.make_async_copy(k_hbm.at[c], kb.at[0], loc_sem.at[0]),
        pltpu.make_async_copy(v_hbm.at[c], vb.at[0], loc_sem.at[1]),
        pltpu.make_async_copy(q_hbm.at[c], qbuf.at[b], loc_sem.at[2]),
        pltpu.make_async_copy(pos_hbm, pos_ref, loc_sem.at[3]),
    ]
    barrier = pltpu.get_barrier_semaphore()
    other = b + 1 - 2 * zl

    def pair_dev(dx, dy, dz):
        return chip(dx, dy) * 2 + (1 - zl if dz else zl)

    for o in FAR3:
        pl.semaphore_signal(barrier, inc=1, device_id=(pair_dev(*o), s), device_id_type=MESH)
    for blk in (b, other):
        for ds in range(1, 4):
            pl.semaphore_signal(barrier, inc=1, device_id=(blk, (s + ds) % 4), device_id_type=MESH)
    for cp in (loc[2], loc[1], loc[0], loc[3]):
        cp.start()

    pl.semaphore_wait(barrier, 37)

    kx = rcopy(k_hbm.at[1 - c], kb.at[1], kv_send.at[0], kv_recv.at[0], sib)
    vx = rcopy(v_hbm.at[1 - c], vb.at[1], kv_send.at[1], kv_recv.at[1], sib)
    kx.start()
    vx.start()

    def q_start(half_no):
        for dx, dy, dz in FAR3:
            for step in ((2, 1), (3, 0))[half_no]:
                cols = pl.ds(pl.multiple_of(lax.rem(hx + dx + step, 4) * 512, 512), 512)
                rcopy(
                    q_hbm.at[c, :, cols], qbuf.at[b, :, cols], q_send.at[0], q_recv.at[half_no],
                    (pair_dev(dx, dy, dz), s),
                ).start()

    q_start(0)
    q_start(1)
    w_to = [
        (wt_hbm, wt.at[s, :, half, :], w_recv.at[s]),
        (wo_hbm, wob.at[s, half, :], w_recv.at[4 + s]),
    ]
    w_away = [rcopy(src, dst, w_send.at[i], rs, (other, 1)) for i, (src, dst, rs) in enumerate(w_to)]
    w_same = [rcopy(src, dst, w_send.at[2 + i], rs, (b, 1)) for i, (src, dst, rs) in enumerate(w_to)]
    gx = rcopy(gain_hbm, gains.at[s], g_sem.at[0], g_sem.at[1], (b, 1))

    @pl.when(s == 1)
    def _():
        for src, dst, rs in w_to:
            pltpu.make_async_copy(src, dst, rs).start()
        pltpu.make_async_copy(gain_hbm, gains.at[s], g_sem.at[1]).start()

    @pl.when(s != 1)
    def _():
        gx.start()

    @pl.when(c == 0)
    def _():
        w_away[0].start()

    @pl.when(s != 1)
    def _():
        w_away[1].start()

    @pl.when(s == 0)
    def _():
        for cp in w_same:
            cp.start()

    loc[1].wait()
    for j in range(HEADS):
        vts[j] = vb[0, :, j * HD : (j + 1) * HD].T
    loc[0].wait()
    kx.wait_recv()
    for cp in loc[2:]:
        cp.wait()
    bytes_of(qbuf.at[0:31, :, 0:1024], q_recv.at[0])

    def e_copy(m, t):
        p = lax.rem(h + t, HEADS)
        dst = p * 2 + 1 - m
        cols = pl.ds(pl.multiple_of(p * HD, HD), HD)
        return (
            e_hbm.at[m, :, cols],
            ebuf.at[b],
            dst,
        )

    @pl.when(s == 1)
    def _():
        for m in range(2):
            def e_start(t, _):
                src, dst_ref, dst = e_copy(m, t)
                rcopy(src, dst_ref, e_sem.at[0], e_sem.at[1], (dst, s)).start()
                return 0
            lax.fori_loop(1, HEADS, e_start, 0)
            src, dst_ref, dst = e_copy(m, 0)

            @pl.when(zl == 1 - m)
            def _():
                pltpu.make_async_copy(src, dst_ref, e_sem.at[1]).start()

            @pl.when(zl == m)
            def _():
                rcopy(src, dst_ref, e_sem.at[0], e_sem.at[1], (dst, s)).start()

    base0 = (b * 4 + s) * ROWS
    base1 = (b * 4 + s + 1 - 2 * c) * ROWS
    pos = pos_ref[pl.ds(c, 1), :]
    ids = lax.broadcasted_iota(jnp.int32, (ROWS, LAT), 0)
    scale = HD ** (-0.5)

    ids1 = ids + base1
    ids0 = ids + base0

    def scores(hh):
        cols = pl.ds(pl.multiple_of(hh * HD, HD), HD)
        qh = qbuf[:, :, cols].astype(f32).reshape(LAT, HD).astype(bf16)
        s0 = jnp.where(ids0 < pos, dot(kb[0, :, cols], qh, NT) * scale, masked)
        s1 = jnp.where(ids1 < pos, dot(kb[1, :, cols], qh, NT) * scale, masked)
        return s0, s1

    def weigh(s0, s1):
        top = jnp.maximum(jnp.max(jnp.maximum(s0, s1), axis=0, keepdims=True), 0.1 * masked)
        e0, e1 = jnp.exp(s0 - top), jnp.exp(s1 - top)
        total = jnp.sum(e0 + e1, axis=0, keepdims=True)
        return top, total, e0.astype(bf16), e1.astype(bf16)

    order = [chip(*o) for o in HALVES[0] + HALVES[1]]
    for g in range(0, HEADS, 4):
        if g == HEADS // 2:
            bytes_of(qbuf.at[0:31, :, 0:1024], q_recv.at[1])
        group = order[g : g + 4]
        ss = [scores(hh) for hh in group]
        ws = [weigh(*v) for v in ss]
        if g == 0:
            vx.wait_recv()
        for hh, (top, total, e0, e1) in zip(group, ws):
            cols = pl.ds(pl.multiple_of(hh * HD, HD), HD)
            ob[hh] = (dot(vts[hh], e0, NN) + dot(vb[1, :, cols].T, e1, NN)).astype(bf16)
            obs[hh, 0:1, :] = top
            obs[hh, 1:2, :] = total
        for i in range(g, g + 4):
            if i < HEADS - 1:
                hh = order[i]
                rcopy(obs.at[hh], r1s.at[h], r1_sem.at[2], r1_sem.at[3], (hh * 2 + zl, s)).start()
                rcopy(ob.at[hh], r1.at[h], r1_sem.at[0], r1_sem.at[1], (hh * 2 + zl, s)).start()

    bytes_of(r1.at[0:15], r1_sem.at[1])
    bytes_of(r1s.at[0:15], r1_sem.at[3])
    r1[h] = ob[h]
    r1s[h] = obs[h]

    def combine(buf, stats, n):
        top = stats[0, 0:1, :]
        for i in range(1, n):
            top = jnp.maximum(top, stats[i, 0:1, :])
        total = jnp.zeros((1, LAT), f32)
        acc = jnp.zeros((HD, LAT), f32)
        for i in range(n):
            w = jnp.exp(stats[i, 0:1, :] - top)
            total = total + w * stats[i, 1:2, :]
            acc = acc + w * buf[i].astype(f32)
        return acc, top, total

    acc, top, total = combine(r1, r1s, HEADS)
    r2o[...] = acc.astype(bf16)
    r2os[0:1, :] = top
    r2os[1:2, :] = total
    z = zh * 2 + zl
    r2_home = (s == 1) & (zl == 1 - c)
    r2_dst = (2 * h + 1 - c, 1)
    r2_copies = [
        rcopy(r2os, r2s.at[z], r2_sem.at[2], r2_sem.at[3], r2_dst),
        rcopy(r2o, r2.at[z], r2_sem.at[0], r2_sem.at[1], r2_dst),
    ]

    @pl.when(r2_home)
    def _():
        pltpu.make_async_copy(r2os, r2s.at[z], r2_sem.at[3]).start()
        pltpu.make_async_copy(r2o, r2.at[z], r2_sem.at[1]).start()

    @pl.when(jnp.logical_not(r2_home))
    def _():
        for cp in r2_copies:
            cp.start()

    @pl.when(s == 2)
    def _():
        pl.semaphore_wait(go_sem.at[0], 2)
        for cp in w_same:
            cp.start()

    @pl.when(s == 3)
    def _():
        pl.semaphore_wait(go_sem.at[0], 2)
        w_away[0].start()
        pl.semaphore_wait(go_sem.at[1], 2)
        for cp in w_same:
            cp.start()

    my_cols = pl.ds(pl.multiple_of(h * HD, HD), HD)

    def column(k):
        return jnp.broadcast_to(gains[k, :, my_cols], (HD, LAT)).T

    seg = h // 4
    jj = lax.broadcasted_iota(jnp.int32, (LAT, LAT), 0)
    ii = lax.broadcasted_iota(jnp.int32, (LAT, LAT), 1)

    pieces = [slice(PR * i, PR * i + PR) for i in range(PIECES)]

    def pack_x(k, i, x, gain, before):
        xs[k, pieces[i], :] = (x * gain[pieces[i]]).astype(bf16)
        ss = before + jnp.sum(x * x, axis=0, keepdims=True)
        if i == PIECES - 1:
            xss[k] = ss
        return ss

    def gather(k, i):
        rows = pieces[i]
        if i == PIECES - 1:
            for p in far:
                rcopy(xss.at[k], xbs.at[k, h], x_send.at[1], x_recv.at[k, 2], (p * 2 + zl, s)).start()
            pltpu.make_async_copy(xss.at[k], xbs.at[k, h], x_recv.at[k, 2]).start()
        for n, p in enumerate(far):
            late = int(FAR[n] in NEARS[NEAR - 1 :])
            rcopy(
                xs.at[k, rows], xb.at[k, h, rows], x_send.at[0], x_recv.at[k, late], (p * 2 + zl, s)
            ).start()
        pltpu.make_async_copy(xs.at[k, rows], xb.at[k, h, rows], x_recv.at[k, 0]).start()

    def attend(k):
        bytes_of(wt.at[k], w_recv.at[k])
        if k == 3:
            fb[...] = xf[k].T.reshape(NB, 4, HD)
            sem = f_recv.at[0]
            dst = fx.at[1 - zl, lax.rem(h, 4)]
            for p in far:
                for dz in range(2):
                    rcopy(fb.at[2 * p + dz], dst, f_send.at[0], sem, (2 * p + dz, seg)).start()
            rcopy(fb.at[other], dst, f_send.at[0], sem, (other, seg)).start()

            @pl.when(seg != s)
            def _():
                rcopy(fb.at[b], dst, f_send.at[0], sem, (b, seg)).start()

            @pl.when(seg == s)
            def _():
                pltpu.make_async_copy(fb.at[b], dst, sem).start()

        qkv = jnp.zeros((3 * HD, LAT), f32)
        for j in range(0, HEADS, 2):
            pair = near[j : j + 2]
            if j == 0:
                bytes_of(xb.at[k, 0:NEAR], x_recv.at[k, 0])
            if j == NEAR:
                bytes_of(wob.at[k], w_recv.at[4 + k])
                for i in range(HEADS if k < 3 else 0):
                    turned = wob[k, :, i * HD : (i + 1) * HD].T
                    for n, rows in enumerate(pieces):
                        wot[k, n, i] = turned[rows]
                bytes_of(xb.at[k, 0 : HEADS - NEAR], x_recv.at[k, 1])
            w2 = [wt[k, :, :, pl.ds(pl.multiple_of(p * HD, HD), HD)].reshape(3 * HD, HD) for p in pair]
            x2 = [xb[k, p] for p in pair]
            qkv = qkv + dot(jnp.concatenate(w2, axis=1), jnp.concatenate(x2, axis=0), NN)
        bytes_of(xbs.at[k], x_recv.at[k, 2])
        factor = lax.rsqrt(jnp.sum(xbs[k], axis=0) * (1.0 / D) + epsilon)
        qkv = (qkv * factor).astype(bf16)
        qt, kt, vt = qkv[0:HD], qkv[HD : 2 * HD], qkv[2 * HD :]
        sc = dot(kt, qt, TN) * scale
        sc = jnp.where(jj <= ii, sc, masked)
        e = jnp.exp(sc - jnp.max(sc, axis=0, keepdims=True))
        soft = (e / jnp.sum(e, axis=0, keepdims=True)).astype(bf16)
        return dot(vt, soft, NN).astype(bf16)

    def exchange(k, att):
        for i, rows in enumerate(pieces):
            u = dot(wot[k, i].reshape(HEADS * PR, HD), att, NN).astype(bf16)
            ub[k, i] = u.reshape(HEADS, PR, LAT)
            for p in far:
                rcopy(
                    ub.at[k, i, p], rb.at[k, h, rows], u_send.at[0], u_recv.at[k, i], (p * 2 + zl, s)
                ).start()
        ss = jnp.zeros((1, LAT), f32)
        for i, rows in enumerate(pieces):
            x = xf[k, rows, :] + ub[k, i, h].astype(f32)
            bytes_of(rb.at[k, 0:15, rows], u_recv.at[k, i])
            for p in near[1:]:
                x = x + rb[k, p, rows, :].astype(f32)
            xf[k + 1, rows, :] = x
            ss = pack_x(k + 1, i, x, column(k + 1), ss)
            gather(k + 1, i)

    @pl.when(s == 1)
    def _():
        bytes_of(gains, g_sem.at[1])
        bytes_of(ebuf, e_sem.at[1])
        emb = ebuf[...].astype(f32).reshape(LAT, HD).T
        bytes_of(r2, r2_sem.at[1])
        bytes_of(r2s, r2_sem.at[3])
        acc, top, total = combine(r2, r2s, 4)
        x0 = emb + acc / total
        xf[0] = x0
        ss = jnp.zeros((1, LAT), f32)
        for i, rows in enumerate(pieces):
            ss = pack_x(0, i, x0[rows], column(0), ss)
            gather(0, i)

        def signal(dev, n=0):
            pl.semaphore_signal(go_sem.at[n], inc=1, device_id=dev, device_id_type=MESH)

        signal((other, 1))
        for n in (2, 3):
            signal((b, n))
            signal((other, n))
        pl.semaphore_wait(go_sem.at[0], 1)
        for cp in w_away:
            cp.start()
        exchange(0, attend(0))
        signal((b, 3), 1)
        signal((other, 3), 1)
        for k in range(1, 3):
            exchange(k, attend(k))
        att = attend(3)
        att_r = att.T
        sem = f_recv.at[1]
        dst = fu.at[1 - zl, h]
        def hand_out(chips, n):
            for p in chips:
                for dz in range(2):
                    i = 2 * p + dz
                    rcopy(uf.at[n * NB + i], dst, f_send.at[1], sem, (i, n)).start()

        for n in range(4):
            u = dot(att_r, wob[3, :, n * 512 : (n + 1) * 512], NN)
            uf[n * NB : (n + 1) * NB] = u.reshape(NB, 4, 512).astype(bf16)
            hand_out(far[:5], n)
        for n in range(4):
            hand_out(far[5:], n)
        for n in range(4):
            rcopy(uf.at[n * NB + other], dst, f_send.at[1], sem, (other, n)).start()
        for n in (0, 2, 3):
            rcopy(uf.at[n * NB + b], dst, f_send.at[1], sem, (b, n)).start()
        pltpu.make_async_copy(uf.at[NB + b], dst, sem).start()
        bytes_of(uf.at[0:127], f_send.at[1])

        @pl.when(seg == s)
        def _():
            bytes_of(fb.at[0:31], f_send.at[0])

        @pl.when(seg != s)
        def _():
            bytes_of(fb, f_send.at[0])

        bytes_of(ub.at[:, :, 0:15], u_send.at[0])
        bytes_of(xb.at[:, 0:15], x_send.at[0])
        bytes_of(xbs.at[:, 0:15], x_send.at[1])

    bytes_of(qbuf.at[0:31], q_send.at[0])
    bytes_of(ob.at[0:15], r1_sem.at[0])
    bytes_of(obs.at[0:15], r1_sem.at[2])
    for cp in [kx, vx] + w_away:
        cp.wait_send()

    @pl.when(s != 1)
    def _():
        for cp in [gx] + w_same:
            cp.wait_send()

    @pl.when(jnp.logical_not(r2_home))
    def _():
        for cp in r2_copies:
            cp.wait_send()

    @pl.when(s == 1)
    def _():
        bytes_of(ebuf.at[0:31], e_sem.at[0])

    bytes_of(fx, f_recv.at[0])
    bytes_of(fu, f_recv.at[1])
    for m in range(2):
        acc = jnp.concatenate([fx[m, i] for i in range(4)], axis=1)
        for i in range(HEADS):
            acc = acc + fu[m, i].astype(f32)
        out_ref[m] = acc


def on_device(
    latent_queries, latent_embed, history_keys, history_values, latent_pos, norm_gain, w_qkv, w_out
):
    wt = jnp.transpose(w_qkv[0], (1, 2, 0))
    hbm = pl.BlockSpec(memory_space=pl.ANY)
    vmem = pl.BlockSpec(memory_space=pltpu.VMEM)
    dma = pltpu.SemaphoreType.DMA
    return pl.pallas_call(
        kernel,
        out_shape=jax.ShapeDtypeStruct((2, 4, 512), f32),
        in_specs=[hbm] * 8,
        out_specs=vmem,
        scratch_shapes=[
            pltpu.VMEM((2, LAT), jnp.int32),
            pltpu.VMEM((4, 1, D), f32),
            pltpu.VMEM((NB, 4, D), bf16),
            pltpu.VMEM((2, ROWS, D), bf16),
            pltpu.VMEM((2, ROWS, D), bf16),
            pltpu.VMEM((HEADS, HD, ROWS), bf16),
            pltpu.VMEM((4, 3, HD, D), bf16),
            pltpu.VMEM((4, HD, D), bf16),
            pltpu.VMEM((3, PIECES, HEADS, PR, HD), bf16),
            pltpu.VMEM((HEADS, HD, LAT), bf16),
            pltpu.VMEM((HEADS, 2, LAT), f32),
            pltpu.VMEM((HEADS, HD, LAT), bf16),
            pltpu.VMEM((HEADS, 2, LAT), f32),
            pltpu.VMEM((HD, LAT), bf16),
            pltpu.VMEM((2, LAT), f32),
            pltpu.VMEM((4, HD, LAT), bf16),
            pltpu.VMEM((4, 2, LAT), f32),
            pltpu.VMEM((NB, 4, HD), bf16),
            pltpu.VMEM((4, HD, LAT), bf16),
            pltpu.VMEM((4, 1, LAT), f32),
            pltpu.VMEM((4, HEADS, HD, LAT), bf16),
            pltpu.VMEM((4, HEADS, 1, LAT), f32),
            pltpu.VMEM((4, HD, LAT), f32),
            pltpu.VMEM((3, PIECES, HEADS, PR, LAT), bf16),
            pltpu.VMEM((3, HEADS, HD, LAT), bf16),
            pltpu.VMEM((NB, 4, HD), f32),
            pltpu.VMEM((2, 4, 4, HD), f32),
            pltpu.VMEM((4 * NB, 4, 512), bf16),
            pltpu.VMEM((2, HEADS, 4, 512), bf16),
            dma((4,)), dma((2,)), dma((2,)), dma((4,)), dma((8,)), dma((2,)), dma((1,)), dma((2,)),
            dma((4,)), dma((4,)), dma((2,)), dma((2,)), dma((4, 3)), dma((1,)), dma((3, PIECES)), dma((2,)), dma((2,)),
            pltpu.SemaphoreType.REGULAR((2,)),
        ],
        compiler_params=pltpu.CompilerParams(
            collective_id=0, has_side_effects=True, vmem_limit_bytes=67043328
        ),
        name="ar_step",
    )(latent_queries, latent_embed, history_keys, history_values, latent_pos, norm_gain, wt, w_out[0])


def solution(mesh):
    return jax.shard_map(
        on_device,
        mesh=mesh,
        in_specs=(
            P(None, "blk", None),
            P(None, "blk", None),
            P(None, ("blk", "segment"), None),
            P(None, ("blk", "segment"), None),
            P(),
            P("segment", None),
            P("segment", None, None, "blk"),
            P("segment", "blk", None),
        ),
        out_specs=P(None, "blk", "segment"),
        check_vma=False,
    )
```

```python
import jax
import jax.numpy as jnp
from jax import lax
from jax.experimental import pallas as pl
from jax.experimental.pallas import tpu as pltpu
from jax.sharding import PartitionSpec as P

HEADS = 16
HD = 128
LAT = 128
D = 2048
ROWS = 256
NB = 32
epsilon = 1e-06
masked = -1e30
MESH = pl.DeviceIdType.MESH
f32, bf16 = jnp.float32, jnp.bfloat16
NN = (((1,), (0,)), ((), ()))
NT = (((1,), (1,)), ((), ()))
TN = (((0,), (0,)), ((), ()))


def hops(o):
    return sum(min(v, 4 - v) for v in o)


FAR = [divmod(o, 10) for o in (22, 12, 32, 21, 23, 11, 13, 31, 33, 2, 20, 1, 3, 10, 30)]
FAR3 = sorted(
    ((dx, dy, dz) for dx in range(4) for dy in range(4) for dz in range(2) if dx or dy or dz),
    key=lambda o: -hops(o),
)
HALVES = [
    sorted(((dx, dy) for dx in steps for dy in range(4)), key=lambda o: -hops(o)) for steps in ((2, 1), (3, 0))
]
NEARS = [divmod(o, 10) for o in (1, 3, 10, 30, 2, 11, 13, 31, 33, 20, 12, 32, 21, 23, 22)]
NEAR = 10
PIECES = 8
PR = HD // PIECES


def dot(a, b, dims):
    return lax.dot_general(a, b, dims, preferred_element_type=f32)


def kernel(
    q_hbm, e_hbm, k_hbm, v_hbm, pos_hbm, gain_hbm, wt_hbm, wo_hbm, out_ref,
    pos_ref, gains, qbuf, kb, vb, vts, wt, wob, wot, ob, obs, r1, r1s, r2o, r2os, r2, r2s, ebuf, xs, xss, xb, xbs, xf, ub, rb, fb, fx, uf, fu,
    loc_sem, kv_send, kv_recv, w_send, w_recv, g_sem, q_send, q_recv,
    r1_sem, r2_sem, e_sem, x_send, x_recv, u_send, u_recv, f_send, f_recv, go_sem,
):
    b = lax.axis_index("blk")
    s = lax.axis_index("segment")
    h = b // 2
    zl = b % 2
    zh = s // 2
    c = s % 2
    sib = (b, s + 1 - 2 * c)
    zpart = (b + 1 - 2 * zl, s)

    def rcopy(src, dst, ss, rs, dev):
        return pltpu.make_async_remote_copy(
            src_ref=src, dst_ref=dst, send_sem=ss, recv_sem=rs, device_id=dev, device_id_type=MESH
        )

    def bytes_of(ref, sem):
        pltpu.make_async_copy(ref, ref, sem).wait()

    hx, hy = h // 4, lax.rem(h, 4)

    def chip(dx, dy):
        return lax.rem(hx + dx, 4) * 4 + lax.rem(hy + dy, 4)

    far = [chip(*o) for o in FAR]
    near = [h] + [chip(*o) for o in NEARS]

    half = pl.ds(pl.multiple_of(64 * zl, 64), 64)
    loc = [
        pltpu.make_async_copy(k_hbm.at[c], kb.at[0], loc_sem.at[0]),
        pltpu.make_async_copy(v_hbm.at[c], vb.at[0], loc_sem.at[1]),
        pltpu.make_async_copy(q_hbm.at[c], qbuf.at[b], loc_sem.at[2]),
        pltpu.make_async_copy(pos_hbm, pos_ref, loc_sem.at[3]),
    ]
    barrier = pltpu.get_barrier_semaphore()
    other = b + 1 - 2 * zl

    def pair_dev(dx, dy, dz):
        return chip(dx, dy) * 2 + (1 - zl if dz else zl)

    for o in FAR3:
        pl.semaphore_signal(barrier, inc=1, device_id=(pair_dev(*o), s), device_id_type=MESH)
    for blk in (b, other):
        for ds in range(1, 4):
            pl.semaphore_signal(barrier, inc=1, device_id=(blk, (s + ds) % 4), device_id_type=MESH)
    for cp in (loc[2], loc[1], loc[0], loc[3]):
        cp.start()

    pl.semaphore_wait(barrier, 37)

    kx = rcopy(k_hbm.at[1 - c], kb.at[1], kv_send.at[0], kv_recv.at[0], sib)
    vx = rcopy(v_hbm.at[1 - c], vb.at[1], kv_send.at[1], kv_recv.at[1], sib)
    kx.start()
    vx.start()

    def q_start(half_no):
        for dx, dy, dz in FAR3:
            for step in ((2, 1), (3, 0))[half_no]:
                cols = pl.ds(pl.multiple_of(lax.rem(hx + dx + step, 4) * 512, 512), 512)
                rcopy(
                    q_hbm.at[c, :, cols], qbuf.at[b, :, cols], q_send.at[0], q_recv.at[half_no],
                    (pair_dev(dx, dy, dz), s),
                ).start()

    q_start(0)
    q_start(1)
    w_to = [
        (wt_hbm, wt.at[s, :, half, :], w_recv.at[s]),
        (wo_hbm, wob.at[s, half, :], w_recv.at[4 + s]),
    ]
    w_away = [rcopy(src, dst, w_send.at[i], rs, (other, 1)) for i, (src, dst, rs) in enumerate(w_to)]
    w_same = [rcopy(src, dst, w_send.at[2 + i], rs, (b, 1)) for i, (src, dst, rs) in enumerate(w_to)]
    gx = rcopy(gain_hbm, gains.at[s], g_sem.at[0], g_sem.at[1], (b, 1))

    @pl.when(s == 1)
    def _():
        for src, dst, rs in w_to:
            pltpu.make_async_copy(src, dst, rs).start()
        pltpu.make_async_copy(gain_hbm, gains.at[s], g_sem.at[1]).start()

    @pl.when(s != 1)
    def _():
        gx.start()

    @pl.when(c == 0)
    def _():
        w_away[0].start()

    @pl.when(s != 1)
    def _():
        w_away[1].start()

    @pl.when(s == 0)
    def _():
        for cp in w_same:
            cp.start()

    loc[1].wait()
    for j in range(HEADS):
        vts[j] = vb[0, :, j * HD : (j + 1) * HD].T
    loc[0].wait()
    kx.wait_recv()
    for cp in loc[2:]:
        cp.wait()
    bytes_of(qbuf.at[0:31, :, 0:1024], q_recv.at[0])

    def e_copy(m, t):
        p = lax.rem(h + t, HEADS)
        dst = p * 2 + 1 - m
        cols = pl.ds(pl.multiple_of(p * HD, HD), HD)
        return (
            e_hbm.at[m, :, cols],
            ebuf.at[b],
            dst,
        )

    @pl.when(s == 1)
    def _():
        for m in range(2):
            def e_start(t, _):
                src, dst_ref, dst = e_copy(m, t)
                rcopy(src, dst_ref, e_sem.at[0], e_sem.at[1], (dst, s)).start()
                return 0
            lax.fori_loop(1, HEADS, e_start, 0)
            src, dst_ref, dst = e_copy(m, 0)

            @pl.when(zl == 1 - m)
            def _():
                pltpu.make_async_copy(src, dst_ref, e_sem.at[1]).start()

            @pl.when(zl == m)
            def _():
                rcopy(src, dst_ref, e_sem.at[0], e_sem.at[1], (dst, s)).start()

    base0 = (b * 4 + s) * ROWS
    base1 = (b * 4 + s + 1 - 2 * c) * ROWS
    pos = pos_ref[pl.ds(c, 1), :]
    ids = lax.broadcasted_iota(jnp.int32, (ROWS, LAT), 0)
    scale = HD ** (-0.5)

    ids1 = ids + base1
    ids0 = ids + base0

    def scores(hh):
        cols = pl.ds(pl.multiple_of(hh * HD, HD), HD)
        qh = qbuf[:, :, cols].astype(f32).reshape(LAT, HD).astype(bf16)
        s0 = jnp.where(ids0 < pos, dot(kb[0, :, cols], qh, NT) * scale, masked)
        s1 = jnp.where(ids1 < pos, dot(kb[1, :, cols], qh, NT) * scale, masked)
        return s0, s1

    def weigh(s0, s1):
        top = jnp.maximum(jnp.max(jnp.maximum(s0, s1), axis=0, keepdims=True), 0.1 * masked)
        e0, e1 = jnp.exp(s0 - top), jnp.exp(s1 - top)
        total = jnp.sum(e0 + e1, axis=0, keepdims=True)
        return top, total, e0.astype(bf16), e1.astype(bf16)

    order = [chip(*o) for o in HALVES[0] + HALVES[1]]
    for g in range(0, HEADS, 4):
        if g == HEADS // 2:
            bytes_of(qbuf.at[0:31, :, 0:1024], q_recv.at[1])
        group = order[g : g + 4]
        ss = [scores(hh) for hh in group]
        ws = [weigh(*v) for v in ss]
        if g == 0:
            vx.wait_recv()
        for hh, (top, total, e0, e1) in zip(group, ws):
            cols = pl.ds(pl.multiple_of(hh * HD, HD), HD)
            ob[hh] = (dot(vts[hh], e0, NN) + dot(vb[1, :, cols].T, e1, NN)).astype(bf16)
            obs[hh, 0:1, :] = top
            obs[hh, 1:2, :] = total
        for i in range(g, g + 4):
            if i < HEADS - 1:
                hh = order[i]
                rcopy(obs.at[hh], r1s.at[h], r1_sem.at[2], r1_sem.at[3], (hh * 2 + zl, s)).start()
                rcopy(ob.at[hh], r1.at[h], r1_sem.at[0], r1_sem.at[1], (hh * 2 + zl, s)).start()

    bytes_of(r1.at[0:15], r1_sem.at[1])
    bytes_of(r1s.at[0:15], r1_sem.at[3])
    r1[h] = ob[h]
    r1s[h] = obs[h]

    def combine(buf, stats, n):
        top = stats[0, 0:1, :]
        for i in range(1, n):
            top = jnp.maximum(top, stats[i, 0:1, :])
        total = jnp.zeros((1, LAT), f32)
        acc = jnp.zeros((HD, LAT), f32)
        for i in range(n):
            w = jnp.exp(stats[i, 0:1, :] - top)
            total = total + w * stats[i, 1:2, :]
            acc = acc + w * buf[i].astype(f32)
        return acc, top, total

    acc, top, total = combine(r1, r1s, HEADS)
    r2o[...] = acc.astype(bf16)
    r2os[0:1, :] = top
    r2os[1:2, :] = total
    z = zh * 2 + zl
    r2_home = (s == 1) & (zl == 1 - c)
    r2_dst = (2 * h + 1 - c, 1)
    r2_copies = [
        rcopy(r2os, r2s.at[z], r2_sem.at[2], r2_sem.at[3], r2_dst),
        rcopy(r2o, r2.at[z], r2_sem.at[0], r2_sem.at[1], r2_dst),
    ]

    @pl.when(r2_home)
    def _():
        pltpu.make_async_copy(r2os, r2s.at[z], r2_sem.at[3]).start()
        pltpu.make_async_copy(r2o, r2.at[z], r2_sem.at[1]).start()

    @pl.when(jnp.logical_not(r2_home))
    def _():
        for cp in r2_copies:
            cp.start()

    @pl.when(s == 2)
    def _():
        pl.semaphore_wait(go_sem.at[0], 2)
        for cp in w_same:
            cp.start()

    @pl.when(s == 3)
    def _():
        pl.semaphore_wait(go_sem.at[0], 2)
        w_away[0].start()
        pl.semaphore_wait(go_sem.at[1], 2)
        for cp in w_same:
            cp.start()

    my_cols = pl.ds(pl.multiple_of(h * HD, HD), HD)

    def column(k):
        return jnp.broadcast_to(gains[k, :, my_cols], (HD, LAT)).T

    seg = h // 4
    jj = lax.broadcasted_iota(jnp.int32, (LAT, LAT), 0)
    ii = lax.broadcasted_iota(jnp.int32, (LAT, LAT), 1)

    pieces = [slice(PR * i, PR * i + PR) for i in range(PIECES)]

    def pack_x(k, i, x, gain, before):
        xs[k, pieces[i], :] = (x * gain[pieces[i]]).astype(bf16)
        ss = before + jnp.sum(x * x, axis=0, keepdims=True)
        if i == PIECES - 1:
            xss[k] = ss
        return ss

    def gather(k, i):
        rows = pieces[i]
        if i == PIECES - 1:
            for p in far:
                rcopy(xss.at[k], xbs.at[k, h], x_send.at[1], x_recv.at[2], (p * 2 + zl, s)).start()
            pltpu.make_async_copy(xss.at[k], xbs.at[k, h], x_recv.at[2]).start()
        for n, p in enumerate(far):
            late = int(FAR[n] in NEARS[NEAR - 1 :])
            rcopy(
                xs.at[k, rows], xb.at[k, h, rows], x_send.at[0], x_recv.at[late], (p * 2 + zl, s)
            ).start()
        pltpu.make_async_copy(xs.at[k, rows], xb.at[k, h, rows], x_recv.at[0]).start()

    def attend(k):
        bytes_of(wt.at[k], w_recv.at[k])
        if k == 3:
            fb[...] = xf[k].T.reshape(NB, 4, HD)
            sem = f_recv.at[0]
            dst = fx.at[1 - zl, lax.rem(h, 4)]
            for p in far:
                for dz in range(2):
                    rcopy(fb.at[2 * p + dz], dst, f_send.at[0], sem, (2 * p + dz, seg)).start()
            rcopy(fb.at[other], dst, f_send.at[0], sem, (other, seg)).start()

            @pl.when(seg != s)
            def _():
                rcopy(fb.at[b], dst, f_send.at[0], sem, (b, seg)).start()

            @pl.when(seg == s)
            def _():
                pltpu.make_async_copy(fb.at[b], dst, sem).start()

        qkv = jnp.zeros((3 * HD, LAT), f32)
        for j in range(0, HEADS, 2):
            pair = near[j : j + 2]
            if j == 0:
                bytes_of(xb.at[k, 0:NEAR], x_recv.at[0])
            if j == NEAR:
                bytes_of(wob.at[k], w_recv.at[4 + k])
                for i in range(HEADS if k < 3 else 0):
                    turned = wob[k, :, i * HD : (i + 1) * HD].T
                    for n, rows in enumerate(pieces):
                        wot[k, n, i] = turned[rows]
                bytes_of(xb.at[k, 0 : HEADS - NEAR], x_recv.at[1])
            w2 = [wt[k, :, :, pl.ds(pl.multiple_of(p * HD, HD), HD)].reshape(3 * HD, HD) for p in pair]
            x2 = [xb[k, p] for p in pair]
            qkv = qkv + dot(jnp.concatenate(w2, axis=1), jnp.concatenate(x2, axis=0), NN)
        bytes_of(xbs.at[k], x_recv.at[2])
        factor = lax.rsqrt(jnp.sum(xbs[k], axis=0) * (1.0 / D) + epsilon)
        qkv = (qkv * factor).astype(bf16)
        qt, kt, vt = qkv[0:HD], qkv[HD : 2 * HD], qkv[2 * HD :]
        sc = dot(kt, qt, TN) * scale
        sc = jnp.where(jj <= ii, sc, masked)
        e = jnp.exp(sc - jnp.max(sc, axis=0, keepdims=True))
        soft = (e / jnp.sum(e, axis=0, keepdims=True)).astype(bf16)
        return dot(vt, soft, NN).astype(bf16)

    def exchange(k, att):
        for i, rows in enumerate(pieces):
            u = dot(wot[k, i].reshape(HEADS * PR, HD), att, NN).astype(bf16)
            ub[k, i] = u.reshape(HEADS, PR, LAT)
            for p in far:
                rcopy(
                    ub.at[k, i, p], rb.at[k, h, rows], u_send.at[0], u_recv.at[i], (p * 2 + zl, s)
                ).start()
        ss = jnp.zeros((1, LAT), f32)
        for i, rows in enumerate(pieces):
            x = xf[k, rows, :] + ub[k, i, h].astype(f32)
            bytes_of(rb.at[k, 0:15, rows], u_recv.at[i])
            for p in near[1:]:
                x = x + rb[k, p, rows, :].astype(f32)
            xf[k + 1, rows, :] = x
            ss = pack_x(k + 1, i, x, column(k + 1), ss)
            gather(k + 1, i)

    @pl.when(s == 1)
    def _():
        bytes_of(gains, g_sem.at[1])
        bytes_of(ebuf, e_sem.at[1])
        emb = ebuf[...].astype(f32).reshape(LAT, HD).T
        bytes_of(r2, r2_sem.at[1])
        bytes_of(r2s, r2_sem.at[3])
        acc, top, total = combine(r2, r2s, 4)
        x0 = emb + acc / total
        xf[0] = x0
        ss = jnp.zeros((1, LAT), f32)
        for i, rows in enumerate(pieces):
            ss = pack_x(0, i, x0[rows], column(0), ss)
            gather(0, i)

        def signal(dev, n=0):
            pl.semaphore_signal(go_sem.at[n], inc=1, device_id=dev, device_id_type=MESH)

        signal((other, 1))
        for n in (2, 3):
            signal((b, n))
            signal((other, n))
        pl.semaphore_wait(go_sem.at[0], 1)
        for cp in w_away:
            cp.start()
        exchange(0, attend(0))
        signal((b, 3), 1)
        signal((other, 3), 1)
        for k in range(1, 3):
            exchange(k, attend(k))
        att = attend(3)
        att_r = att.T
        sem = f_recv.at[1]
        dst = fu.at[1 - zl, h]
        def hand_out(chips, n):
            for p in chips:
                for dz in range(2):
                    i = 2 * p + dz
                    rcopy(uf.at[n * NB + i], dst, f_send.at[1], sem, (i, n)).start()

        for n in range(4):
            u = dot(att_r, wob[3, :, n * 512 : (n + 1) * 512], NN)
            uf[n * NB : (n + 1) * NB] = u.reshape(NB, 4, 512).astype(bf16)
            hand_out(far[:5], n)
        for n in range(4):
            hand_out(far[5:], n)
        for n in range(4):
            rcopy(uf.at[n * NB + other], dst, f_send.at[1], sem, (other, n)).start()
        for n in (0, 2, 3):
            rcopy(uf.at[n * NB + b], dst, f_send.at[1], sem, (b, n)).start()
        pltpu.make_async_copy(uf.at[NB + b], dst, sem).start()
        bytes_of(uf.at[0:127], f_send.at[1])

        @pl.when(seg == s)
        def _():
            bytes_of(fb.at[0:31], f_send.at[0])

        @pl.when(seg != s)
        def _():
            bytes_of(fb, f_send.at[0])

        bytes_of(ub.at[:, :, 0:15], u_send.at[0])
        bytes_of(xb.at[:, 0:15], x_send.at[0])
        bytes_of(xbs.at[:, 0:15], x_send.at[1])

    bytes_of(qbuf.at[0:31], q_send.at[0])
    bytes_of(ob.at[0:15], r1_sem.at[0])
    bytes_of(obs.at[0:15], r1_sem.at[2])
    for cp in [kx, vx] + w_away:
        cp.wait_send()

    @pl.when(s != 1)
    def _():
        for cp in [gx] + w_same:
            cp.wait_send()

    @pl.when(jnp.logical_not(r2_home))
    def _():
        for cp in r2_copies:
            cp.wait_send()

    @pl.when(s == 1)
    def _():
        bytes_of(ebuf.at[0:31], e_sem.at[0])

    bytes_of(fx, f_recv.at[0])
    bytes_of(fu, f_recv.at[1])
    for m in range(2):
        acc = jnp.concatenate([fx[m, i] for i in range(4)], axis=1)
        for i in range(HEADS):
            acc = acc + fu[m, i].astype(f32)
        out_ref[m] = acc


def on_device(
    latent_queries, latent_embed, history_keys, history_values, latent_pos, norm_gain, w_qkv, w_out
):
    wt = jnp.transpose(w_qkv[0], (1, 2, 0))
    hbm = pl.BlockSpec(memory_space=pl.ANY)
    vmem = pl.BlockSpec(memory_space=pltpu.VMEM)
    dma = pltpu.SemaphoreType.DMA
    return pl.pallas_call(
        kernel,
        out_shape=jax.ShapeDtypeStruct((2, 4, 512), f32),
        in_specs=[hbm] * 8,
        out_specs=vmem,
        scratch_shapes=[
            pltpu.VMEM((2, LAT), jnp.int32),
            pltpu.VMEM((4, 1, D), f32),
            pltpu.VMEM((NB, 4, D), bf16),
            pltpu.VMEM((2, ROWS, D), bf16),
            pltpu.VMEM((2, ROWS, D), bf16),
            pltpu.VMEM((HEADS, HD, ROWS), bf16),
            pltpu.VMEM((4, 3, HD, D), bf16),
            pltpu.VMEM((4, HD, D), bf16),
            pltpu.VMEM((3, PIECES, HEADS, PR, HD), bf16),
            pltpu.VMEM((HEADS, HD, LAT), bf16),
            pltpu.VMEM((HEADS, 2, LAT), f32),
            pltpu.VMEM((HEADS, HD, LAT), bf16),
            pltpu.VMEM((HEADS, 2, LAT), f32),
            pltpu.VMEM((HD, LAT), bf16),
            pltpu.VMEM((2, LAT), f32),
            pltpu.VMEM((4, HD, LAT), bf16),
            pltpu.VMEM((4, 2, LAT), f32),
            pltpu.VMEM((NB, 4, HD), bf16),
            pltpu.VMEM((4, HD, LAT), bf16),
            pltpu.VMEM((4, 1, LAT), f32),
            pltpu.VMEM((4, HEADS, HD, LAT), bf16),
            pltpu.VMEM((4, HEADS, 1, LAT), f32),
            pltpu.VMEM((4, HD, LAT), f32),
            pltpu.VMEM((3, PIECES, HEADS, PR, LAT), bf16),
            pltpu.VMEM((3, HEADS, HD, LAT), bf16),
            pltpu.VMEM((NB, 4, HD), f32),
            pltpu.VMEM((2, 4, 4, HD), f32),
            pltpu.VMEM((4 * NB, 4, 512), bf16),
            pltpu.VMEM((2, HEADS, 4, 512), bf16),
            dma((4,)), dma((2,)), dma((2,)), dma((4,)), dma((8,)), dma((2,)), dma((1,)), dma((2,)),
            dma((4,)), dma((4,)), dma((2,)), dma((2,)), dma((3,)), dma((1,)), dma((PIECES,)), dma((2,)), dma((2,)),
            pltpu.SemaphoreType.REGULAR((2,)),
        ],
        compiler_params=pltpu.CompilerParams(
            collective_id=0, has_side_effects=True, vmem_limit_bytes=67043328
        ),
        name="ar_step",
    )(latent_queries, latent_embed, history_keys, history_values, latent_pos, norm_gain, wt, w_out[0])


def solution(mesh):
    return jax.shard_map(
        on_device,
        mesh=mesh,
        in_specs=(
            P(None, "blk", None),
            P(None, "blk", None),
            P(None, ("blk", "segment"), None),
            P(None, ("blk", "segment"), None),
            P(),
            P("segment", None),
            P("segment", None, None, "blk"),
            P("segment", "blk", None),
        ),
        out_specs=P(None, "blk", "segment"),
        check_vma=False,
    )
```

```python
import jax
import jax.numpy as jnp
from jax import lax
from jax.experimental import pallas as pl
from jax.experimental.pallas import tpu as pltpu
from jax.sharding import PartitionSpec as P

HEADS = 16
HD = 128
LAT = 128
D = 2048
ROWS = 256
NB = 32
epsilon = 1e-06
masked = -1e30
MESH = pl.DeviceIdType.MESH
f32, bf16 = jnp.float32, jnp.bfloat16
NN = (((1,), (0,)), ((), ()))
NT = (((1,), (1,)), ((), ()))
TN = (((0,), (0,)), ((), ()))


def hops(o):
    return sum(min(v, 4 - v) for v in o)


FAR = [divmod(o, 10) for o in (22, 12, 32, 21, 23, 11, 13, 31, 33, 2, 20, 1, 3, 10, 30)]
FAR3 = sorted(
    ((dx, dy, dz) for dx in range(4) for dy in range(4) for dz in range(2) if dx or dy or dz),
    key=lambda o: -hops(o),
)
HALVES = [
    sorted(((dx, dy) for dx in steps for dy in range(4)), key=lambda o: -hops(o)) for steps in ((2, 1), (3, 0))
]
NEARS = [divmod(o, 10) for o in (1, 3, 10, 30, 2, 11, 13, 31, 33, 20, 12, 32, 21, 23, 22)]
NEAR = 10
PIECES = 8
PR = HD // PIECES


def dot(a, b, dims):
    return lax.dot_general(a, b, dims, preferred_element_type=f32)


def kernel(
    q_hbm, e_hbm, k_hbm, v_hbm, pos_hbm, gain_hbm, wt_hbm, wo_hbm, out_ref,
    pos_ref, gains, qbuf, kb, vb, vts, wt, wob, wot, ob, obs, r1, r1s, r2o, r2os, r2, r2s, ebuf, xs, xss, xb, xbs, xf, ub, rb, fb, fx, uf, fu,
    loc_sem, kv_send, kv_recv, w_send, w_recv, g_sem, q_send, q_recv,
    r1_sem, r2_sem, e_sem, x_send, x_recv, u_send, u_recv, f_send, f_recv, go_sem,
):
    b = lax.axis_index("blk")
    s = lax.axis_index("segment")
    h = b // 2
    zl = b % 2
    zh = s // 2
    c = s % 2
    sib = (b, s + 1 - 2 * c)
    zpart = (b + 1 - 2 * zl, s)

    def rcopy(src, dst, ss, rs, dev):
        return pltpu.make_async_remote_copy(
            src_ref=src, dst_ref=dst, send_sem=ss, recv_sem=rs, device_id=dev, device_id_type=MESH
        )

    def bytes_of(ref, sem):
        pltpu.make_async_copy(ref, ref, sem).wait()

    hx, hy = h // 4, lax.rem(h, 4)

    def chip(dx, dy):
        return lax.rem(hx + dx, 4) * 4 + lax.rem(hy + dy, 4)

    far = [chip(*o) for o in FAR]
    near = [h] + [chip(*o) for o in NEARS]

    half = pl.ds(pl.multiple_of(64 * zl, 64), 64)
    loc = [
        pltpu.make_async_copy(k_hbm.at[c], kb.at[0], loc_sem.at[0]),
        pltpu.make_async_copy(v_hbm.at[c], vb.at[0], loc_sem.at[1]),
        pltpu.make_async_copy(q_hbm.at[c], qbuf.at[b], loc_sem.at[2]),
        pltpu.make_async_copy(pos_hbm, pos_ref, loc_sem.at[3]),
    ]
    barrier = pltpu.get_barrier_semaphore()
    other = b + 1 - 2 * zl

    def pair_dev(dx, dy, dz):
        return chip(dx, dy) * 2 + (1 - zl if dz else zl)

    for o in FAR3:
        pl.semaphore_signal(barrier, inc=1, device_id=(pair_dev(*o), s), device_id_type=MESH)
    for blk in (b, other):
        for ds in range(1, 4):
            pl.semaphore_signal(barrier, inc=1, device_id=(blk, (s + ds) % 4), device_id_type=MESH)
    for cp in (loc[2], loc[1], loc[0], loc[3]):
        cp.start()

    pl.semaphore_wait(barrier, 37)

    kx = rcopy(k_hbm.at[1 - c], kb.at[1], kv_send.at[0], kv_recv.at[0], sib)
    vx = rcopy(v_hbm.at[1 - c], vb.at[1], kv_send.at[1], kv_recv.at[1], sib)
    kx.start()
    vx.start()

    def q_start(half_no):
        for dx, dy, dz in FAR3:
            for step in ((2, 1), (3, 0))[half_no]:
                cols = pl.ds(pl.multiple_of(lax.rem(hx + dx + step, 4) * 512, 512), 512)
                rcopy(
                    q_hbm.at[c, :, cols], qbuf.at[b, :, cols], q_send.at[0], q_recv.at[half_no],
                    (pair_dev(dx, dy, dz), s),
                ).start()

    q_start(0)
    q_start(1)
    w_to = [
        (wt_hbm, wt.at[s, :, half, :], w_recv.at[s]),
        (wo_hbm, wob.at[s, half, :], w_recv.at[4 + s]),
    ]
    w_away = [rcopy(src, dst, w_send.at[i], rs, (other, 1)) for i, (src, dst, rs) in enumerate(w_to)]
    w_same = [rcopy(src, dst, w_send.at[2 + i], rs, (b, 1)) for i, (src, dst, rs) in enumerate(w_to)]
    gx = rcopy(gain_hbm, gains.at[s], g_sem.at[0], g_sem.at[1], (b, 1))

    @pl.when(s == 1)
    def _():
        for src, dst, rs in w_to:
            pltpu.make_async_copy(src, dst, rs).start()
        pltpu.make_async_copy(gain_hbm, gains.at[s], g_sem.at[1]).start()

    @pl.when(s != 1)
    def _():
        gx.start()

    @pl.when(c == 0)
    def _():
        w_away[0].start()

    @pl.when(s != 1)
    def _():
        w_away[1].start()

    @pl.when(s == 0)
    def _():
        for cp in w_same:
            cp.start()

    loc[1].wait()
    for j in range(HEADS):
        vts[j] = vb[0, :, j * HD : (j + 1) * HD].T
    loc[0].wait()
    kx.wait_recv()
    for cp in loc[2:]:
        cp.wait()
    bytes_of(qbuf.at[0:31, :, 0:1024], q_recv.at[0])

    def e_copy(m, t):
        p = lax.rem(h + t, HEADS)
        dst = p * 2 + 1 - m
        cols = pl.ds(pl.multiple_of(p * HD, HD), HD)
        return (
            e_hbm.at[m, :, cols],
            ebuf.at[b],
            dst,
        )

    @pl.when(s == 1)
    def _():
        for m in range(2):
            def e_start(t, _):
                src, dst_ref, dst = e_copy(m, t)
                rcopy(src, dst_ref, e_sem.at[0], e_sem.at[1], (dst, s)).start()
                return 0
            lax.fori_loop(1, HEADS, e_start, 0)
            src, dst_ref, dst = e_copy(m, 0)

            @pl.when(zl == 1 - m)
            def _():
                pltpu.make_async_copy(src, dst_ref, e_sem.at[1]).start()

            @pl.when(zl == m)
            def _():
                rcopy(src, dst_ref, e_sem.at[0], e_sem.at[1], (dst, s)).start()

    base0 = (b * 4 + s) * ROWS
    base1 = (b * 4 + s + 1 - 2 * c) * ROWS
    pos = pos_ref[pl.ds(c, 1), :]
    ids = lax.broadcasted_iota(jnp.int32, (ROWS, LAT), 0)
    scale = HD ** (-0.5)

    ids1 = ids + base1
    ids0 = ids + base0

    def scores(hh):
        cols = pl.ds(pl.multiple_of(hh * HD, HD), HD)
        qh = qbuf[:, :, cols].astype(f32).reshape(LAT, HD).astype(bf16)
        s0 = jnp.where(ids0 < pos, dot(kb[0, :, cols], qh, NT) * scale, masked)
        s1 = jnp.where(ids1 < pos, dot(kb[1, :, cols], qh, NT) * scale, masked)
        return s0, s1

    def weigh(s0, s1):
        top = jnp.maximum(jnp.max(jnp.maximum(s0, s1), axis=0, keepdims=True), 0.1 * masked)
        e0, e1 = jnp.exp(s0 - top), jnp.exp(s1 - top)
        total = jnp.sum(e0 + e1, axis=0, keepdims=True)
        return top, total, e0.astype(bf16), e1.astype(bf16)

    order = [chip(*o) for o in HALVES[0] + HALVES[1]]
    for g in range(0, HEADS, 4):
        if g == HEADS // 2:
            bytes_of(qbuf.at[0:31, :, 0:1024], q_recv.at[1])
        group = order[g : g + 4]
        ss = [scores(hh) for hh in group]
        ws = [weigh(*v) for v in ss]
        if g == 0:
            vx.wait_recv()
        for hh, (top, total, e0, e1) in zip(group, ws):
            cols = pl.ds(pl.multiple_of(hh * HD, HD), HD)
            ob[hh] = (dot(vts[hh], e0, NN) + dot(vb[1, :, cols].T, e1, NN)).astype(bf16)
            obs[hh, 0:1, :] = top
            obs[hh, 1:2, :] = total
        for i in range(g, g + 4):
            if i < HEADS - 1:
                hh = order[i]
                rcopy(obs.at[hh], r1s.at[h], r1_sem.at[2], r1_sem.at[3], (hh * 2 + zl, s)).start()
                rcopy(ob.at[hh], r1.at[h], r1_sem.at[0], r1_sem.at[1], (hh * 2 + zl, s)).start()

    bytes_of(r1.at[0:15], r1_sem.at[1])
    bytes_of(r1s.at[0:15], r1_sem.at[3])
    r1[h] = ob[h]
    r1s[h] = obs[h]

    def combine(buf, stats, n):
        top = stats[0, 0:1, :]
        for i in range(1, n):
            top = jnp.maximum(top, stats[i, 0:1, :])
        total = jnp.zeros((1, LAT), f32)
        acc = jnp.zeros((HD, LAT), f32)
        for i in range(n):
            w = jnp.exp(stats[i, 0:1, :] - top)
            total = total + w * stats[i, 1:2, :]
            acc = acc + w * buf[i].astype(f32)
        return acc, top, total

    acc, top, total = combine(r1, r1s, HEADS)
    r2o[...] = acc.astype(bf16)
    r2os[0:1, :] = top
    r2os[1:2, :] = total
    z = zh * 2 + zl
    r2_home = (s == 1) & (zl == 1 - c)
    r2_dst = (2 * h + 1 - c, 1)
    r2_copies = [
        rcopy(r2os, r2s.at[z], r2_sem.at[2], r2_sem.at[3], r2_dst),
        rcopy(r2o, r2.at[z], r2_sem.at[0], r2_sem.at[1], r2_dst),
    ]

    @pl.when(r2_home)
    def _():
        pltpu.make_async_copy(r2os, r2s.at[z], r2_sem.at[3]).start()
        pltpu.make_async_copy(r2o, r2.at[z], r2_sem.at[1]).start()

    @pl.when(jnp.logical_not(r2_home))
    def _():
        for cp in r2_copies:
            cp.start()

    @pl.when(s == 2)
    def _():
        pl.semaphore_wait(go_sem.at[0], 2)
        for cp in w_same:
            cp.start()

    @pl.when(s == 3)
    def _():
        pl.semaphore_wait(go_sem.at[0], 2)
        w_away[0].start()
        pl.semaphore_wait(go_sem.at[1], 2)
        for cp in w_same:
            cp.start()

    my_cols = pl.ds(pl.multiple_of(h * HD, HD), HD)

    def column(k):
        return jnp.broadcast_to(gains[k, :, my_cols], (HD, LAT)).T

    seg = h // 4
    jj = lax.broadcasted_iota(jnp.int32, (LAT, LAT), 0)
    ii = lax.broadcasted_iota(jnp.int32, (LAT, LAT), 1)

    pieces = [slice(PR * i, PR * i + PR) for i in range(PIECES)]

    def pack_x(k, i, x, gain, before):
        xs[k, pieces[i], :] = (x * gain[pieces[i]]).astype(bf16)
        ss = before + jnp.sum(x * x, axis=0, keepdims=True)
        if i == PIECES - 1:
            xss[k] = ss
        return ss

    def gather(k, i, rows):
        if i == PIECES - 1:
            for p in far:
                rcopy(xss.at[k], xbs.at[k, h], x_send.at[1], x_recv.at[2], (p * 2 + zl, s)).start()
            pltpu.make_async_copy(xss.at[k], xbs.at[k, h], x_recv.at[2]).start()
        for n, p in enumerate(far):
            late = int(FAR[n] in NEARS[NEAR - 1 :])
            rcopy(
                xs.at[k, rows], xb.at[k, h, rows], x_send.at[0], x_recv.at[late], (p * 2 + zl, s)
            ).start()
        pltpu.make_async_copy(xs.at[k, rows], xb.at[k, h, rows], x_recv.at[0]).start()

    def attend(k):
        bytes_of(wt.at[k], w_recv.at[k])
        if k == 3:
            fb[...] = xf[k].T.reshape(NB, 4, HD)
            sem = f_recv.at[0]
            dst = fx.at[1 - zl, lax.rem(h, 4)]
            for p in far:
                for dz in range(2):
                    rcopy(fb.at[2 * p + dz], dst, f_send.at[0], sem, (2 * p + dz, seg)).start()
            rcopy(fb.at[other], dst, f_send.at[0], sem, (other, seg)).start()

            @pl.when(seg != s)
            def _():
                rcopy(fb.at[b], dst, f_send.at[0], sem, (b, seg)).start()

            @pl.when(seg == s)
            def _():
                pltpu.make_async_copy(fb.at[b], dst, sem).start()

        qkv = jnp.zeros((3 * HD, LAT), f32)
        for j in range(0, HEADS, 2):
            pair = near[j : j + 2]
            if j == 0:
                bytes_of(xb.at[k, 0:NEAR], x_recv.at[0])
            if j == NEAR:
                bytes_of(wob.at[k], w_recv.at[4 + k])
                for i in range(HEADS if k < 3 else 0):
                    turned = wob[k, :, i * HD : (i + 1) * HD].T
                    for n, rows in enumerate(pieces):
                        wot[k, n, i] = turned[rows]
                bytes_of(xb.at[k, 0 : HEADS - NEAR], x_recv.at[1])
            w2 = [wt[k, :, :, pl.ds(pl.multiple_of(p * HD, HD), HD)].reshape(3 * HD, HD) for p in pair]
            x2 = [xb[k, p] for p in pair]
            qkv = qkv + dot(jnp.concatenate(w2, axis=1), jnp.concatenate(x2, axis=0), NN)
        bytes_of(xbs.at[k], x_recv.at[2])
        factor = lax.rsqrt(jnp.sum(xbs[k], axis=0) * (1.0 / D) + epsilon)
        qkv = (qkv * factor).astype(bf16)
        qt, kt, vt = qkv[0:HD], qkv[HD : 2 * HD], qkv[2 * HD :]
        sc = dot(kt, qt, TN) * scale
        sc = jnp.where(jj <= ii, sc, masked)
        e = jnp.exp(sc - jnp.max(sc, axis=0, keepdims=True))
        soft = (e / jnp.sum(e, axis=0, keepdims=True)).astype(bf16)
        return dot(vt, soft, NN).astype(bf16)

    def exchange(k, att):
        for i, rows in enumerate(pieces):
            u = dot(wot[k, i].reshape(HEADS * PR, HD), att, NN).astype(bf16)
            ub[k, i] = u.reshape(HEADS, PR, LAT)
            for p in far:
                rcopy(
                    ub.at[k, i, p], rb.at[k, h, rows], u_send.at[0], u_recv.at[i], (p * 2 + zl, s)
                ).start()
        ss = jnp.zeros((1, LAT), f32)
        for i, rows in enumerate(pieces):
            x = xf[k, rows, :] + ub[k, i, h].astype(f32)
            bytes_of(rb.at[k, 0:15, rows], u_recv.at[i])
            for p in near[1:]:
                x = x + rb[k, p, rows, :].astype(f32)
            xf[k + 1, rows, :] = x
            ss = pack_x(k + 1, i, x, column(k + 1), ss)
            gather(k + 1, i, rows)

    @pl.when(s == 1)
    def _():
        bytes_of(gains, g_sem.at[1])
        bytes_of(ebuf, e_sem.at[1])
        emb = ebuf[...].astype(f32).reshape(LAT, HD).T
        bytes_of(r2, r2_sem.at[1])
        bytes_of(r2s, r2_sem.at[3])
        acc, top, total = combine(r2, r2s, 4)
        x0 = emb + acc / total
        xf[0] = x0
        ss = jnp.zeros((1, LAT), f32)
        for i, rows in enumerate(pieces):
            ss = pack_x(0, i, x0[rows], column(0), ss)
        gather(0, PIECES - 1, slice(0, HD))

        def signal(dev, n=0):
            pl.semaphore_signal(go_sem.at[n], inc=1, device_id=dev, device_id_type=MESH)

        signal((other, 1))
        for n in (2, 3):
            signal((b, n))
            signal((other, n))
        pl.semaphore_wait(go_sem.at[0], 1)
        for cp in w_away:
            cp.start()
        exchange(0, attend(0))
        signal((b, 3), 1)
        signal((other, 3), 1)
        for k in range(1, 3):
            exchange(k, attend(k))
        att = attend(3)
        att_r = att.T
        sem = f_recv.at[1]
        dst = fu.at[1 - zl, h]
        def hand_out(chips, n):
            for p in chips:
                for dz in range(2):
                    i = 2 * p + dz
                    rcopy(uf.at[n * NB + i], dst, f_send.at[1], sem, (i, n)).start()

        for n in range(4):
            u = dot(att_r, wob[3, :, n * 512 : (n + 1) * 512], NN)
            uf[n * NB : (n + 1) * NB] = u.reshape(NB, 4, 512).astype(bf16)
            hand_out(far[:5], n)
        for n in range(4):
            hand_out(far[5:], n)
        for n in range(4):
            rcopy(uf.at[n * NB + other], dst, f_send.at[1], sem, (other, n)).start()
        for n in (0, 2, 3):
            rcopy(uf.at[n * NB + b], dst, f_send.at[1], sem, (b, n)).start()
        pltpu.make_async_copy(uf.at[NB + b], dst, sem).start()
        bytes_of(uf.at[0:127], f_send.at[1])

        @pl.when(seg == s)
        def _():
            bytes_of(fb.at[0:31], f_send.at[0])

        @pl.when(seg != s)
        def _():
            bytes_of(fb, f_send.at[0])

        bytes_of(ub.at[:, :, 0:15], u_send.at[0])
        bytes_of(xb.at[:, 0:15], x_send.at[0])
        bytes_of(xbs.at[:, 0:15], x_send.at[1])

    bytes_of(qbuf.at[0:31], q_send.at[0])
    bytes_of(ob.at[0:15], r1_sem.at[0])
    bytes_of(obs.at[0:15], r1_sem.at[2])
    for cp in [kx, vx] + w_away:
        cp.wait_send()

    @pl.when(s != 1)
    def _():
        for cp in [gx] + w_same:
            cp.wait_send()

    @pl.when(jnp.logical_not(r2_home))
    def _():
        for cp in r2_copies:
            cp.wait_send()

    @pl.when(s == 1)
    def _():
        bytes_of(ebuf.at[0:31], e_sem.at[0])

    bytes_of(fx, f_recv.at[0])
    bytes_of(fu, f_recv.at[1])
    for m in range(2):
        acc = jnp.concatenate([fx[m, i] for i in range(4)], axis=1)
        for i in range(HEADS):
            acc = acc + fu[m, i].astype(f32)
        out_ref[m] = acc


def on_device(
    latent_queries, latent_embed, history_keys, history_values, latent_pos, norm_gain, w_qkv, w_out
):
    wt = jnp.transpose(w_qkv[0], (1, 2, 0))
    hbm = pl.BlockSpec(memory_space=pl.ANY)
    vmem = pl.BlockSpec(memory_space=pltpu.VMEM)
    dma = pltpu.SemaphoreType.DMA
    return pl.pallas_call(
        kernel,
        out_shape=jax.ShapeDtypeStruct((2, 4, 512), f32),
        in_specs=[hbm] * 8,
        out_specs=vmem,
        scratch_shapes=[
            pltpu.VMEM((2, LAT), jnp.int32),
            pltpu.VMEM((4, 1, D), f32),
            pltpu.VMEM((NB, 4, D), bf16),
            pltpu.VMEM((2, ROWS, D), bf16),
            pltpu.VMEM((2, ROWS, D), bf16),
            pltpu.VMEM((HEADS, HD, ROWS), bf16),
            pltpu.VMEM((4, 3, HD, D), bf16),
            pltpu.VMEM((4, HD, D), bf16),
            pltpu.VMEM((3, PIECES, HEADS, PR, HD), bf16),
            pltpu.VMEM((HEADS, HD, LAT), bf16),
            pltpu.VMEM((HEADS, 2, LAT), f32),
            pltpu.VMEM((HEADS, HD, LAT), bf16),
            pltpu.VMEM((HEADS, 2, LAT), f32),
            pltpu.VMEM((HD, LAT), bf16),
            pltpu.VMEM((2, LAT), f32),
            pltpu.VMEM((4, HD, LAT), bf16),
            pltpu.VMEM((4, 2, LAT), f32),
            pltpu.VMEM((NB, 4, HD), bf16),
            pltpu.VMEM((4, HD, LAT), bf16),
            pltpu.VMEM((4, 1, LAT), f32),
            pltpu.VMEM((4, HEADS, HD, LAT), bf16),
            pltpu.VMEM((4, HEADS, 1, LAT), f32),
            pltpu.VMEM((4, HD, LAT), f32),
            pltpu.VMEM((3, PIECES, HEADS, PR, LAT), bf16),
            pltpu.VMEM((3, HEADS, HD, LAT), bf16),
            pltpu.VMEM((NB, 4, HD), f32),
            pltpu.VMEM((2, 4, 4, HD), f32),
            pltpu.VMEM((4 * NB, 4, 512), bf16),
            pltpu.VMEM((2, HEADS, 4, 512), bf16),
            dma((4,)), dma((2,)), dma((2,)), dma((4,)), dma((8,)), dma((2,)), dma((1,)), dma((2,)),
            dma((4,)), dma((4,)), dma((2,)), dma((2,)), dma((3,)), dma((1,)), dma((PIECES,)), dma((2,)), dma((2,)),
            pltpu.SemaphoreType.REGULAR((2,)),
        ],
        compiler_params=pltpu.CompilerParams(
            collective_id=0, has_side_effects=True, vmem_limit_bytes=67043328
        ),
        name="ar_step",
    )(latent_queries, latent_embed, history_keys, history_values, latent_pos, norm_gain, wt, w_out[0])


def solution(mesh):
    return jax.shard_map(
        on_device,
        mesh=mesh,
        in_specs=(
            P(None, "blk", None),
            P(None, "blk", None),
            P(None, ("blk", "segment"), None),
            P(None, ("blk", "segment"), None),
            P(),
            P("segment", None),
            P("segment", None, None, "blk"),
            P("segment", "blk", None),
        ),
        out_specs=P(None, "blk", "segment"),
        check_vma=False,
    )
```
